32 devices in a mesh: batch: 8 (over y, x, core), rows: 4 (over z).
Axes of the slice: x: 2, y: 2, z: 4, core: 2. Of those that a mesh axis runs over, the one named last changes fastest.
Arguments:
- feat_in: bfloat16 [16, 8, 8, 1024], P('batch', 'rows'), may hold values from -6 to 6
- style_vec: bfloat16 [16, 512], P('batch'), may hold values from -6 to 6
- labels: int32 [16], P('batch'), may hold values from 0 to 999
- noise_map: float32 [16, 16, 16], P('batch', 'rows'), may hold values from -6 to 6
- cot_feat: bfloat16 [16, 16, 16, 1024], P('batch', 'rows'), may hold values from -18 to 18
- cot_rgb: float32 [16, 3, 16, 16], P('batch', None, 'rows'), may hold values from -6 to 6
- mod_w: bfloat16 [512, 1024], P('batch'), may hold values from -0.078125 to 0.078125
- sel_w: bfloat16 [512, 2], P('batch'), may hold values from -0.25 to 0.25
- kernel_bank: bfloat16 [18432, 1024], P('batch'), may hold values from -0.0625 to 0.0625
- conv_bias: bfloat16 [1024], P('batch'), may hold values from -3 to 3
- noise_gain: bfloat16 [1024], P('batch'), may hold values from -3 to 3
- qk_w: bfloat16 [1024, 1024], P('batch'), may hold values from -0.1875 to 0.1875
- val_w: bfloat16 [1024, 1024], P('batch'), may hold values from -0.1875 to 0.1875
- out_w: bfloat16 [1024, 1024], P('batch'), may hold values from -0.5 to 0.5
- cq_w: bfloat16 [1024, 1024], P('batch'), may hold values from -0.1875 to 0.1875
- ck_w: bfloat16 [1024, 1024], P('batch'), may hold values from -0.1875 to 0.1875
- cv_w: bfloat16 [1024, 1024], P('batch'), may hold values from -0.1875 to 0.1875
- co_w: bfloat16 [1024, 1024], P('batch'), may hold values from -0.25 to 0.25
- up_w: bfloat16 [1024, 4096], P('batch'), may hold values from -0.1875 to 0.1875
- up_b: bfloat16 [4096], P('batch'), may hold values from -1.75 to 1.75
- down_w: bfloat16 [4096, 1024], P('batch'), may hold values from -0.09375 to 0.09375
- class_table: bfloat16 [1000, 4096], P(None, 'batch'), may hold values from -6 to 6
- rgb_w: bfloat16 [3, 1024], P(None, 'batch'), may hold values from -0.1875 to 0.1875
Outputs:
- feat_out: bfloat16 [16, 16, 16, 1024], P('batch', 'rows')
- rgb_out: float32 [16, 3, 16, 16], P('batch', None, 'rows')
- grad_input: float32 [16, 8, 8, 1024], P('batch', 'rows')
- r1_value: float32 [], replicated
- grad_mod_w: float32 [512, 1024], P('batch')
- grad_sel_w: float32 [512, 2], P('batch')
- grad_bank: float32 [18432, 1024], P('batch')
- grad_conv_bias: float32 [1024], P('batch')
- grad_noise_gain: float32 [1024], P('batch')
- grad_qk_w: float32 [1024, 1024], P('batch')
- grad_val_w: float32 [1024, 1024], P('batch')
- grad_out_w: float32 [1024, 1024], P('batch')
- grad_cq_w: float32 [1024, 1024], P('batch')
- grad_ck_w: float32 [1024, 1024], P('batch')
- grad_cv_w: float32 [1024, 1024], P('batch')
- grad_co_w: float32 [1024, 1024], P('batch')
- grad_up_w: float32 [1024, 4096], P('batch')
- grad_up_b: float32 [4096], P('batch')
- grad_down_w: float32 [4096, 1024], P('batch')
- grad_table: float32 [1000, 4096], P(None, 'batch')
- grad_rgb_w: float32 [3, 1024], P(None, 'batch')
The draws below stay inside these ranges and needn't reach their ends.
All inputs are finite; a program needn't handle non-finite values.
Results may differ from the reference program's by a relative error of at most 0.029.
The reference program's roundings to bfloat16 on the way count: a program that leaves them out, or rounds other values in their place, can miss the bound.
Values may be sent and summed in bfloat16 or wider, within the bound.
No kernel may reach another device: no remote copies, remote signals or barrier semaphores. Data moves between devices by JAX's collectives and lax.ppermute only.
A program may use at most 640 MiB of HBM per device.

```python
import jax
import jax.numpy as jnp
from jax import lax

D = 1024
WDIM = 512
HEADS = 16
HEAD_DIM = 64
KERNELS = 2
FFN = 4096
CLASSES = 1000
CTX = 4
IN_SIDE = 8
SIDE = 16
BATCH = 16


def draw_cot_feat(key, part):
    first_key = jax.random.fold_in(key, 0)
    position = jnp.arange(BATCH, dtype=jnp.float32) / max(BATCH - 1, 1)
    ramp = jnp.exp(position * jnp.log(3.0))[:, None, None, None]
    return jnp.clip(ramp * jax.random.normal(first_key, (BATCH, SIDE, SIDE, D), jnp.float32), -18.0, 18.0).astype(jnp.bfloat16)


def touch_ends(values, rng, smallest, top_value):
    extent = values.shape
    place = [jax.random.randint(jax.random.fold_in(rng, axis), (), 0, extent[axis]) for axis in range(len(extent))]
    values = values.at[tuple(place)].set(smallest)
    longest = extent.index(max(extent))
    place[longest] = (place[longest] + 1) % extent[longest]
    return values.at[tuple(place)].set(top_value)


def block_levels(rng, dims, cuts, low, top_value):
    gain = 1.0
    for dim, shards_of in cuts:
        heights = jax.random.uniform(jax.random.fold_in(jax.random.fold_in(rng, 6), dim), (shards_of,), jnp.float32, low / len(cuts), top_value / len(cuts))
        gain = gain * jnp.repeat(jnp.exp(heights), dims[dim] // shards_of).reshape((-1,) + (1,) * (len(dims) - 1 - dim))
    return gain


def scatter_about(stream_key, dims, deviation, bound, cuts=(), held_as=jnp.bfloat16):
    loudness = block_levels(stream_key, dims, cuts, -0.22, 0.18) if cuts else 1.0
    values = jax.random.normal(stream_key, dims, jnp.float32) * deviation * loudness
    return jnp.minimum(jnp.maximum(values, -bound), bound).astype(held_as)


def setup_inputs(seed: int = 0) -> dict:
    key_of = jax.random.split(jax.random.key(seed), 24)
    feat_in = scatter_about(key_of[0], (BATCH, IN_SIDE, IN_SIDE, D), 1.0, 6.0, ((0, 8), (1, 4)))
    style_vec = scatter_about(key_of[1], (BATCH, WDIM), 1.0, 6.0, ((0, 8),))
    labels = touch_ends(jax.random.randint(key_of[2], (BATCH,), 0, CLASSES), jax.random.fold_in(key_of[2], 1), 0, CLASSES - 1).astype(jnp.int32)
    noise_map = scatter_about(key_of[3], (BATCH, SIDE, SIDE), 1.0, 6.0, ((0, 8), (1, 4)), jnp.float32)
    cot_feat = draw_cot_feat(jax.random.fold_in(key_of[23], 71), 0)
    cot_rgb = scatter_about(key_of[5], (BATCH, 3, SIDE, SIDE), 1.0, 6.0, ((0, 8), (2, 4)), jnp.float32)
    mod_w = scatter_about(key_of[6], (WDIM, D), (0.3 / WDIM ** 0.5), 0.078125, ((0, 8),))
    sel_w = scatter_about(key_of[7], (WDIM, KERNELS), WDIM ** -0.5, 0.25, ((0, 8),))
    kernel_bank = scatter_about(key_of[8], (KERNELS * 9 * D, D), (9 * D) ** -0.5, 0.0625, ((0, 8),))
    conv_bias = scatter_about(key_of[9], (D,), 0.5, 3.0, ((0, 8),))
    noise_gain = scatter_about(key_of[10], (D,), 0.5, 3.0, ((0, 8),))
    qk_w = scatter_about(key_of[11], (D, D), D ** -0.5, 0.1875, ((0, 8),))
    val_w = scatter_about(key_of[12], (D, D), D ** -0.5, 0.1875, ((0, 8),))
    out_w = scatter_about(key_of[13], (D, D), (D // 8) ** -0.5, 0.5, ((0, 8),))
    cq_w = scatter_about(key_of[14], (D, D), D ** -0.5, 0.1875, ((0, 8),))
    ck_w = scatter_about(key_of[15], (D, D), D ** -0.5, 0.1875, ((0, 8),))
    cv_w = scatter_about(key_of[16], (D, D), D ** -0.5, 0.1875, ((0, 8),))
    co_w = scatter_about(key_of[17], (D, D), (D // 2) ** -0.5, 0.25, ((0, 8),))
    up_w = scatter_about(key_of[18], (D, FFN), D ** -0.5, 0.1875, ((0, 8),))
    up_b = scatter_about(key_of[19], (FFN,), 0.3, 1.75, ((0, 8),))
    down_w = scatter_about(key_of[20], (FFN, D), FFN ** -0.5, 0.09375, ((0, 8),))
    class_table = scatter_about(key_of[21], (CLASSES, CTX * D), 1.0, 6.0, ((1, 8),))
    rgb_w = scatter_about(key_of[22], (3, D), D ** -0.5, 0.1875, ((1, 8),))
    return dict(feat_in=feat_in, style_vec=style_vec, labels=labels, noise_map=noise_map, cot_feat=cot_feat, cot_rgb=cot_rgb, mod_w=mod_w, sel_w=sel_w, kernel_bank=kernel_bank, conv_bias=conv_bias, noise_gain=noise_gain, qk_w=qk_w, val_w=val_w, out_w=out_w, cq_w=cq_w, ck_w=ck_w, cv_w=cv_w, co_w=co_w, up_w=up_w, up_b=up_b, down_w=down_w, class_table=class_table, rgb_w=rgb_w)


HIGH = lax.Precision.HIGHEST
EPSILON = 1e-08
SLOPE = 0.2

@jax.custom_vjp
def low(v):
    return lax.optimization_barrier(v.astype(jnp.bfloat16)).astype(jnp.float32)

@jax.custom_vjp
def low_back(v):
    return v

def low_keep(v):
    return (low(v), None)

def low_pass(kept, grad):
    return (grad,)

def back_keep(v):
    return (v, None)

def back_low(kept, grad):
    return (low(grad),)
low.defvjp(low_keep, low_pass)
low_back.defvjp(back_keep, back_low)

def hdot(left, right):
    return jnp.dot(left, right, precision=HIGH, preferred_element_type=jnp.float32)

def sample_forward(params, image, style_row, noise_row, label):
    mod_w, sel_w, kernel_bank, conv_bias, noise_gain, qk_w, val_w, out_w, cq_w, ck_w, cv_w, co_w, up_w, up_b, down_w, class_table, rgb_w = params
    upsampled = jnp.repeat(jnp.repeat(image, 2, axis=0), 2, axis=1)
    scales = 1.0 + hdot(style_row, mod_w)
    select = jax.nn.softmax(hdot(style_row, sel_w))
    modulated = low(upsampled * scales)
    padded = jnp.pad(modulated, ((1, 1), (1, 1), (0, 0)))
    pieces = []
    for row_off in range(3):
        for col_off in range(3):
            pieces.append(padded[row_off:row_off + SIDE, col_off:col_off + SIDE])
    patches = jnp.concatenate(pieces, axis=-1).reshape(SIDE * SIDE, 9 * D)
    mixed = jnp.einsum('k,kto->to', select, kernel_bank.reshape(KERNELS, 9 * D, D), precision=HIGH)
    demod = lax.rsqrt(lax.optimization_barrier(jnp.sum(jnp.square(mixed * jnp.tile(scales, 9)[:, None]), axis=0)) + EPSILON)
    conv_out = low_back(hdot(patches, low(mixed)))
    pre_act = conv_out * demod + noise_gain * noise_row.reshape(-1, 1) + conv_bias
    hidden = jnp.where(pre_act > 0, pre_act, SLOPE * pre_act)
    hidden_low = low(hidden)
    queries = low(low_back(hdot(hidden_low, qk_w))).reshape(-1, HEADS, HEAD_DIM)
    values = low(low_back(hdot(hidden_low, val_w))).reshape(-1, HEADS, HEAD_DIM)
    key_norm = lax.optimization_barrier(jnp.sum(queries * queries, axis=-1))
    l2_scale = 0.5 * HEAD_DIM ** (-0.5)
    scores = low_back(l2_scale * (2.0 * jnp.einsum('qhd,khd->hqk', queries, queries, precision=HIGH) - key_norm.T[:, None, :]))
    probs = low(jax.nn.softmax(scores, axis=-1))
    attended = low(low_back(jnp.einsum('hqk,khd->qhd', probs, values, precision=HIGH).reshape(-1, D)))
    after_self = hidden + low_back(hdot(attended, out_w))
    self_low = low(after_self)
    cross_q = low(low_back(hdot(self_low, cq_w))).reshape(-1, HEADS, HEAD_DIM)
    context = class_table[label].reshape(CTX, D)
    cross_k = low(low_back(hdot(context, ck_w))).reshape(CTX, HEADS, HEAD_DIM)
    cross_v = low(low_back(hdot(context, cv_w))).reshape(CTX, HEADS, HEAD_DIM)
    cross_s = low_back(jnp.einsum('qhd,jhd->hqj', cross_q, cross_k, precision=HIGH) * HEAD_DIM ** (-0.5))
    cross_p = low(jax.nn.softmax(cross_s, axis=-1))
    cross_o = low(low_back(jnp.einsum('hqj,jhd->qhd', cross_p, cross_v, precision=HIGH).reshape(-1, D)))
    after_cross = after_self + low_back(hdot(cross_o, co_w))
    cross_low = low(after_cross)
    inner = low_back(hdot(cross_low, up_w) + up_b)
    activated = low(jax.nn.gelu(inner))
    after_mlp = after_cross + low_back(hdot(activated, down_w))
    result = low(after_mlp)
    colour = hdot(result, rgb_w.T)
    return (result.reshape(SIDE, SIDE, D), colour.T.reshape(3, SIDE, SIDE))

def reference(feat_in, style_vec, labels, noise_map, cot_feat, cot_rgb, mod_w, sel_w, kernel_bank, conv_bias, noise_gain, qk_w, val_w, out_w, cq_w, ck_w, cv_w, co_w, up_w, up_b, down_w, class_table, rgb_w):
    params = tuple((weight.astype(jnp.float32) for weight in (mod_w, sel_w, kernel_bank, conv_bias, noise_gain, qk_w, val_w, out_w, cq_w, ck_w, cv_w, co_w, up_w, up_b, down_w, class_table, rgb_w)))
    images = feat_in.astype(jnp.float32)
    styles = style_vec.astype(jnp.float32)

    def forward(image_all, param_all):

        def one_sample(sample_item):
            image, style_row, noise_row, label = sample_item
            return sample_forward(param_all, image, style_row, noise_row, label)
        return lax.map(jax.checkpoint(one_sample), (image_all, styles, noise_map, labels))
    outputs, pull = jax.vjp(forward, images, params)
    feat_out, rgb_out = outputs
    grad_x, grads = pull((cot_feat.astype(jnp.float32), cot_rgb))
    r1_value = jnp.mean(grad_x * grad_x)
    return (feat_out.astype(jnp.bfloat16), rgb_out, grad_x, r1_value, grads[0], grads[1], grads[2], grads[3], grads[4], grads[5], grads[6], grads[7], grads[8], grads[9], grads[10], grads[11], grads[12], grads[13], grads[14], grads[15], grads[16])
```

```python
import jax
import jax.numpy as jnp
from jax import lax
from jax.experimental import pallas as pl
from jax.experimental.pallas import tpu as pltpu
from jax.sharding import PartitionSpec as P

HEAD_DIM = 64


HIGH = lax.Precision.HIGHEST
EPSILON = 1e-08
SLOPE = 0.2


def with_halo(cells, sides, width):
    for axis, dim in sides:
        count = lax.axis_size(axis)
        ends = count - 1
        head = lax.slice_in_dim(cells, 0, width, axis=dim)
        tail = lax.slice_in_dim(cells, cells.shape[dim] - width, cells.shape[dim], axis=dim)
        cells = jnp.concatenate(
            [
                lax.ppermute(tail, axis, [(i, (i + 1) % count) for i in range(ends)]),
                cells,
                lax.ppermute(head, axis, [((i + 1) % count, i) for i in range(ends)]),
            ],
            axis=dim,
        )
    return cells


def product(left, right):
    return jnp.dot(left, right, preferred_element_type=jnp.float32)


def kernel_mix(bank_split, select_row):
    mixed_kernel = select_row[0] * bank_split[0].astype(jnp.float32)
    mixed_kernel = mixed_kernel + select_row[1] * bank_split[1].astype(jnp.float32)
    return mixed_kernel


def gather_taps(padded, out_rows, out_cols, flipped):
    pieces = []
    for row_off in range(3):
        for col_off in range(3):
            if flipped:
                pieces.append(
                    padded[
                        :,
                        2 - row_off : 2 - row_off + out_rows,
                        2 - col_off : 2 - col_off + out_cols,
                    ]
                )
            else:
                pieces.append(padded[:, row_off : row_off + out_rows, col_off : col_off + out_cols])
    return jnp.concatenate(pieces, axis=-1)


def per_device(
    feat_in,
    style_vec,
    labels,
    noise_map,
    cot_feat,
    cot_rgb,
    mod_w,
    sel_w,
    kernel_bank,
    conv_bias,
    noise_gain,
    qk_w,
    val_w,
    out_w,
    cq_w,
    ck_w,
    cv_w,
    co_w,
    up_w,
    up_b,
    down_w,
    class_table,
    rgb_w,
):
    f32 = jnp.float32
    bf16 = jnp.bfloat16
    (
        mod_full,
        sel_full,
        bias_full,
        gain_full,
        qk_full,
        val_full,
        out_full,
        cq_full,
        ck_full,
        cv_full,
        co_full,
        up_full,
        upb_full,
        down_full,
        table_full,
        rgb_full,
    ) = (
        lax.all_gather(mod_w, "batch", axis=0, tiled=True),
        lax.all_gather(sel_w, "batch", axis=0, tiled=True),
        lax.all_gather(conv_bias, "batch", axis=0, tiled=True),
        lax.all_gather(noise_gain, "batch", axis=0, tiled=True),
        lax.all_gather(qk_w, "batch", axis=0, tiled=True),
        lax.all_gather(val_w, "batch", axis=0, tiled=True),
        lax.all_gather(out_w, "batch", axis=0, tiled=True),
        lax.all_gather(cq_w, "batch", axis=0, tiled=True),
        lax.all_gather(ck_w, "batch", axis=0, tiled=True),
        lax.all_gather(cv_w, "batch", axis=0, tiled=True),
        lax.all_gather(co_w, "batch", axis=0, tiled=True),
        lax.all_gather(up_w, "batch", axis=0, tiled=True),
        lax.all_gather(up_b, "batch", axis=0, tiled=True),
        lax.all_gather(down_w, "batch", axis=0, tiled=True),
        lax.all_gather(class_table, "batch", axis=1, tiled=True),
        lax.all_gather(rgb_w, "batch", axis=1, tiled=True),
    )
    bank_full = lax.all_gather(kernel_bank, "batch", axis=0, tiled=True)
    samples, in_rows, in_cols, channels = feat_in.shape
    out_rows = 2 * in_rows
    out_cols = 2 * in_cols
    pixels = out_rows * out_cols
    span = 9 * channels
    kernels = bank_full.shape[0] // span
    head_dim = HEAD_DIM
    head_count = channels // head_dim
    bank_split = bank_full.reshape(kernels, span, channels)
    scales = 1.0 + product(style_vec, mod_full)
    select = jax.nn.softmax(product(style_vec, sel_full), axis=-1)
    scale_tiled = jnp.tile(scales, (1, 9))
    upsampled = jnp.repeat(jnp.repeat(feat_in, 2, axis=1), 2, axis=2)
    modulated = (upsampled.astype(f32) * scales[:, None, None, :]).astype(bf16)
    with_rim = with_halo(modulated, (("rows", 1),), 1)
    padded = jnp.pad(with_rim, ((0, 0), (0, 0), (1, 1), (0, 0)))
    patches = gather_taps(padded, out_rows, out_cols, False).reshape(samples, pixels, span)

    def conv_forward(sample_item):
        patch_row, select_row, scale_row = sample_item
        mixed_kernel = kernel_mix(bank_split, select_row)
        demod_row = lax.rsqrt(
            jnp.sum(jnp.square(mixed_kernel * scale_row[:, None]), axis=0) + EPSILON
        )
        return (product(patch_row, mixed_kernel.astype(bf16)), demod_row, mixed_kernel)

    conv_out, demodulate, mixed_all = lax.map(conv_forward, (patches, select, scale_tiled))
    noise_flat = noise_map.reshape(samples, pixels, 1)
    pre_act = (
        conv_out * demodulate[:, None, :]
        + gain_full.astype(f32) * noise_flat
        + bias_full.astype(f32)
    )
    hidden = jnp.where(pre_act > 0, pre_act, SLOPE * pre_act)
    hidden_low = hidden.astype(bf16)
    queries = product(hidden_low, qk_full).astype(bf16)
    values = product(hidden_low, val_full).astype(bf16)
    all_queries, all_values = (
        lax.all_gather(queries, "rows", axis=1, tiled=True),
        lax.all_gather(values, "rows", axis=1, tiled=True),
    )
    query_h = queries.reshape(samples, pixels, head_count, head_dim)
    key_h = all_queries.reshape(samples, -1, head_count, head_dim)
    value_h = all_values.reshape(samples, -1, head_count, head_dim)
    key_f32 = key_h.astype(f32)
    key_norm = jnp.transpose(jnp.sum(jnp.square(key_f32), axis=-1), (0, 2, 1))[:, :, None, :]
    l2_scale = 0.5 * head_dim ** (-0.5)

    def self_scores():
        inner_dots = jnp.einsum("bqhd,bkhd->bhqk", query_h, key_h, preferred_element_type=f32)
        return l2_scale * (2.0 * inner_dots - key_norm)

    scores = self_scores()
    row_max = jnp.max(scores, axis=-1, keepdims=True)
    log_total = row_max + jnp.log(jnp.sum(jnp.exp(scores - row_max), axis=-1, keepdims=True))
    probs_low = jnp.exp(scores - log_total).astype(bf16)
    attended = (
        jnp.einsum("bhqk,bkhd->bqhd", probs_low, value_h, preferred_element_type=f32)
        .reshape(samples, pixels, channels)
        .astype(bf16)
    )
    after_self = hidden + product(attended, out_full)
    self_low = after_self.astype(bf16)
    cross_q = product(self_low, cq_full).astype(bf16).reshape(samples, pixels, head_count, head_dim)
    classes = table_full.shape[0]
    one_hot = (labels[:, None] == jnp.arange(classes)[None, :]).astype(bf16)
    contexts = table_full.shape[1] // channels
    context = product(one_hot, table_full).astype(bf16).reshape(samples, contexts, channels)
    cross_k = jnp.einsum("bjc,cd->bjd", context, ck_full, preferred_element_type=f32).astype(bf16)
    cross_v = jnp.einsum("bjc,cd->bjd", context, cv_full, preferred_element_type=f32).astype(bf16)
    key_cross = cross_k.reshape(samples, contexts, head_count, head_dim)
    value_cross = cross_v.reshape(samples, contexts, head_count, head_dim)
    cross_scale = head_dim ** (-0.5)
    cross_s = (
        jnp.einsum("bqhd,bjhd->bhqj", cross_q, key_cross, preferred_element_type=f32) * cross_scale
    )
    cross_p = jax.nn.softmax(cross_s, axis=-1)
    cross_plow = cross_p.astype(bf16)
    cross_o = (
        jnp.einsum("bhqj,bjhd->bqhd", cross_plow, value_cross, preferred_element_type=f32)
        .reshape(samples, pixels, channels)
        .astype(bf16)
    )
    after_cross = after_self + product(cross_o, co_full)
    cross_low = after_cross.astype(bf16)
    inner = product(cross_low, up_full) + upb_full.astype(f32)
    activated, gelu_pull = jax.vjp(jax.nn.gelu, inner)
    act_low = activated.astype(bf16)
    after_mlp = after_cross + product(act_low, down_full)
    result = after_mlp.astype(bf16)
    colour = product(result, rgb_full.T)
    rgb_out = jnp.transpose(colour, (0, 2, 1)).reshape(samples, 3, out_rows, out_cols)
    grad_rgb = jnp.transpose(cot_rgb.reshape(samples, 3, pixels), (0, 2, 1))
    grad_res = cot_feat.reshape(samples, pixels, channels).astype(f32) + jnp.dot(
        grad_rgb, rgb_full.astype(f32), precision=HIGH
    )
    grad_rgb_w = jnp.einsum("bpk,bpc->kc", grad_rgb, result.astype(f32), precision=HIGH)
    branch = grad_res.astype(bf16)
    grad_down_w = jnp.einsum("bpf,bpc->fc", act_low, branch, preferred_element_type=f32)
    (grad_inner,) = gelu_pull(product(branch, down_full.T))
    inner_low = grad_inner.astype(bf16)
    grad_up_b = jnp.sum(inner_low.astype(f32), axis=(0, 1))
    grad_up_w = jnp.einsum("bpc,bpf->cf", cross_low, inner_low, preferred_element_type=f32)
    grad_cross = grad_res + product(inner_low, up_full.T)
    cbranch = grad_cross.astype(bf16)
    grad_co_w = jnp.einsum("bpc,bpd->cd", cross_o, cbranch, preferred_element_type=f32)
    grad_co = (
        product(cbranch, co_full.T).astype(bf16).reshape(samples, pixels, head_count, head_dim)
    )
    grad_cp = jnp.einsum("bqhd,bjhd->bhqj", grad_co, value_cross, preferred_element_type=f32)
    grad_cv = (
        jnp.einsum("bhqj,bqhd->bjhd", cross_plow, grad_co, preferred_element_type=f32)
        .astype(bf16)
        .reshape(samples, contexts, channels)
    )
    grad_cs = (cross_p * (grad_cp - jnp.sum(grad_cp * cross_p, axis=-1, keepdims=True))).astype(
        bf16
    )
    grad_cq = (
        (
            jnp.einsum("bhqj,bjhd->bqhd", grad_cs, key_cross, preferred_element_type=f32)
            * cross_scale
        )
        .astype(bf16)
        .reshape(samples, pixels, channels)
    )
    grad_ck = (
        (jnp.einsum("bhqj,bqhd->bjhd", grad_cs, cross_q, preferred_element_type=f32) * cross_scale)
        .astype(bf16)
        .reshape(samples, contexts, channels)
    )
    grad_cq_w = jnp.einsum("bpc,bpd->cd", self_low, grad_cq, preferred_element_type=f32)
    grad_ck_w = jnp.einsum("bjc,bjd->cd", context, grad_ck, preferred_element_type=f32)
    grad_cv_w = jnp.einsum("bjc,bjd->cd", context, grad_cv, preferred_element_type=f32)
    grad_context = jnp.einsum(
        "bjd,cd->bjc", grad_ck, ck_full, preferred_element_type=f32
    ) + jnp.einsum("bjd,cd->bjc", grad_cv, cv_full, preferred_element_type=f32)
    grad_table = jnp.dot(
        one_hot.astype(f32).T, grad_context.reshape(samples, contexts * channels), precision=HIGH
    )
    grad_self = grad_cross + product(grad_cq, cq_full.T)
    sbranch = grad_self.astype(bf16)
    grad_out_w = jnp.einsum("bpc,bpd->cd", attended, sbranch, preferred_element_type=f32)
    grad_att = (
        product(sbranch, out_full.T).astype(bf16).reshape(samples, pixels, head_count, head_dim)
    )
    probs = jnp.exp(self_scores() - log_total)
    probs_again = probs.astype(bf16)
    grad_probs = jnp.einsum("bqhd,bkhd->bhqk", grad_att, value_h, preferred_element_type=f32)
    grad_vall = jnp.einsum("bhqk,bqhd->bkhd", probs_again, grad_att, preferred_element_type=f32)
    grad_s = (probs * (grad_probs - jnp.sum(grad_probs * probs, axis=-1, keepdims=True))).astype(
        bf16
    )
    grad_qloc = (
        2.0 * l2_scale * jnp.einsum("bhqk,bkhd->bqhd", grad_s, key_h, preferred_element_type=f32)
    )
    col_total = jnp.transpose(jnp.sum(grad_s.astype(f32), axis=2), (0, 2, 1))[:, :, :, None]
    grad_kall = (
        2.0
        * l2_scale
        * (
            jnp.einsum("bhqk,bqhd->bkhd", grad_s, query_h, preferred_element_type=f32)
            - key_f32 * col_total
        )
    )
    back_keys, back_values = (
        lax.psum_scatter(
            grad_kall.reshape(samples, -1, channels).astype(jnp.bfloat16),
            "rows",
            scatter_dimension=1,
            tiled=True,
        ).astype(jnp.float32),
        lax.psum_scatter(
            grad_vall.reshape(samples, -1, channels).astype(jnp.bfloat16),
            "rows",
            scatter_dimension=1,
            tiled=True,
        ).astype(jnp.float32),
    )
    grad_q = (grad_qloc.reshape(samples, pixels, channels) + back_keys).astype(bf16)
    grad_v = back_values.astype(bf16)
    grad_qk_w = jnp.einsum("bpc,bpd->cd", hidden_low, grad_q, preferred_element_type=f32)
    grad_val_w = jnp.einsum("bpc,bpd->cd", hidden_low, grad_v, preferred_element_type=f32)
    grad_hidden = grad_self + product(grad_q, qk_full.T) + product(grad_v, val_full.T)
    grad_pre = grad_hidden * jnp.where(pre_act > 0, 1.0, SLOPE)
    grad_gain = jnp.sum(grad_pre * noise_flat, axis=(0, 1))
    grad_bias = jnp.sum(grad_pre, axis=(0, 1))
    grad_demod = jnp.sum(grad_pre * conv_out, axis=1)
    demod_coef = demodulate**3 * grad_demod
    grad_conv = (grad_pre * demodulate[:, None, :]).astype(bf16)
    grad_rim = with_halo(
        grad_conv.reshape(samples, out_rows, out_cols, channels), (("rows", 1),), 1
    )
    grad_pad = jnp.pad(grad_rim, ((0, 0), (0, 0), (1, 1), (0, 0)))
    grad_patches = gather_taps(grad_pad, out_rows, out_cols, True).reshape(samples, pixels, span)

    def conv_backward(sample_item):
        gpatch_row, mixed_kernel, scale_row, coef_row = sample_item
        taps_low = mixed_kernel.astype(bf16).reshape(9, channels, channels)
        grad_mod = jnp.einsum(
            "pto,tio->pi",
            gpatch_row.reshape(pixels, 9, channels),
            taps_low,
            preferred_element_type=f32,
        )
        scale_term = -scale_row[:channels] * jnp.sum(
            (jnp.square(mixed_kernel) * coef_row[None, :]).reshape(9, channels, channels),
            axis=(0, 2),
        )
        return (grad_mod, scale_term)

    grad_mod, scale_term = lax.map(
        conv_backward, (grad_patches, mixed_all, scale_tiled, demod_coef)
    )
    block_rows = span // 8

    def tap_block(index, carry):
        bank_acc, select_acc = carry
        tap_row = index * block_rows
        patch_cols = lax.dynamic_slice_in_dim(patches, tap_row, block_rows, 2)
        grad_taps = jnp.einsum("bpt,bpo->bto", patch_cols, grad_conv, preferred_element_type=f32)
        bank_rows = lax.dynamic_slice_in_dim(bank_split, tap_row, block_rows, 1).astype(f32)
        mixed_rows = lax.dynamic_slice_in_dim(mixed_all, tap_row, block_rows, 1)
        scale_rows = lax.dynamic_slice_in_dim(scale_tiled, tap_row, block_rows, 1)
        grad_mixed = (
            grad_taps - mixed_rows * jnp.square(scale_rows)[:, :, None] * demod_coef[:, None, :]
        )
        select_acc = select_acc + jnp.einsum("kto,bto->bk", bank_rows, grad_mixed, precision=HIGH)
        bank_piece = jnp.einsum("bk,bto->kto", select, grad_mixed, precision=HIGH)
        bank_acc = lax.dynamic_update_slice_in_dim(bank_acc, bank_piece, tap_row, 1)
        return (bank_acc, select_acc)

    bank_acc, grad_select = lax.fori_loop(
        0,
        8,
        tap_block,
        (jnp.zeros((kernels, span, channels), f32), jnp.zeros((samples, kernels), f32)),
    )
    bank_flat = bank_acc.reshape(kernels * span, channels)
    grad_mod = grad_mod.reshape(samples, out_rows, out_cols, channels)
    grad_scales = jnp.sum(grad_mod * upsampled.astype(f32), axis=(1, 2)) + scale_term
    grad_up = grad_mod * scales[:, None, None, :]
    grad_input = grad_up.reshape(samples, in_rows, 2, in_cols, 2, channels).sum(axis=(2, 4))
    grad_logits = select * (grad_select - jnp.sum(grad_select * select, axis=-1, keepdims=True))
    style_f32 = style_vec.astype(f32)
    grad_mod_w = jnp.dot(style_f32.T, grad_scales, precision=HIGH)
    grad_sel_w = jnp.dot(style_f32.T, grad_logits, precision=HIGH)
    (
        sum_mod,
        sum_sel,
        sum_bias,
        sum_gain,
        sum_qk,
        sum_val,
        sum_out,
        sum_cq,
        sum_ck,
        sum_cv,
        sum_co,
        sum_up,
        sum_upb,
        sum_down,
        sum_table,
        sum_rgb,
    ) = (
        lax.psum_scatter(grad_mod_w, "batch", scatter_dimension=0, tiled=True),
        lax.psum_scatter(grad_sel_w, "batch", scatter_dimension=0, tiled=True),
        lax.psum_scatter(grad_bias, "batch", scatter_dimension=0, tiled=True),
        lax.psum_scatter(grad_gain, "batch", scatter_dimension=0, tiled=True),
        lax.psum_scatter(grad_qk_w, "batch", scatter_dimension=0, tiled=True),
        lax.psum_scatter(grad_val_w, "batch", scatter_dimension=0, tiled=True),
        lax.psum_scatter(grad_out_w, "batch", scatter_dimension=0, tiled=True),
        lax.psum_scatter(grad_cq_w, "batch", scatter_dimension=0, tiled=True),
        lax.psum_scatter(grad_ck_w, "batch", scatter_dimension=0, tiled=True),
        lax.psum_scatter(grad_cv_w, "batch", scatter_dimension=0, tiled=True),
        lax.psum_scatter(grad_co_w, "batch", scatter_dimension=0, tiled=True),
        lax.psum_scatter(grad_up_w, "batch", scatter_dimension=0, tiled=True),
        lax.psum_scatter(grad_up_b, "batch", scatter_dimension=0, tiled=True),
        lax.psum_scatter(grad_down_w, "batch", scatter_dimension=0, tiled=True),
        lax.psum_scatter(grad_table, "batch", scatter_dimension=1, tiled=True),
        lax.psum_scatter(grad_rgb_w, "batch", scatter_dimension=1, tiled=True),
    )
    bank_part = lax.psum_scatter(bank_flat, "batch", scatter_dimension=0, tiled=True)
    (
        sum_mod,
        sum_sel,
        sum_bias,
        sum_gain,
        sum_qk,
        sum_val,
        sum_out,
        sum_cq,
        sum_ck,
        sum_cv,
        sum_co,
        sum_up,
        sum_upb,
        sum_down,
        sum_table,
        sum_rgb,
        bank_total,
    ) = (
        lax.psum(sum_mod.astype(jnp.bfloat16), "rows").astype(jnp.float32),
        lax.psum(sum_sel.astype(jnp.bfloat16), "rows").astype(jnp.float32),
        lax.psum(sum_bias.astype(jnp.bfloat16), "rows").astype(jnp.float32),
        lax.psum(sum_gain.astype(jnp.bfloat16), "rows").astype(jnp.float32),
        lax.psum(sum_qk.astype(jnp.bfloat16), "rows").astype(jnp.float32),
        lax.psum(sum_val.astype(jnp.bfloat16), "rows").astype(jnp.float32),
        lax.psum(sum_out.astype(jnp.bfloat16), "rows").astype(jnp.float32),
        lax.psum(sum_cq.astype(jnp.bfloat16), "rows").astype(jnp.float32),
        lax.psum(sum_ck.astype(jnp.bfloat16), "rows").astype(jnp.float32),
        lax.psum(sum_cv.astype(jnp.bfloat16), "rows").astype(jnp.float32),
        lax.psum(sum_co.astype(jnp.bfloat16), "rows").astype(jnp.float32),
        lax.psum(sum_up.astype(jnp.bfloat16), "rows").astype(jnp.float32),
        lax.psum(sum_upb.astype(jnp.bfloat16), "rows").astype(jnp.float32),
        lax.psum(sum_down.astype(jnp.bfloat16), "rows").astype(jnp.float32),
        lax.psum(sum_table.astype(jnp.bfloat16), "rows").astype(jnp.float32),
        lax.psum(sum_rgb.astype(jnp.bfloat16), "rows").astype(jnp.float32),
        lax.psum(bank_part.astype(jnp.bfloat16), "rows").astype(jnp.float32),
    )
    entry_count = float(
        samples * lax.axis_size("batch") * in_rows * lax.axis_size("rows") * in_cols * channels
    )
    r1_value = lax.psum(jnp.sum(jnp.square(grad_input)), ("batch", "rows")) / entry_count
    feat_out = result.reshape(samples, out_rows, out_cols, channels)
    return (
        feat_out,
        rgb_out,
        grad_input,
        r1_value,
        sum_mod,
        sum_sel,
        bank_total,
        sum_bias,
        sum_gain,
        sum_qk,
        sum_val,
        sum_out,
        sum_cq,
        sum_ck,
        sum_cv,
        sum_co,
        sum_up,
        sum_upb,
        sum_down,
        sum_table,
        sum_rgb,
    )


def gather(x, axis_name, axis=0):
    return lax.all_gather(x, axis_name, axis=axis, tiled=True)


def trade(x):
    return lax.all_to_all(x, "batch", 0, 0, tiled=True)


def swap_pair(x):
    return lax.ppermute(x, "batch", [(i, i ^ 1) for i in range(8)])


def move_table(turn):
    table = []
    for d in range(8):
        for z in range(4):
            slot = (z % 2) ^ turn
            pair = 2 * (d % 2) + slot
            table.append((4 * d + z, 4 * (2 * pair + z // 2) + d // 2))
    return table


def to_pixels(x, odd_z, odd_pair):
    sent = jnp.where(odd_z, x[::-1], x)
    first = lax.ppermute(sent[0], ("batch", "rows"), move_table(0))
    second = lax.ppermute(sent[1], ("batch", "rows"), move_table(1))
    return jnp.where(odd_pair, jnp.stack([second, first]), jnp.stack([first, second]))


def from_pixels(x, odd_z, odd_pair):
    sent = jnp.where(odd_pair, x[::-1], x)
    back = [[(b, a) for a, b in move_table(turn)] for turn in range(2)]
    first = lax.ppermute(sent[0], ("batch", "rows"), back[0])
    second = lax.ppermute(sent[1], ("batch", "rows"), back[1])
    return jnp.where(odd_z, jnp.stack([second, first]), jnp.stack([first, second]))


def contract(left, right, dims, precision=None):
    return lax.dot_general(
        left, right, (dims, ((), ())), precision=precision, preferred_element_type=jnp.float32
    )


def conv_kernel(select_ref, patch_ref, bank_ref, scale_ref, out_ref, square_ref, acc_ref, sum_ref):
    col, row = pl.program_id(0), pl.program_id(1)
    start = jnp.logical_and(col == 0, row == 0)
    last = jnp.logical_and(col == 2, row == 2)

    @pl.when(start)
    def _():
        acc_ref[...] = jnp.zeros_like(acc_ref)
        sum_ref[...] = jnp.zeros_like(sum_ref)

    first = bank_ref[0, 0].astype(jnp.float32)
    second = bank_ref[1, 0].astype(jnp.float32)
    for b in range(4):
        mixed = select_ref[b, 0] * first + select_ref[b, 1] * second
        scaled = mixed * scale_ref[b]
        sum_ref[b] += jnp.sum(jnp.square(scaled).reshape(-1, 8, 128), axis=0)
        begin = pl.multiple_of(row * 16, 16)
        left = patch_ref[0, b, pl.ds(begin, 256), :]
        acc_ref[b] += jnp.dot(left, mixed.astype(jnp.bfloat16), preferred_element_type=jnp.float32)

    @pl.when(last)
    def _():
        out_ref[...] = acc_ref[...]
        square_ref[...] = sum_ref[...]


def conv_forward_plane(select, patch_cols, bank_cols, scale_cols):
    samples, _, width = patch_cols.shape[1:]
    cols = bank_cols.shape[-1]
    return pl.pallas_call(
        conv_kernel,
        grid=(3, 3),
        in_specs=[
            pl.BlockSpec(memory_space=pltpu.SMEM),
            pl.BlockSpec((1, samples, 288, width), lambda c, a: (c, 0, 0, 0)),
            pl.BlockSpec((2, 1, width, cols), lambda c, a: (0, 3 * a + c, 0, 0)),
            pl.BlockSpec((samples, width, cols), lambda c, a: (0, 0, 0)),
        ],
        out_specs=[
            pl.BlockSpec((samples, 256, cols), lambda c, a: (0, 0, 0)),
            pl.BlockSpec((samples, 8, cols), lambda c, a: (0, 0, 0)),
        ],
        out_shape=[
            jax.ShapeDtypeStruct((samples, 256, cols), jnp.float32),
            jax.ShapeDtypeStruct((samples, 8, cols), jnp.float32),
        ],
        scratch_shapes=[
            pltpu.VMEM((samples, 256, cols), jnp.float32),
            pltpu.VMEM((samples, 8, cols), jnp.float32),
        ],
        compiler_params=pltpu.CompilerParams(vmem_limit_bytes=40 << 20),
        cost_estimate=pl.CostEstimate(
            flops=2 * samples * 256 * 9 * width * cols, bytes_accessed=20 << 20, transcendentals=0
        ),
        name="conv_plane",
    )(select, patch_cols, bank_cols, scale_cols)


def head_scores(query, key):
    squares = jnp.square(key.astype(jnp.float32))
    upper = squares.astype(jnp.bfloat16)
    lower = (squares - upper.astype(jnp.float32)).astype(jnp.bfloat16)
    ones = jnp.ones((8, HEAD_DIM), jnp.bfloat16)
    over_last = ((1,), (1,))
    norms = contract(ones, upper, over_last) + contract(ones, lower, over_last)
    scale = 0.5 * HEAD_DIM ** (-0.5)
    return scale * (2.0 * contract(query, key, over_last) - norms[0:1])


def head_softmax(scores):
    raised = jnp.exp(scores - jnp.max(scores, axis=-1, keepdims=True))
    return raised / jnp.sum(raised, axis=-1, keepdims=True)


def attend_kernel(query_ref, key_ref, value_ref, out_ref):
    for h in range(2):
        part = slice(h * HEAD_DIM, (h + 1) * HEAD_DIM)
        probs = head_softmax(head_scores(query_ref[:, part], key_ref[:, part]))
        out_ref[:, part] = jnp.dot(
            probs.astype(jnp.bfloat16), value_ref[:, part], preferred_element_type=jnp.float32
        ).astype(jnp.bfloat16)


def attend(query, key, value):
    pixels, width = query.shape
    everything = key.shape[0]
    pair = 2 * HEAD_DIM
    return pl.pallas_call(
        attend_kernel,
        grid=(width // pair,),
        in_specs=[
            pl.BlockSpec((pixels, pair), lambda i: (0, i)),
            pl.BlockSpec((everything, pair), lambda i: (0, i)),
            pl.BlockSpec((everything, pair), lambda i: (0, i)),
        ],
        out_specs=pl.BlockSpec((pixels, pair), lambda i: (0, i)),
        out_shape=jax.ShapeDtypeStruct((pixels, width), jnp.bfloat16),
        cost_estimate=pl.CostEstimate(
            flops=4 * pixels * everything * width, bytes_accessed=3 << 20, transcendentals=1 << 19
        ),
        name="attend",
    )(query, key, value)


def attend_back_kernel(query_ref, key_ref, value_ref, grad_ref, gq_ref, gk_ref, gv_ref):
    bf16 = jnp.bfloat16
    twice = 2.0 * (0.5 * HEAD_DIM ** (-0.5))
    for h in range(2):
        part = slice(h * HEAD_DIM, (h + 1) * HEAD_DIM)
        query, key, value, grad = query_ref[:, part], key_ref[:, part], value_ref[:, part], grad_ref[:, part]
        probs = head_softmax(head_scores(query, key))
        grad_probs = contract(grad, value, ((1,), (1,)))
        mean = jnp.sum(grad_probs * probs, axis=-1, keepdims=True)
        grad_s = (probs * (grad_probs - mean)).astype(bf16)
        gv_ref[:, part] = contract(probs.astype(bf16), grad, ((0,), (0,)))
        gq_ref[:, part] = twice * jnp.dot(grad_s, key, preferred_element_type=jnp.float32)
        both = jnp.concatenate([query, jnp.ones_like(query)], axis=1)
        sums = contract(grad_s, both, ((0,), (0,)))
        gk_ref[:, part] = twice * (
            sums[:, :HEAD_DIM] - key.astype(jnp.float32) * sums[:, HEAD_DIM:]
        )


def attend_back(query, key, value, grad):
    pixels, width = query.shape
    everything = key.shape[0]
    pair = 2 * HEAD_DIM
    few = pl.BlockSpec((pixels, pair), lambda i: (0, i))
    many = pl.BlockSpec((everything, pair), lambda i: (0, i))
    f32 = jnp.float32
    return pl.pallas_call(
        attend_back_kernel,
        grid=(width // pair,),
        in_specs=[few, many, many, few],
        out_specs=[few, many, many],
        out_shape=[
            jax.ShapeDtypeStruct((pixels, width), f32),
            jax.ShapeDtypeStruct((everything, width), f32),
            jax.ShapeDtypeStruct((everything, width), f32),
        ],
        cost_estimate=pl.CostEstimate(
            flops=14 * pixels * everything * width, bytes_accessed=5 << 20, transcendentals=1 << 19
        ),
        name="attend_back",
    )(query, key, value, grad)


def bank_kernel(tap_ref, part_ref, left_ref, right_ref, own_ref, other_ref, same_ref, cross_ref, coef_ref, out_ref):
    del tap_ref, part_ref
    first = ((0,), (0,))
    out_ref[...] = (
        contract(left_ref[...], right_ref[0], first)
        - own_ref[...].astype(jnp.float32) * contract(same_ref[...], coef_ref[...], first, HIGH)
        - other_ref[...].astype(jnp.float32) * contract(cross_ref[...], coef_ref[...], first, HIGH)
    )


def bank_gradient(taps, parts, left, right, own, other, same, cross, coef):
    lows, width = left.shape
    count = taps.shape[0]
    rows = own.shape[0] // count
    out_cols = own.shape[1]
    samples = coef.shape[0]
    return pl.pallas_call(
        bank_kernel,
        grid_spec=pltpu.PrefetchScalarGridSpec(
            num_scalar_prefetch=2,
            grid=(count,),
            in_specs=[
                pl.BlockSpec((lows, rows), lambda m, t, q: (0, q[m])),
                pl.BlockSpec((1, lows, out_cols), lambda m, t, q: (t[m], 0, 0)),
                pl.BlockSpec((rows, out_cols), lambda m, t, q: (m, 0)),
                pl.BlockSpec((rows, out_cols), lambda m, t, q: (m, 0)),
                pl.BlockSpec((samples, rows), lambda m, t, q: (0, q[m])),
                pl.BlockSpec((samples, rows), lambda m, t, q: (0, q[m])),
                pl.BlockSpec((samples, out_cols), lambda m, t, q: (0, 0)),
            ],
            out_specs=pl.BlockSpec((rows, out_cols), lambda m, t, q: (m, 0)),
        ),
        out_shape=jax.ShapeDtypeStruct((own.shape[0], out_cols), jnp.float32),
        compiler_params=pltpu.CompilerParams(vmem_limit_bytes=40 << 20),
        cost_estimate=pl.CostEstimate(
            flops=2 * lows * own.shape[0] * out_cols, bytes_accessed=32 << 20, transcendentals=0
        ),
        name="bank_gradient",
    )(taps, parts, left, right, own, other, same, cross, coef)


def pooled_taps(grid):
    n, side, _, channels = grid.shape
    half = side // 2

    def pool(x, axis):
        shape = x.shape[:axis] + (half, 2) + x.shape[axis + 1 :]
        split = x.reshape(shape)
        even = lax.index_in_dim(split, 0, axis + 1, keepdims=False)
        odd = lax.index_in_dim(split, 1, axis + 1, keepdims=False)
        pad = [(0, 0)] * even.ndim
        pad[axis] = (0, 1)
        later = lax.slice_in_dim(jnp.pad(even, pad), 1, half + 1, axis=axis)
        pad[axis] = (1, 0)
        earlier = lax.slice_in_dim(jnp.pad(odd, pad), 0, half, axis=axis)
        return [odd + later, even + odd, earlier + even]

    wide = grid.astype(jnp.float32)
    return jnp.stack(
        [piece.astype(jnp.bfloat16) for by_row in pool(wide, 1) for piece in pool(by_row, 2)]
    )


def by_planes(
    feat_in,
    style_vec,
    labels,
    noise_map,
    cot_feat,
    cot_rgb,
    mod_w,
    sel_w,
    kernel_bank,
    conv_bias,
    noise_gain,
    qk_w,
    val_w,
    out_w,
    cq_w,
    ck_w,
    cv_w,
    co_w,
    up_w,
    up_b,
    down_w,
    class_table,
    rgb_w,
):
    f32, bf16 = jnp.float32, jnp.bfloat16
    device, plane = lax.axis_index("batch"), lax.axis_index("rows")
    pair, member = device // 2, device % 2
    odd_z, odd_pair = plane % 2 == 1, pair % 2 == 1
    slots, in_rows, in_cols, channels = feat_in.shape
    total = 8 * slots
    held = total // 4
    piece = 2 * in_rows * 2 * in_cols
    pixels = 2 * piece
    lows = 4 * in_rows * in_cols
    style_width = style_vec.shape[1]
    own_style = style_width // 8
    slim = channels // 8
    head_count = channels // HEAD_DIM

    packed = jnp.concatenate(
        [
            style_vec.astype(f32).reshape(-1),
            conv_bias.astype(f32),
            noise_gain.astype(f32),
            rgb_w.astype(f32).reshape(-1),
            labels.astype(f32),
            jnp.zeros((126,), f32),
        ]
    ).reshape(-1, 128)
    smalls = gather(packed[None], "batch").reshape(8, -1)
    at = slots * style_width
    style_all = smalls[:, :at].reshape(total, style_width).astype(bf16)
    bias_full = smalls[:, at : at + slim].reshape(channels)
    gain_full = smalls[:, at + slim : at + 2 * slim].reshape(channels)
    rgb_full = jnp.transpose(smalls[:, at + 2 * slim : at + 5 * slim].reshape(8, 3, slim), (1, 0, 2)).reshape(3, channels)
    labels_all = smalls[:, at + 5 * slim : at + 5 * slim + slots].reshape(total).astype(jnp.int32)

    feat_part = gather(feat_in, "batch")
    style_own = lax.dynamic_slice_in_dim(style_all, device * own_style, own_style, 1)
    context_own = jnp.take(class_table, labels_all, axis=0)
    partial_styles = jnp.concatenate(
        [
            product(style_own, mod_w),
            jnp.pad(product(style_own, sel_w), ((0, 0), (0, 126))),
            context_own.astype(f32),
        ],
        axis=1,
    )
    styles = gather(partial_styles[None], "batch")
    sums = jnp.sum(styles[:, :, : channels + 128], axis=0)
    scales = 1.0 + sums[:, :channels]
    select = jax.nn.softmax(sums[:, channels : channels + 2], axis=-1)
    context_all = jnp.transpose(styles[:, :, channels + 128 :], (1, 0, 2)).reshape(total, -1).astype(bf16)

    kernels = 2
    bank_sent = jnp.transpose(kernel_bank.reshape(-1, 8, slim), (1, 0, 2))
    bank_cols = trade(bank_sent).reshape(kernels, 9, channels, slim)

    weights = gather(jnp.stack([qk_w, val_w, out_w, cq_w, co_w]), "batch", 1)
    qk_full, val_full, out_full, cq_full, co_full = [weights[i] for i in range(5)]
    feat_all = gather(feat_part[None], "rows")
    feat_all = jnp.transpose(feat_all, (1, 0, 2, 3, 4)).reshape(total, 4 * in_rows, in_cols, channels)
    up_cols = trade(jnp.transpose(up_w.reshape(slim, 8, -1), (1, 0, 2))).reshape(channels, -1)

    quarter = kernel_bank.shape[0] // 4
    bank_quarter = lax.dynamic_slice_in_dim(kernel_bank, plane * quarter, quarter, 0)
    bank_quarter = lax.ppermute(bank_quarter, "batch", [(i, i ^ 4) for i in range(8)])
    bank_other = gather(bank_quarter, "rows")

    cot_pixels = to_pixels(cot_feat.reshape(slots, piece, channels), odd_z, odd_pair).reshape(pixels, channels)
    point_maps = jnp.concatenate(
        [noise_map.reshape(slots, 1, piece), cot_rgb.reshape(slots, 3, piece)], axis=1
    )
    point_maps = to_pixels(point_maps, odd_z, odd_pair)
    point_cols = jnp.transpose(point_maps, (0, 2, 1)).reshape(pixels, 4)
    noise_col, grad_rgb = point_cols[:, :1], point_cols[:, 1:]

    modulated = (feat_all.astype(f32) * scales[:, None, None, :]).astype(bf16)
    first = held * plane
    own_mod = lax.dynamic_slice_in_dim(modulated, first, held, 0)
    own_scales = lax.dynamic_slice_in_dim(scales, first, held, 0)
    own_select = lax.dynamic_slice_in_dim(select, first, held, 0)
    sides = 2 * in_cols
    up_map = jnp.repeat(jnp.repeat(own_mod, 2, axis=1), 2, axis=2)
    up_map = jnp.pad(up_map, ((0, 0), (1, 1), (1, 1), (0, 0)))
    patch_cols = jnp.stack([up_map[:, :, c : c + sides] for c in range(3)])
    patch_cols = patch_cols.reshape(3, held, (sides + 2) * sides, channels)
    scale_cols = jnp.broadcast_to(own_scales[:, :, None], (held, channels, slim))
    conv_cols, square_cols = conv_forward_plane(own_select, patch_cols, bank_cols, scale_cols)
    demod_cols = lax.rsqrt(jnp.sum(square_cols, axis=1) + EPSILON)
    extra = jnp.broadcast_to(jnp.repeat(demod_cols, 2, axis=0)[:, None, :], (8, 8, slim))
    sent = jnp.concatenate([conv_cols.reshape(8, pixels, slim), extra], axis=1)
    back = jnp.transpose(trade(sent), (1, 0, 2)).reshape(pixels + 8, channels)
    conv_out, demodulate = back[:pixels], back[pixels]

    pre_act = conv_out * demodulate + gain_full * noise_col + bias_full
    hidden = jnp.where(pre_act > 0, pre_act, SLOPE * pre_act)
    hidden_low = hidden.astype(bf16)

    queries = product(hidden_low, qk_full).astype(bf16)
    values = product(hidden_low, val_full).astype(bf16)
    theirs = swap_pair(jnp.concatenate([queries, values], axis=1))
    keys_all = jnp.concatenate([queries, theirs[:, :channels]])
    values_all = jnp.concatenate([values, theirs[:, channels:]])
    attended = attend(queries, keys_all, values_all)
    after_self = hidden + product(attended, out_full)
    self_low = after_self.astype(bf16)

    tokens = context_all.shape[1] // channels
    own_context = lax.dynamic_slice_in_dim(context_all, first, held, 0).reshape(held * tokens, channels)
    context_cols = lax.dynamic_slice_in_dim(own_context, device * slim, slim, 1)
    cross_partial = product(context_cols, jnp.concatenate([ck_w, cv_w], axis=1)).reshape(held, tokens, 2 * channels)
    cross_kv = jnp.sum(trade(jnp.repeat(cross_partial, 2, axis=0)), axis=0).astype(bf16)
    in_head = (jnp.arange(channels)[None, :] // HEAD_DIM == jnp.arange(head_count)[:, None])[None]

    def by_head(rows):
        return jnp.where(in_head, rows[:, None, :], 0).astype(bf16).reshape(tokens * head_count, channels)

    key_blocks, value_blocks = by_head(cross_kv[:, :channels]), by_head(cross_kv[:, channels:])
    cross_scale = HEAD_DIM ** (-0.5)
    cross_q = product(self_low, cq_full).astype(bf16)

    def per_token(x):
        return [x[:, i * head_count : (i + 1) * head_count] for i in range(tokens)]

    cross_s = per_token(contract(cross_q, key_blocks, ((1,), (1,))) * cross_scale)
    top = jnp.maximum(jnp.maximum(cross_s[0], cross_s[1]), jnp.maximum(cross_s[2], cross_s[3]))
    raised = [jnp.exp(x - top) for x in cross_s]
    whole = raised[0] + raised[1] + raised[2] + raised[3]
    cross_p = [x / whole for x in raised]
    cross_plow = jnp.concatenate(cross_p, axis=1).astype(bf16)
    cross_o = product(cross_plow, value_blocks).astype(bf16)
    after_cross = after_self + product(cross_o, co_full)
    cross_low = after_cross.astype(bf16)

    grad_res = cot_pixels.astype(f32) + jnp.dot(grad_rgb, rgb_full, precision=HIGH)
    branch_all = gather(grad_res.astype(bf16), "batch")
    cross_all = gather(cross_low, "batch")

    def spread_sum(partial):
        parts = trade(partial.astype(bf16).reshape(8, pixels, channels))
        return jnp.sum(parts.astype(f32), axis=0)

    inner = product(cross_all, up_cols) + up_b.astype(f32)
    activated, gelu_pull = jax.vjp(jax.nn.gelu, inner)
    act_low = activated.astype(bf16)
    (grad_inner,) = gelu_pull(contract(branch_all, down_w, ((1,), (1,))))
    inner_low = grad_inner.astype(bf16)
    grad_cross = grad_res + spread_sum(contract(inner_low, up_cols, ((1,), (1,))))
    result = (after_cross + spread_sum(product(act_low, down_w))).astype(bf16)
    colour = contract(rgb_full.astype(bf16), result, ((1,), (1,)))
    grad_rgb_w = contract(grad_rgb, result.astype(f32), ((0,), (0,)), HIGH)
    over_rows = ((0,), (0,))
    grad_down = contract(act_low, branch_all, over_rows).astype(bf16)
    grad_upb = jnp.sum(inner_low.astype(f32), axis=0)
    grad_up = contract(cross_all, inner_low, over_rows).astype(bf16)
    grad_up = jnp.transpose(trade(grad_up.reshape(8, slim, -1)), (1, 0, 2)).reshape(slim, -1)

    cbranch = grad_cross.astype(bf16)
    grad_co = contract(cbranch, co_full, ((1,), (1,))).astype(bf16)
    grad_cp = per_token(contract(grad_co, value_blocks, ((1,), (1,))))
    mean = grad_cp[0] * cross_p[0] + grad_cp[1] * cross_p[1] + grad_cp[2] * cross_p[2] + grad_cp[3] * cross_p[3]
    grad_cs = jnp.concatenate([p * (g - mean) for p, g in zip(cross_p, grad_cp)], axis=1).astype(bf16)
    grad_cq = (product(grad_cs, key_blocks) * cross_scale).astype(bf16)

    def from_heads(blocks):
        return jnp.sum(jnp.where(in_head, blocks.reshape(tokens, head_count, channels), 0.0), axis=1)

    grad_kv = jnp.concatenate(
        [
            from_heads(contract(grad_cs, cross_q, over_rows)) * cross_scale,
            from_heads(contract(cross_plow, grad_co, over_rows)),
        ],
        axis=1,
    )
    grad_kv = (grad_kv + swap_pair(grad_kv)).astype(bf16)
    kv_all = gather(grad_kv[None], "batch").reshape(held, 2, tokens, 2 * channels)[:, 0].reshape(held * tokens, 2 * channels)
    grad_ck_w = contract(context_cols, kv_all[:, :channels], over_rows).astype(bf16)
    grad_cv_w = contract(context_cols, kv_all[:, channels:], over_rows).astype(bf16)
    grad_context = contract(kv_all[:, :channels], ck_w, ((1,), (1,))) + contract(kv_all[:, channels:], cv_w, ((1,), (1,)))
    grad_self = grad_cross + contract(grad_cq, cq_full, ((1,), (1,)))

    sbranch = grad_self.astype(bf16)
    grad_att = contract(sbranch, out_full, ((1,), (1,))).astype(bf16)
    grad_qloc, grad_kall, grad_vall = attend_back(queries, keys_all, values_all, grad_att)
    theirs = swap_pair(jnp.concatenate([grad_kall[pixels:], grad_vall[pixels:]], axis=1))
    grad_q = (grad_qloc + (grad_kall[:pixels] + theirs[:, :channels])).astype(bf16)
    grad_v = (grad_vall[:pixels] + theirs[:, channels:]).astype(bf16)
    grad_hidden = grad_self + contract(grad_q, qk_full, ((1,), (1,))) + contract(grad_v, val_full, ((1,), (1,)))
    grad_pre = grad_hidden * jnp.where(pre_act > 0, 1.0, SLOPE)
    grad_conv = (grad_pre * demodulate).astype(bf16)

    conv_rows = gather(grad_conv[None], "rows")
    conv_all = gather(conv_rows[None], "batch")
    grad_cols = trade(jnp.transpose(grad_conv.reshape(pixels, 8, slim), (1, 0, 2)))
    point_sums = jnp.concatenate(
        [
            jnp.sum(grad_pre, axis=0)[None],
            jnp.sum(grad_pre * noise_col, axis=0)[None],
            grad_rgb_w,
            jnp.sum(grad_pre * conv_out, axis=0)[None],
            grad_context.reshape(-1, channels),
        ]
    )
    point_all = gather(point_sums[None], "batch")
    demod_all = gather(demodulate[None], "batch")
    col_sums = jnp.sum(lax.dynamic_slice_in_dim(point_all[:, :5], device * slim, slim, 2), axis=0)
    coef_plane = jnp.sum(point_all[:, 5].reshape(held, 2, channels), axis=1) * demod_all[::2] ** 3
    context_grads = jnp.transpose(point_all[:, 6:].reshape(8, held * tokens, slim), (1, 0, 2)).reshape(held, -1)
    table_cols = class_table.shape[1]
    context_grads = lax.dynamic_slice_in_dim(context_grads, device * table_cols, table_cols, 1)
    rows_sent = jnp.concatenate(
        [coef_plane.reshape(-1), context_grads.reshape(-1), col_sums.reshape(-1), grad_upb]
    )
    rows_all = gather(rows_sent.reshape(1, -1, 128), "rows").reshape(4, -1)
    at = held * channels
    coef = rows_all[:, :at].reshape(total, channels)
    context_grads = rows_all[:, at : at + held * table_cols].reshape(total, table_cols)
    at = at + held * table_cols
    rows_total = jnp.sum(rows_all[:, at:], axis=0)
    sum_bias, sum_gain = rows_total[:slim], rows_total[slim : 2 * slim]
    sum_rgb = rows_total[2 * slim : 5 * slim].reshape(3, slim)
    sum_upb = rows_total[5 * slim :]
    classes = class_table.shape[0]
    one_hot = (labels_all[:, None] == jnp.arange(classes)[None, :]).astype(f32)
    sum_table = contract(one_hot, context_grads, over_rows, HIGH)

    shifted = pooled_taps(grad_cols.reshape(held, sides, sides, slim)).reshape(9, held * lows, slim)
    grad_low = lax.dot_general(
        shifted, bank_cols[0], (((0, 2), (0, 2)), ((), ())), preferred_element_type=f32
    ).reshape(held, lows, channels)
    grad_low_other = lax.dot_general(
        shifted, bank_cols[1], (((0, 2), (0, 2)), ((), ())), preferred_element_type=f32
    ).reshape(held, lows, channels)
    mod_low = own_mod.reshape(held, lows, channels).astype(f32)
    select_taps = jnp.stack(
        [jnp.sum(mod_low * grad_low, axis=(1, 2)), jnp.sum(mod_low * grad_low_other, axis=(1, 2))], axis=1
    )
    low_partial = own_select[:, 0, None, None] * grad_low + own_select[:, 1, None, None] * grad_low_other
    low_parts = trade(low_partial.astype(bf16).reshape(8, lows // 2, channels))
    low_total = jnp.sum(low_parts.astype(f32), axis=0)

    bank_wide = bank_cols.astype(f32)
    coef_cols = lax.dynamic_slice_in_dim(coef_plane, device * slim, slim, 1)
    products = [
        jnp.sum(bank_wide[a] * bank_wide[b], axis=0) for a, b in ((0, 0), (0, 1), (1, 1))
    ]
    to_channel = [contract(coef_cols, x, ((1,), (1,)), HIGH) for x in products]
    first_share, other_share = own_select[:, :1], own_select[:, 1:]
    scale_term = -own_scales * (
        first_share * first_share * to_channel[0]
        + 2.0 * first_share * other_share * to_channel[1]
        + other_share * other_share * to_channel[2]
    )
    square_scales = jnp.square(own_scales)
    energy = [jnp.sum(square_scales * x, axis=1, keepdims=True) for x in to_channel]
    select_term = jnp.concatenate(
        [
            first_share * energy[0] + other_share * energy[1],
            first_share * energy[1] + other_share * energy[2],
        ],
        axis=1,
    )
    select_partial = select_taps - select_term

    member_scales = lax.dynamic_index_in_dim(own_scales, pair, 0, keepdims=False)
    feat_own = lax.dynamic_slice_in_dim(feat_all, first, held, 0).reshape(8, lows // 2, channels)
    feat_own = lax.dynamic_index_in_dim(feat_own, device, 0, keepdims=False).astype(f32)
    grad_input_rows = low_total * member_scales
    square_sum = jnp.sum(jnp.square(grad_input_rows))
    last_sent = jnp.concatenate(
        [
            jnp.sum(low_total * feat_own, axis=0),
            scale_term.reshape(-1),
            select_partial.reshape(-1),
            square_sum[None],
            jnp.zeros((127 - 2 * held,), f32),
        ]
    )
    last_all = gather(last_sent.reshape(1, -1, 128), "batch").reshape(8, -1)
    grad_scales = jnp.sum(last_all[:, :channels].reshape(held, 2, channels), axis=1)
    last_total = jnp.sum(last_all[:, channels:], axis=0)
    grad_scales = grad_scales + last_total[: held * channels].reshape(held, channels)
    last_rows = jnp.concatenate([grad_scales.reshape(-1), last_total[held * channels :]])
    last_rows = gather(last_rows.reshape(1, -1, 128), "rows").reshape(4, -1)
    grad_scales = last_rows[:, : held * channels].reshape(total, channels)
    grad_select = last_rows[:, held * channels : held * channels + 2 * held].reshape(total, 2)
    entries = float(total * 4 * in_rows * in_cols * channels)
    r1_value = jnp.sum(last_rows[:, held * channels + 2 * held]) / entries
    style_f32 = style_own.astype(f32)
    grad_logits = select * (grad_select - jnp.sum(grad_select * select, axis=-1, keepdims=True))
    sum_mod = contract(style_f32, grad_scales, over_rows, HIGH)
    sum_sel = contract(style_f32, grad_logits, over_rows, HIGH)

    conv_maps = jnp.transpose(conv_all.reshape(4, 2, 4, pixels, channels), (2, 0, 1, 3, 4))
    conv_maps = conv_maps.reshape(total, sides, sides, channels)
    shifted_all = pooled_taps(conv_maps).reshape(9, total * lows, channels)
    kernel_id = device // 4
    own_share = lax.dynamic_index_in_dim(select, kernel_id, 1)
    share_other = lax.dynamic_index_in_dim(select, 1 - kernel_id, 1)
    left = (own_share[:, :, None] * modulated.reshape(total, lows, channels).astype(f32)).astype(bf16)
    square_all = jnp.square(scales)
    blocks = (device % 4) * 9 + jnp.arange(9, dtype=jnp.int32)
    bank_total = bank_gradient(
        blocks // 4,
        blocks % 4,
        left.reshape(total * lows, channels),
        shifted_all,
        kernel_bank,
        bank_other,
        own_share * own_share * square_all,
        own_share * share_other * square_all,
        coef,
    )

    inputs = jnp.concatenate([cross_o, self_low, attended, hidden_low], axis=1)
    inputs = jnp.transpose(inputs.reshape(pixels, 4, 8, slim), (2, 0, 1, 3)).reshape(8, pixels, 4 * slim)
    inputs = trade(inputs).reshape(8 * pixels, 4 * slim)
    grads = [gather(x, "batch") for x in (cbranch, grad_cq, sbranch, grad_q, grad_v)]
    columns = (0, 1, 2, 3, 3)
    weight_grads = [
        contract(inputs[:, i * slim : (i + 1) * slim], g, over_rows).astype(bf16) for i, g in zip(columns, grads)
    ]

    def over_planes(x):
        return lax.psum(x, "rows").astype(f32)

    sum_down, sum_up = over_planes(grad_down), over_planes(grad_up)
    sum_co, sum_cq, sum_out, sum_qk, sum_val = [over_planes(x) for x in weight_grads]
    sum_ck, sum_cv = over_planes(grad_ck_w), over_planes(grad_cv_w)

    feat_out = from_pixels(result.reshape(2, piece, channels), odd_z, odd_pair)
    feat_out = feat_out.reshape(slots, 2 * in_rows, sides, channels)
    colour_sent = jnp.transpose(colour.reshape(3, 2, piece), (1, 0, 2))
    rgb_out = from_pixels(colour_sent, odd_z, odd_pair).reshape(slots, 3, 2 * in_rows, sides)
    grad_input = from_pixels(grad_input_rows.reshape(2, lows // 4, channels), odd_z, odd_pair)
    grad_input = grad_input.reshape(slots, in_rows, in_cols, channels)
    return (
        feat_out,
        rgb_out,
        grad_input,
        r1_value,
        sum_mod,
        sum_sel,
        bank_total,
        sum_bias,
        sum_gain,
        sum_qk,
        sum_val,
        sum_out,
        sum_cq,
        sum_ck,
        sum_cv,
        sum_co,
        sum_up,
        sum_upb,
        sum_down,
        sum_table,
        sum_rgb,
    )


def solution(mesh):
    split = mesh.shape["batch"] == 8 and mesh.shape["rows"] == 4
    return jax.shard_map(
        by_planes if split else per_device,
        mesh=mesh,
        in_specs=(
            P("batch", "rows", None, None),
            P("batch", None),
            P("batch"),
            P("batch", "rows", None),
            P("batch", "rows", None, None),
            P("batch", None, "rows", None),
            P("batch", None),
            P("batch", None),
            P("batch", None),
            P("batch"),
            P("batch"),
            P("batch", None),
            P("batch", None),
            P("batch", None),
            P("batch", None),
            P("batch", None),
            P("batch", None),
            P("batch", None),
            P("batch", None),
            P("batch"),
            P("batch", None),
            P(None, "batch"),
            P(None, "batch"),
        ),
        out_specs=(
            P("batch", "rows", None, None),
            P("batch", None, "rows", None),
            P("batch", "rows", None, None),
            P(),
            P("batch", None),
            P("batch", None),
            P("batch", None),
            P("batch"),
            P("batch"),
            P("batch", None),
            P("batch", None),
            P("batch", None),
            P("batch", None),
            P("batch", None),
            P("batch", None),
            P("batch", None),
            P("batch", None),
            P("batch"),
            P("batch", None),
            P(None, "batch"),
            P(None, "batch"),
        ),
        check_vma=False,
    )
```

```python
import jax
import jax.numpy as jnp
from jax import lax
from jax.experimental import pallas as pl
from jax.experimental.pallas import tpu as pltpu
from jax.sharding import PartitionSpec as P

HEAD_DIM = 64


HIGH = lax.Precision.HIGHEST
EPSILON = 1e-08
SLOPE = 0.2


def with_halo(cells, sides, width):
    for axis, dim in sides:
        count = lax.axis_size(axis)
        ends = count - 1
        head = lax.slice_in_dim(cells, 0, width, axis=dim)
        tail = lax.slice_in_dim(cells, cells.shape[dim] - width, cells.shape[dim], axis=dim)
        cells = jnp.concatenate(
            [
                lax.ppermute(tail, axis, [(i, (i + 1) % count) for i in range(ends)]),
                cells,
                lax.ppermute(head, axis, [((i + 1) % count, i) for i in range(ends)]),
            ],
            axis=dim,
        )
    return cells


def product(left, right):
    return jnp.dot(left, right, preferred_element_type=jnp.float32)


def kernel_mix(bank_split, select_row):
    mixed_kernel = select_row[0] * bank_split[0].astype(jnp.float32)
    mixed_kernel = mixed_kernel + select_row[1] * bank_split[1].astype(jnp.float32)
    return mixed_kernel


def gather_taps(padded, out_rows, out_cols, flipped):
    pieces = []
    for row_off in range(3):
        for col_off in range(3):
            if flipped:
                pieces.append(
                    padded[
                        :,
                        2 - row_off : 2 - row_off + out_rows,
                        2 - col_off : 2 - col_off + out_cols,
                    ]
                )
            else:
                pieces.append(padded[:, row_off : row_off + out_rows, col_off : col_off + out_cols])
    return jnp.concatenate(pieces, axis=-1)


def per_device(
    feat_in,
    style_vec,
    labels,
    noise_map,
    cot_feat,
    cot_rgb,
    mod_w,
    sel_w,
    kernel_bank,
    conv_bias,
    noise_gain,
    qk_w,
    val_w,
    out_w,
    cq_w,
    ck_w,
    cv_w,
    co_w,
    up_w,
    up_b,
    down_w,
    class_table,
    rgb_w,
):
    f32 = jnp.float32
    bf16 = jnp.bfloat16
    (
        mod_full,
        sel_full,
        bias_full,
        gain_full,
        qk_full,
        val_full,
        out_full,
        cq_full,
        ck_full,
        cv_full,
        co_full,
        up_full,
        upb_full,
        down_full,
        table_full,
        rgb_full,
    ) = (
        lax.all_gather(mod_w, "batch", axis=0, tiled=True),
        lax.all_gather(sel_w, "batch", axis=0, tiled=True),
        lax.all_gather(conv_bias, "batch", axis=0, tiled=True),
        lax.all_gather(noise_gain, "batch", axis=0, tiled=True),
        lax.all_gather(qk_w, "batch", axis=0, tiled=True),
        lax.all_gather(val_w, "batch", axis=0, tiled=True),
        lax.all_gather(out_w, "batch", axis=0, tiled=True),
        lax.all_gather(cq_w, "batch", axis=0, tiled=True),
        lax.all_gather(ck_w, "batch", axis=0, tiled=True),
        lax.all_gather(cv_w, "batch", axis=0, tiled=True),
        lax.all_gather(co_w, "batch", axis=0, tiled=True),
        lax.all_gather(up_w, "batch", axis=0, tiled=True),
        lax.all_gather(up_b, "batch", axis=0, tiled=True),
        lax.all_gather(down_w, "batch", axis=0, tiled=True),
        lax.all_gather(class_table, "batch", axis=1, tiled=True),
        lax.all_gather(rgb_w, "batch", axis=1, tiled=True),
    )
    bank_full = lax.all_gather(kernel_bank, "batch", axis=0, tiled=True)
    samples, in_rows, in_cols, channels = feat_in.shape
    out_rows = 2 * in_rows
    out_cols = 2 * in_cols
    pixels = out_rows * out_cols
    span = 9 * channels
    kernels = bank_full.shape[0] // span
    head_dim = HEAD_DIM
    head_count = channels // head_dim
    bank_split = bank_full.reshape(kernels, span, channels)
    scales = 1.0 + product(style_vec, mod_full)
    select = jax.nn.softmax(product(style_vec, sel_full), axis=-1)
    scale_tiled = jnp.tile(scales, (1, 9))
    upsampled = jnp.repeat(jnp.repeat(feat_in, 2, axis=1), 2, axis=2)
    modulated = (upsampled.astype(f32) * scales[:, None, None, :]).astype(bf16)
    with_rim = with_halo(modulated, (("rows", 1),), 1)
    padded = jnp.pad(with_rim, ((0, 0), (0, 0), (1, 1), (0, 0)))
    patches = gather_taps(padded, out_rows, out_cols, False).reshape(samples, pixels, span)

    def conv_forward(sample_item):
        patch_row, select_row, scale_row = sample_item
        mixed_kernel = kernel_mix(bank_split, select_row)
        demod_row = lax.rsqrt(
            jnp.sum(jnp.square(mixed_kernel * scale_row[:, None]), axis=0) + EPSILON
        )
        return (product(patch_row, mixed_kernel.astype(bf16)), demod_row, mixed_kernel)

    conv_out, demodulate, mixed_all = lax.map(conv_forward, (patches, select, scale_tiled))
    noise_flat = noise_map.reshape(samples, pixels, 1)
    pre_act = (
        conv_out * demodulate[:, None, :]
        + gain_full.astype(f32) * noise_flat
        + bias_full.astype(f32)
    )
    hidden = jnp.where(pre_act > 0, pre_act, SLOPE * pre_act)
    hidden_low = hidden.astype(bf16)
    queries = product(hidden_low, qk_full).astype(bf16)
    values = product(hidden_low, val_full).astype(bf16)
    all_queries, all_values = (
        lax.all_gather(queries, "rows", axis=1, tiled=True),
        lax.all_gather(values, "rows", axis=1, tiled=True),
    )
    query_h = queries.reshape(samples, pixels, head_count, head_dim)
    key_h = all_queries.reshape(samples, -1, head_count, head_dim)
    value_h = all_values.reshape(samples, -1, head_count, head_dim)
    key_f32 = key_h.astype(f32)
    key_norm = jnp.transpose(jnp.sum(jnp.square(key_f32), axis=-1), (0, 2, 1))[:, :, None, :]
    l2_scale = 0.5 * head_dim ** (-0.5)

    def self_scores():
        inner_dots = jnp.einsum("bqhd,bkhd->bhqk", query_h, key_h, preferred_element_type=f32)
        return l2_scale * (2.0 * inner_dots - key_norm)

    scores = self_scores()
    row_max = jnp.max(scores, axis=-1, keepdims=True)
    log_total = row_max + jnp.log(jnp.sum(jnp.exp(scores - row_max), axis=-1, keepdims=True))
    probs_low = jnp.exp(scores - log_total).astype(bf16)
    attended = (
        jnp.einsum("bhqk,bkhd->bqhd", probs_low, value_h, preferred_element_type=f32)
        .reshape(samples, pixels, channels)
        .astype(bf16)
    )
    after_self = hidden + product(attended, out_full)
    self_low = after_self.astype(bf16)
    cross_q = product(self_low, cq_full).astype(bf16).reshape(samples, pixels, head_count, head_dim)
    classes = table_full.shape[0]
    one_hot = (labels[:, None] == jnp.arange(classes)[None, :]).astype(bf16)
    contexts = table_full.shape[1] // channels
    context = product(one_hot, table_full).astype(bf16).reshape(samples, contexts, channels)
    cross_k = jnp.einsum("bjc,cd->bjd", context, ck_full, preferred_element_type=f32).astype(bf16)
    cross_v = jnp.einsum("bjc,cd->bjd", context, cv_full, preferred_element_type=f32).astype(bf16)
    key_cross = cross_k.reshape(samples, contexts, head_count, head_dim)
    value_cross = cross_v.reshape(samples, contexts, head_count, head_dim)
    cross_scale = head_dim ** (-0.5)
    cross_s = (
        jnp.einsum("bqhd,bjhd->bhqj", cross_q, key_cross, preferred_element_type=f32) * cross_scale
    )
    cross_p = jax.nn.softmax(cross_s, axis=-1)
    cross_plow = cross_p.astype(bf16)
    cross_o = (
        jnp.einsum("bhqj,bjhd->bqhd", cross_plow, value_cross, preferred_element_type=f32)
        .reshape(samples, pixels, channels)
        .astype(bf16)
    )
    after_cross = after_self + product(cross_o, co_full)
    cross_low = after_cross.astype(bf16)
    inner = product(cross_low, up_full) + upb_full.astype(f32)
    activated, gelu_pull = jax.vjp(jax.nn.gelu, inner)
    act_low = activated.astype(bf16)
    after_mlp = after_cross + product(act_low, down_full)
    result = after_mlp.astype(bf16)
    colour = product(result, rgb_full.T)
    rgb_out = jnp.transpose(colour, (0, 2, 1)).reshape(samples, 3, out_rows, out_cols)
    grad_rgb = jnp.transpose(cot_rgb.reshape(samples, 3, pixels), (0, 2, 1))
    grad_res = cot_feat.reshape(samples, pixels, channels).astype(f32) + jnp.dot(
        grad_rgb, rgb_full.astype(f32), precision=HIGH
    )
    grad_rgb_w = jnp.einsum("bpk,bpc->kc", grad_rgb, result.astype(f32), precision=HIGH)
    branch = grad_res.astype(bf16)
    grad_down_w = jnp.einsum("bpf,bpc->fc", act_low, branch, preferred_element_type=f32)
    (grad_inner,) = gelu_pull(product(branch, down_full.T))
    inner_low = grad_inner.astype(bf16)
    grad_up_b = jnp.sum(inner_low.astype(f32), axis=(0, 1))
    grad_up_w = jnp.einsum("bpc,bpf->cf", cross_low, inner_low, preferred_element_type=f32)
    grad_cross = grad_res + product(inner_low, up_full.T)
    cbranch = grad_cross.astype(bf16)
    grad_co_w = jnp.einsum("bpc,bpd->cd", cross_o, cbranch, preferred_element_type=f32)
    grad_co = (
        product(cbranch, co_full.T).astype(bf16).reshape(samples, pixels, head_count, head_dim)
    )
    grad_cp = jnp.einsum("bqhd,bjhd->bhqj", grad_co, value_cross, preferred_element_type=f32)
    grad_cv = (
        jnp.einsum("bhqj,bqhd->bjhd", cross_plow, grad_co, preferred_element_type=f32)
        .astype(bf16)
        .reshape(samples, contexts, channels)
    )
    grad_cs = (cross_p * (grad_cp - jnp.sum(grad_cp * cross_p, axis=-1, keepdims=True))).astype(
        bf16
    )
    grad_cq = (
        (
            jnp.einsum("bhqj,bjhd->bqhd", grad_cs, key_cross, preferred_element_type=f32)
            * cross_scale
        )
        .astype(bf16)
        .reshape(samples, pixels, channels)
    )
    grad_ck = (
        (jnp.einsum("bhqj,bqhd->bjhd", grad_cs, cross_q, preferred_element_type=f32) * cross_scale)
        .astype(bf16)
        .reshape(samples, contexts, channels)
    )
    grad_cq_w = jnp.einsum("bpc,bpd->cd", self_low, grad_cq, preferred_element_type=f32)
    grad_ck_w = jnp.einsum("bjc,bjd->cd", context, grad_ck, preferred_element_type=f32)
    grad_cv_w = jnp.einsum("bjc,bjd->cd", context, grad_cv, preferred_element_type=f32)
    grad_context = jnp.einsum(
        "bjd,cd->bjc", grad_ck, ck_full, preferred_element_type=f32
    ) + jnp.einsum("bjd,cd->bjc", grad_cv, cv_full, preferred_element_type=f32)
    grad_table = jnp.dot(
        one_hot.astype(f32).T, grad_context.reshape(samples, contexts * channels), precision=HIGH
    )
    grad_self = grad_cross + product(grad_cq, cq_full.T)
    sbranch = grad_self.astype(bf16)
    grad_out_w = jnp.einsum("bpc,bpd->cd", attended, sbranch, preferred_element_type=f32)
    grad_att = (
        product(sbranch, out_full.T).astype(bf16).reshape(samples, pixels, head_count, head_dim)
    )
    probs = jnp.exp(self_scores() - log_total)
    probs_again = probs.astype(bf16)
    grad_probs = jnp.einsum("bqhd,bkhd->bhqk", grad_att, value_h, preferred_element_type=f32)
    grad_vall = jnp.einsum("bhqk,bqhd->bkhd", probs_again, grad_att, preferred_element_type=f32)
    grad_s = (probs * (grad_probs - jnp.sum(grad_probs * probs, axis=-1, keepdims=True))).astype(
        bf16
    )
    grad_qloc = (
        2.0 * l2_scale * jnp.einsum("bhqk,bkhd->bqhd", grad_s, key_h, preferred_element_type=f32)
    )
    col_total = jnp.transpose(jnp.sum(grad_s.astype(f32), axis=2), (0, 2, 1))[:, :, :, None]
    grad_kall = (
        2.0
        * l2_scale
        * (
            jnp.einsum("bhqk,bqhd->bkhd", grad_s, query_h, preferred_element_type=f32)
            - key_f32 * col_total
        )
    )
    back_keys, back_values = (
        lax.psum_scatter(
            grad_kall.reshape(samples, -1, channels).astype(jnp.bfloat16),
            "rows",
            scatter_dimension=1,
            tiled=True,
        ).astype(jnp.float32),
        lax.psum_scatter(
            grad_vall.reshape(samples, -1, channels).astype(jnp.bfloat16),
            "rows",
            scatter_dimension=1,
            tiled=True,
        ).astype(jnp.float32),
    )
    grad_q = (grad_qloc.reshape(samples, pixels, channels) + back_keys).astype(bf16)
    grad_v = back_values.astype(bf16)
    grad_qk_w = jnp.einsum("bpc,bpd->cd", hidden_low, grad_q, preferred_element_type=f32)
    grad_val_w = jnp.einsum("bpc,bpd->cd", hidden_low, grad_v, preferred_element_type=f32)
    grad_hidden = grad_self + product(grad_q, qk_full.T) + product(grad_v, val_full.T)
    grad_pre = grad_hidden * jnp.where(pre_act > 0, 1.0, SLOPE)
    grad_gain = jnp.sum(grad_pre * noise_flat, axis=(0, 1))
    grad_bias = jnp.sum(grad_pre, axis=(0, 1))
    grad_demod = jnp.sum(grad_pre * conv_out, axis=1)
    demod_coef = demodulate**3 * grad_demod
    grad_conv = (grad_pre * demodulate[:, None, :]).astype(bf16)
    grad_rim = with_halo(
        grad_conv.reshape(samples, out_rows, out_cols, channels), (("rows", 1),), 1
    )
    grad_pad = jnp.pad(grad_rim, ((0, 0), (0, 0), (1, 1), (0, 0)))
    grad_patches = gather_taps(grad_pad, out_rows, out_cols, True).reshape(samples, pixels, span)

    def conv_backward(sample_item):
        gpatch_row, mixed_kernel, scale_row, coef_row = sample_item
        taps_low = mixed_kernel.astype(bf16).reshape(9, channels, channels)
        grad_mod = jnp.einsum(
            "pto,tio->pi",
            gpatch_row.reshape(pixels, 9, channels),
            taps_low,
            preferred_element_type=f32,
        )
        scale_term = -scale_row[:channels] * jnp.sum(
            (jnp.square(mixed_kernel) * coef_row[None, :]).reshape(9, channels, channels),
            axis=(0, 2),
        )
        return (grad_mod, scale_term)

    grad_mod, scale_term = lax.map(
        conv_backward, (grad_patches, mixed_all, scale_tiled, demod_coef)
    )
    block_rows = span // 8

    def tap_block(index, carry):
        bank_acc, select_acc = carry
        tap_row = index * block_rows
        patch_cols = lax.dynamic_slice_in_dim(patches, tap_row, block_rows, 2)
        grad_taps = jnp.einsum("bpt,bpo->bto", patch_cols, grad_conv, preferred_element_type=f32)
        bank_rows = lax.dynamic_slice_in_dim(bank_split, tap_row, block_rows, 1).astype(f32)
        mixed_rows = lax.dynamic_slice_in_dim(mixed_all, tap_row, block_rows, 1)
        scale_rows = lax.dynamic_slice_in_dim(scale_tiled, tap_row, block_rows, 1)
        grad_mixed = (
            grad_taps - mixed_rows * jnp.square(scale_rows)[:, :, None] * demod_coef[:, None, :]
        )
        select_acc = select_acc + jnp.einsum("kto,bto->bk", bank_rows, grad_mixed, precision=HIGH)
        bank_piece = jnp.einsum("bk,bto->kto", select, grad_mixed, precision=HIGH)
        bank_acc = lax.dynamic_update_slice_in_dim(bank_acc, bank_piece, tap_row, 1)
        return (bank_acc, select_acc)

    bank_acc, grad_select = lax.fori_loop(
        0,
        8,
        tap_block,
        (jnp.zeros((kernels, span, channels), f32), jnp.zeros((samples, kernels), f32)),
    )
    bank_flat = bank_acc.reshape(kernels * span, channels)
    grad_mod = grad_mod.reshape(samples, out_rows, out_cols, channels)
    grad_scales = jnp.sum(grad_mod * upsampled.astype(f32), axis=(1, 2)) + scale_term
    grad_up = grad_mod * scales[:, None, None, :]
    grad_input = grad_up.reshape(samples, in_rows, 2, in_cols, 2, channels).sum(axis=(2, 4))
    grad_logits = select * (grad_select - jnp.sum(grad_select * select, axis=-1, keepdims=True))
    style_f32 = style_vec.astype(f32)
    grad_mod_w = jnp.dot(style_f32.T, grad_scales, precision=HIGH)
    grad_sel_w = jnp.dot(style_f32.T, grad_logits, precision=HIGH)
    (
        sum_mod,
        sum_sel,
        sum_bias,
        sum_gain,
        sum_qk,
        sum_val,
        sum_out,
        sum_cq,
        sum_ck,
        sum_cv,
        sum_co,
        sum_up,
        sum_upb,
        sum_down,
        sum_table,
        sum_rgb,
    ) = (
        lax.psum_scatter(grad_mod_w, "batch", scatter_dimension=0, tiled=True),
        lax.psum_scatter(grad_sel_w, "batch", scatter_dimension=0, tiled=True),
        lax.psum_scatter(grad_bias, "batch", scatter_dimension=0, tiled=True),
        lax.psum_scatter(grad_gain, "batch", scatter_dimension=0, tiled=True),
        lax.psum_scatter(grad_qk_w, "batch", scatter_dimension=0, tiled=True),
        lax.psum_scatter(grad_val_w, "batch", scatter_dimension=0, tiled=True),
        lax.psum_scatter(grad_out_w, "batch", scatter_dimension=0, tiled=True),
        lax.psum_scatter(grad_cq_w, "batch", scatter_dimension=0, tiled=True),
        lax.psum_scatter(grad_ck_w, "batch", scatter_dimension=0, tiled=True),
        lax.psum_scatter(grad_cv_w, "batch", scatter_dimension=0, tiled=True),
        lax.psum_scatter(grad_co_w, "batch", scatter_dimension=0, tiled=True),
        lax.psum_scatter(grad_up_w, "batch", scatter_dimension=0, tiled=True),
        lax.psum_scatter(grad_up_b, "batch", scatter_dimension=0, tiled=True),
        lax.psum_scatter(grad_down_w, "batch", scatter_dimension=0, tiled=True),
        lax.psum_scatter(grad_table, "batch", scatter_dimension=1, tiled=True),
        lax.psum_scatter(grad_rgb_w, "batch", scatter_dimension=1, tiled=True),
    )
    bank_part = lax.psum_scatter(bank_flat, "batch", scatter_dimension=0, tiled=True)
    (
        sum_mod,
        sum_sel,
        sum_bias,
        sum_gain,
        sum_qk,
        sum_val,
        sum_out,
        sum_cq,
        sum_ck,
        sum_cv,
        sum_co,
        sum_up,
        sum_upb,
        sum_down,
        sum_table,
        sum_rgb,
        bank_total,
    ) = (
        lax.psum(sum_mod.astype(jnp.bfloat16), "rows").astype(jnp.float32),
        lax.psum(sum_sel.astype(jnp.bfloat16), "rows").astype(jnp.float32),
        lax.psum(sum_bias.astype(jnp.bfloat16), "rows").astype(jnp.float32),
        lax.psum(sum_gain.astype(jnp.bfloat16), "rows").astype(jnp.float32),
        lax.psum(sum_qk.astype(jnp.bfloat16), "rows").astype(jnp.float32),
        lax.psum(sum_val.astype(jnp.bfloat16), "rows").astype(jnp.float32),
        lax.psum(sum_out.astype(jnp.bfloat16), "rows").astype(jnp.float32),
        lax.psum(sum_cq.astype(jnp.bfloat16), "rows").astype(jnp.float32),
        lax.psum(sum_ck.astype(jnp.bfloat16), "rows").astype(jnp.float32),
        lax.psum(sum_cv.astype(jnp.bfloat16), "rows").astype(jnp.float32),
        lax.psum(sum_co.astype(jnp.bfloat16), "rows").astype(jnp.float32),
        lax.psum(sum_up.astype(jnp.bfloat16), "rows").astype(jnp.float32),
        lax.psum(sum_upb.astype(jnp.bfloat16), "rows").astype(jnp.float32),
        lax.psum(sum_down.astype(jnp.bfloat16), "rows").astype(jnp.float32),
        lax.psum(sum_table.astype(jnp.bfloat16), "rows").astype(jnp.float32),
        lax.psum(sum_rgb.astype(jnp.bfloat16), "rows").astype(jnp.float32),
        lax.psum(bank_part.astype(jnp.bfloat16), "rows").astype(jnp.float32),
    )
    entry_count = float(
        samples * lax.axis_size("batch") * in_rows * lax.axis_size("rows") * in_cols * channels
    )
    r1_value = lax.psum(jnp.sum(jnp.square(grad_input)), ("batch", "rows")) / entry_count
    feat_out = result.reshape(samples, out_rows, out_cols, channels)
    return (
        feat_out,
        rgb_out,
        grad_input,
        r1_value,
        sum_mod,
        sum_sel,
        bank_total,
        sum_bias,
        sum_gain,
        sum_qk,
        sum_val,
        sum_out,
        sum_cq,
        sum_ck,
        sum_cv,
        sum_co,
        sum_up,
        sum_upb,
        sum_down,
        sum_table,
        sum_rgb,
    )


def gather(x, axis_name, axis=0):
    return lax.all_gather(x, axis_name, axis=axis, tiled=True)


def trade(x):
    return lax.all_to_all(x, "batch", 0, 0, tiled=True)


def to_pair(x, step):
    return lax.ppermute(x, "batch", [(i, i ^ (2 * step)) for i in range(8)])


def spread(x):
    return jnp.concatenate([x] + [to_pair(x, step) for step in range(1, 4)])


def exchange(x):
    return [x] + [to_pair(x, step) for step in range(1, 4)]


def member_sum(parts):
    total = parts[0].astype(jnp.float32)
    for step in range(1, 4):
        total = total + to_pair(parts[step].astype(jnp.bfloat16), step).astype(jnp.float32)
    return total


def after(x, *earlier):
    return lax.optimization_barrier((x,) + earlier)[0]


def behind(x, earlier):
    nothing = jnp.minimum(jnp.abs(earlier[(0,) * earlier.ndim].astype(jnp.float32)), 0.0)
    return x + nothing.astype(x.dtype)


def swap_pair(x):
    return lax.ppermute(x, "batch", [(i, i ^ 1) for i in range(8)])


def move_table(turn):
    table = []
    for d in range(8):
        for z in range(4):
            slot = (z % 2) ^ turn
            pair = 2 * (d % 2) + slot
            table.append((4 * d + z, 4 * (2 * pair + z // 2) + d // 2))
    return table


def to_pixels(x, odd_z, odd_pair):
    sent = jnp.where(odd_z, x[::-1], x)
    first = lax.ppermute(sent[0], ("batch", "rows"), move_table(0))
    second = lax.ppermute(sent[1], ("batch", "rows"), move_table(1))
    return jnp.where(odd_pair, jnp.stack([second, first]), jnp.stack([first, second]))


def from_pixels(x, odd_z, odd_pair):
    sent = jnp.where(odd_pair, x[::-1], x)
    back = [[(b, a) for a, b in move_table(turn)] for turn in range(2)]
    first = lax.ppermute(sent[0], ("batch", "rows"), back[0])
    second = lax.ppermute(sent[1], ("batch", "rows"), back[1])
    return jnp.where(odd_z, jnp.stack([second, first]), jnp.stack([first, second]))


def contract(left, right, dims, precision=None):
    return lax.dot_general(
        left, right, (dims, ((), ())), precision=precision, preferred_element_type=jnp.float32
    )


def conv_kernel(
    select_ref, patch_ref, bank_ref, scale_ref, out_ref, square_ref, product_ref, acc_ref, sum_ref
):
    col, row = pl.program_id(0), pl.program_id(1)
    start = jnp.logical_and(col == 0, row == 0)
    last = jnp.logical_and(col == 2, row == 2)

    @pl.when(start)
    def _():
        acc_ref[...] = jnp.zeros_like(acc_ref)
        sum_ref[...] = jnp.zeros_like(sum_ref)
        product_ref[...] = jnp.zeros_like(product_ref)

    first = bank_ref[0, 0].astype(jnp.float32)
    second = bank_ref[1, 0].astype(jnp.float32)
    product_ref[0] += first * first
    product_ref[1] += first * second
    product_ref[2] += second * second
    for b in range(4):
        mixed = select_ref[b, 0] * first + select_ref[b, 1] * second
        scaled = mixed * scale_ref[b]
        sum_ref[b] += jnp.sum(jnp.square(scaled).reshape(-1, 8, 128), axis=0)
        begin = pl.multiple_of(row * 16, 16)
        left = patch_ref[b, 0, pl.ds(begin, 256), :]
        acc_ref[b] += jnp.dot(left, mixed.astype(jnp.bfloat16), preferred_element_type=jnp.float32)

    @pl.when(last)
    def _():
        out_ref[...] = acc_ref[...]
        square_ref[...] = sum_ref[...]


def conv_forward_plane(select, patch_cols, bank_cols, scale_cols):
    samples, _, _, width = patch_cols.shape
    cols = bank_cols.shape[-1]
    f32 = jnp.float32
    return pl.pallas_call(
        conv_kernel,
        grid=(3, 3),
        in_specs=[
            pl.BlockSpec(memory_space=pltpu.SMEM),
            pl.BlockSpec((samples, 1, 288, width), lambda c, a: (0, c, 0, 0)),
            pl.BlockSpec((2, 1, width, cols), lambda c, a: (0, 3 * a + c, 0, 0)),
            pl.BlockSpec((samples, width, cols), lambda c, a: (0, 0, 0)),
        ],
        out_specs=[
            pl.BlockSpec((samples, 256, cols), lambda c, a: (0, 0, 0)),
            pl.BlockSpec((samples, 8, cols), lambda c, a: (0, 0, 0)),
            pl.BlockSpec((3, width, cols), lambda c, a: (0, 0, 0)),
        ],
        out_shape=[
            jax.ShapeDtypeStruct((samples, 256, cols), f32),
            jax.ShapeDtypeStruct((samples, 8, cols), f32),
            jax.ShapeDtypeStruct((3, width, cols), f32),
        ],
        scratch_shapes=[
            pltpu.VMEM((samples, 256, cols), f32),
            pltpu.VMEM((samples, 8, cols), f32),
        ],
        compiler_params=pltpu.CompilerParams(vmem_limit_bytes=40 << 20),
        cost_estimate=pl.CostEstimate(
            flops=2 * samples * 256 * 9 * width * cols, bytes_accessed=20 << 20, transcendentals=0
        ),
        name="conv_plane",
    )(select, patch_cols, bank_cols, scale_cols)


def head_scores(query, key):
    squares = jnp.square(key.astype(jnp.float32))
    upper = squares.astype(jnp.bfloat16)
    lower = (squares - upper.astype(jnp.float32)).astype(jnp.bfloat16)
    ones = jnp.ones((8, HEAD_DIM), jnp.bfloat16)
    over_last = ((1,), (1,))
    norms = contract(ones, upper, over_last) + contract(ones, lower, over_last)
    scale = 0.5 * HEAD_DIM ** (-0.5)
    return scale * (2.0 * contract(query, key, over_last) - norms[0:1])


def head_softmax(scores):
    raised = jnp.exp(scores - jnp.max(scores, axis=-1, keepdims=True))
    return raised * (1.0 / jnp.sum(raised, axis=-1, keepdims=True))


def attend_kernel(query_ref, key_ref, value_ref, out_ref):
    for h in range(query_ref.shape[1] // HEAD_DIM):
        part = slice(h * HEAD_DIM, (h + 1) * HEAD_DIM)
        probs = head_softmax(head_scores(query_ref[:, part], key_ref[:, part]))
        out_ref[:, part] = jnp.dot(
            probs.astype(jnp.bfloat16), value_ref[:, part], preferred_element_type=jnp.float32
        ).astype(jnp.bfloat16)


def attend(query, key, value):
    pixels, width = query.shape
    everything = key.shape[0]
    pair = 4 * HEAD_DIM
    return pl.pallas_call(
        attend_kernel,
        grid=(width // pair,),
        in_specs=[
            pl.BlockSpec((pixels, pair), lambda i: (0, i)),
            pl.BlockSpec((everything, pair), lambda i: (0, i)),
            pl.BlockSpec((everything, pair), lambda i: (0, i)),
        ],
        out_specs=pl.BlockSpec((pixels, pair), lambda i: (0, i)),
        out_shape=jax.ShapeDtypeStruct((pixels, width), jnp.bfloat16),
        cost_estimate=pl.CostEstimate(
            flops=4 * pixels * everything * width, bytes_accessed=3 << 20, transcendentals=1 << 19
        ),
        name="attend",
    )(query, key, value)


def attend_back_kernel(query_ref, key_ref, value_ref, grad_ref, gq_ref, gk_ref, gv_ref):
    bf16 = jnp.bfloat16
    twice = 2.0 * (0.5 * HEAD_DIM ** (-0.5))
    for h in range(query_ref.shape[1] // HEAD_DIM):
        part = slice(h * HEAD_DIM, (h + 1) * HEAD_DIM)
        query, key, value, grad = query_ref[:, part], key_ref[:, part], value_ref[:, part], grad_ref[:, part]
        probs = head_softmax(head_scores(query, key))
        grad_probs = contract(grad, value, ((1,), (1,)))
        mean = jnp.sum(grad_probs * probs, axis=-1, keepdims=True)
        grad_s = (probs * (grad_probs - mean)).astype(bf16)
        gv_ref[:, part] = contract(probs.astype(bf16), grad, ((0,), (0,)))
        gq_ref[:, part] = twice * jnp.dot(grad_s, key, preferred_element_type=jnp.float32)
        both = jnp.concatenate([query, jnp.ones_like(query)], axis=1)
        sums = contract(grad_s, both, ((0,), (0,)))
        gk_ref[:, part] = twice * (
            sums[:, :HEAD_DIM] - key.astype(jnp.float32) * sums[:, HEAD_DIM:]
        )


def attend_back(query, key, value, grad):
    pixels, width = query.shape
    everything = key.shape[0]
    pair = 4 * HEAD_DIM
    few = pl.BlockSpec((pixels, pair), lambda i: (0, i))
    many = pl.BlockSpec((everything, pair), lambda i: (0, i))
    f32 = jnp.float32
    return pl.pallas_call(
        attend_back_kernel,
        grid=(width // pair,),
        in_specs=[few, many, many, few],
        out_specs=[few, many, many],
        out_shape=[
            jax.ShapeDtypeStruct((pixels, width), f32),
            jax.ShapeDtypeStruct((everything, width), f32),
            jax.ShapeDtypeStruct((everything, width), f32),
        ],
        cost_estimate=pl.CostEstimate(
            flops=14 * pixels * everything * width, bytes_accessed=5 << 20, transcendentals=1 << 19
        ),
        name="attend_back",
    )(query, key, value, grad)


def split_terms(x, left):
    upper = x.astype(jnp.bfloat16)
    lower = (x - upper.astype(jnp.float32)).astype(jnp.bfloat16)
    return jnp.concatenate([upper, upper, lower] if left else [upper, lower, upper])


def bank_kernel(tap_ref, part_ref, left_ref, right_ref, own_ref, other_ref, same_ref, cross_ref, coef_ref, out_ref):
    del tap_ref, part_ref
    first = ((0,), (0,))
    out_ref[...] = (
        jnp.dot(left_ref[...], right_ref[0], preferred_element_type=jnp.float32)
        - own_ref[...].astype(jnp.float32) * contract(same_ref[...], coef_ref[...], first)
        - other_ref[...].astype(jnp.float32) * contract(cross_ref[...], coef_ref[...], first)
    )


def bank_gradient(taps, parts, left, right, own, other, same, cross, coef):
    lows = left.shape[1]
    count = taps.shape[0]
    rows = own.shape[0] // count
    out_cols = own.shape[1]
    terms = coef.shape[0]
    return pl.pallas_call(
        bank_kernel,
        grid_spec=pltpu.PrefetchScalarGridSpec(
            num_scalar_prefetch=2,
            grid=(count,),
            in_specs=[
                pl.BlockSpec((rows, lows), lambda m, t, q: (q[m], 0)),
                pl.BlockSpec((1, lows, out_cols), lambda m, t, q: (t[m], 0, 0)),
                pl.BlockSpec((rows, out_cols), lambda m, t, q: (m, 0)),
                pl.BlockSpec((rows, out_cols), lambda m, t, q: (m, 0)),
                pl.BlockSpec((terms, rows), lambda m, t, q: (0, q[m])),
                pl.BlockSpec((terms, rows), lambda m, t, q: (0, q[m])),
                pl.BlockSpec((terms, out_cols), lambda m, t, q: (0, 0)),
            ],
            out_specs=pl.BlockSpec((rows, out_cols), lambda m, t, q: (m, 0)),
        ),
        out_shape=jax.ShapeDtypeStruct((own.shape[0], out_cols), jnp.float32),
        compiler_params=pltpu.CompilerParams(vmem_limit_bytes=40 << 20),
        cost_estimate=pl.CostEstimate(
            flops=2 * lows * own.shape[0] * out_cols, bytes_accessed=32 << 20, transcendentals=0
        ),
        name="bank_gradient",
    )(taps, parts, left, right, own, other, same, cross, coef)


def pool_matrix(taps, side):
    half = side // 2
    shape = (taps.shape[0], half * half, side * side)
    block = lax.broadcasted_iota(jnp.int32, shape, 1)
    pixel = lax.broadcasted_iota(jnp.int32, shape, 2)
    tap = taps[:, None, None]
    row = pixel // side + tap // 3 - 1 - 2 * (block // half)
    col = pixel % side + tap % 3 - 1 - 2 * (block % half)
    inside = (row >= 0) & (row < 2) & (col >= 0) & (col < 2)
    return inside.astype(jnp.bfloat16)


def patch_matrix(low):
    side = 2 * low
    shape = (3 * (side + 2) * side, low * low)
    place = lax.broadcasted_iota(jnp.int32, shape, 0)
    source = lax.broadcasted_iota(jnp.int32, shape, 1)
    offset, place = place // ((side + 2) * side), place % ((side + 2) * side)
    row, col = place // side - 1, place % side + offset - 1
    inside = (row >= 0) & (row < side) & (col >= 0) & (col < side)
    return (inside & (source == (row // 2) * low + col // 2)).astype(jnp.bfloat16)


def pool_kernel(order_ref, matrix_ref, map_ref, out_ref):
    del order_ref
    pixels = matrix_ref.shape[1]
    taps, _, lows, width = out_ref.shape
    grid = map_ref[...].reshape(pixels, width)
    pooled = jnp.dot(matrix_ref[...], grid, preferred_element_type=jnp.float32)
    out_ref[...] = pooled.astype(jnp.bfloat16).reshape(taps, 1, lows, width)


def pool_samples(order, matrix, maps):
    taps, lows, pixels = matrix.shape
    pairs, members, steps, piece, width = maps.shape
    return pl.pallas_call(
        pool_kernel,
        grid_spec=pltpu.PrefetchScalarGridSpec(
            num_scalar_prefetch=1,
            grid=(steps, pairs),
            in_specs=[
                pl.BlockSpec((taps * lows, pixels), lambda k, c, o: (0, 0)),
                pl.BlockSpec((1, members, 1, piece, width), lambda k, c, o: (c, 0, k, 0, 0)),
            ],
            out_specs=pl.BlockSpec((taps, 1, lows, width), lambda k, c, o: (0, o[k] * pairs + c, 0, 0)),
        ),
        out_shape=jax.ShapeDtypeStruct((taps, steps * pairs, lows, width), jnp.bfloat16),
        compiler_params=pltpu.CompilerParams(vmem_limit_bytes=24 << 20),
        cost_estimate=pl.CostEstimate(
            flops=2 * taps * lows * pixels * width * steps * pairs, bytes_accessed=14 << 20, transcendentals=0
        ),
        name="pool_samples",
    )(order, matrix.reshape(taps * lows, pixels), maps)


def by_planes(
    feat_in,
    style_vec,
    labels,
    noise_map,
    cot_feat,
    cot_rgb,
    mod_w,
    sel_w,
    kernel_bank,
    conv_bias,
    noise_gain,
    qk_w,
    val_w,
    out_w,
    cq_w,
    ck_w,
    cv_w,
    co_w,
    up_w,
    up_b,
    down_w,
    class_table,
    rgb_w,
):
    f32, bf16 = jnp.float32, jnp.bfloat16
    device, plane = lax.axis_index("batch"), lax.axis_index("rows")
    pair, member = device // 2, device % 2
    odd_z, odd_pair = plane % 2 == 1, pair % 2 == 1
    slots, in_rows, in_cols, channels = feat_in.shape
    total = 8 * slots
    held = total // 4
    piece = 2 * in_rows * 2 * in_cols
    pixels = 2 * piece
    lows = 4 * in_rows * in_cols
    style_width = style_vec.shape[1]
    own_style = style_width // 8
    slim = channels // 8
    head_count = channels // HEAD_DIM

    point_maps = jnp.concatenate(
        [noise_map.reshape(slots, 1, piece), cot_rgb.reshape(slots, 3, piece)], axis=1
    )
    point_maps = to_pixels(point_maps, odd_z, odd_pair)
    point_cols = jnp.transpose(point_maps, (0, 2, 1)).reshape(pixels, 4)
    noise_col, grad_rgb = point_cols[:, :1], point_cols[:, 1:]

    packed = jnp.concatenate(
        [
            feat_in.reshape(-1, 128),
            style_vec.reshape(-1, 128),
            conv_bias.reshape(-1, 128),
            noise_gain.reshape(-1, 128),
            rgb_w.reshape(-1, 128),
            jnp.pad(jnp.stack([labels // 32, labels % 32]).astype(bf16), ((0, 0), (0, 128 - slots))),
        ]
    )
    bank_sent = jnp.transpose(kernel_bank.reshape(-1, 8, slim), (1, 0, 2))
    smalls = gather(after(packed, bank_sent, point_cols)[None], "batch")
    feat_rows = feat_in.size // 128
    style_rows = style_vec.size // 128
    at = feat_rows + style_rows
    feat_part = smalls[:, :feat_rows].reshape(total, in_rows * in_cols, channels)
    style_all = smalls[:, feat_rows:at].reshape(total, style_width)
    bias_full = smalls[:, at].astype(f32).reshape(channels)
    gain_full = smalls[:, at + 1].astype(f32).reshape(channels)
    rgb_full = jnp.transpose(smalls[:, at + 2 : at + 5], (1, 0, 2)).astype(f32).reshape(3, channels)
    label_parts = smalls[:, at + 5 : at + 7, :slots].astype(jnp.int32)
    labels_all = (32 * label_parts[:, 0] + label_parts[:, 1]).reshape(total)

    style_own = lax.dynamic_slice_in_dim(style_all, device * own_style, own_style, 1)
    context_own = jnp.take(class_table, labels_all, axis=0)
    partial_styles = jnp.concatenate(
        [
            product(style_own, mod_w),
            jnp.pad(product(style_own, sel_w), ((0, 0), (0, 126))),
            context_own.astype(f32),
        ],
        axis=1,
    )
    styles = gather(partial_styles[None], "batch")
    sums = jnp.sum(styles[:, :, : channels + 128], axis=0)
    scales = 1.0 + sums[:, :channels]
    select = jax.nn.softmax(sums[:, channels : channels + 2], axis=-1)
    context_all = jnp.transpose(styles[:, :, channels + 128 :], (1, 0, 2)).reshape(total, -1).astype(bf16)
    feat_all = gather(feat_part[None], "rows")
    feat_all = jnp.transpose(feat_all, (1, 0, 2, 3)).reshape(total, lows, channels)

    kernels = 2
    bank_cols = trade(after(bank_sent, styles)).reshape(kernels, 9, channels, slim)

    first_weights = gather(after(jnp.stack([qk_w, val_w]), styles), "batch", 1)
    qk_full, val_full = first_weights[0], first_weights[1]

    weights = gather(after(jnp.stack([out_w, cq_w, co_w]), styles), "batch", 1)
    out_full, cq_full, co_full = weights[0], weights[1], weights[2]


    first = held * plane
    tokens = context_all.shape[1] // channels
    modulated = (feat_all.astype(f32) * scales[:, None, :]).astype(bf16)
    own_mod = lax.dynamic_slice_in_dim(modulated, first, held, 0)
    own_scales = lax.dynamic_slice_in_dim(scales, first, held, 0)
    own_select = lax.dynamic_slice_in_dim(select, first, held, 0)
    sides = 2 * in_cols
    patch_cols = jnp.einsum(
        "srl,slc->src",
        jnp.broadcast_to(patch_matrix(in_cols)[None], (held, 3 * (sides + 2) * sides, lows)),
        own_mod,
        preferred_element_type=f32,
    )
    patch_cols = patch_cols.astype(bf16).reshape(held, 3, (sides + 2) * sides, channels)
    kernel_id = device // 4
    own_share = lax.dynamic_index_in_dim(select, kernel_id, 1)
    share_other = lax.dynamic_index_in_dim(select, 1 - kernel_id, 1)
    left = (own_share[:, :, None] * modulated.astype(f32)).astype(bf16)
    left = jnp.transpose(left.reshape(total * lows, channels))
    patch_cols = after(patch_cols, left, point_cols)
    scale_cols = jnp.broadcast_to(own_scales[:, :, None], (held, channels, slim))
    conv_cols, square_cols, products = conv_forward_plane(own_select, patch_cols, bank_cols, scale_cols)

    demod_cols = lax.rsqrt(jnp.sum(square_cols, axis=1) + EPSILON)
    extra = jnp.broadcast_to(jnp.repeat(demod_cols, 2, axis=0)[:, None, :], (8, 8, slim))
    own_context = lax.dynamic_slice_in_dim(context_all, first, held, 0).reshape(held * tokens, channels)
    context_cols = lax.dynamic_slice_in_dim(own_context, device * slim, slim, 1)
    cross_partial = product(context_cols, jnp.concatenate([ck_w, cv_w], axis=1)).reshape(held, -1, slim)
    cross_partial = jnp.repeat(cross_partial, 2, axis=0)
    sent = jnp.concatenate([conv_cols.reshape(8, pixels, slim), extra, cross_partial], axis=1)
    back = trade(sent)
    cross_kv = jnp.sum(back[:, pixels + 8 :], axis=0).reshape(tokens, 2 * channels).astype(bf16)
    back = jnp.transpose(back[:, : pixels + 8], (1, 0, 2)).reshape(pixels + 8, channels)
    conv_out, demodulate = back[:pixels], back[pixels]

    pre_act = conv_out * demodulate + gain_full * noise_col + bias_full
    hidden = jnp.where(pre_act > 0, pre_act, SLOPE * pre_act)
    hidden_low = hidden.astype(bf16)

    queries = product(hidden_low, qk_full).astype(bf16)
    values = product(hidden_low, val_full).astype(bf16)
    up_sent = jnp.transpose(up_w.reshape(slim, 8, -1), (1, 0, 2))
    up_cols = trade(after(up_sent, queries)).reshape(channels, -1)
    units = up_cols.shape[1]
    up_two = jnp.concatenate([up_cols, swap_pair(up_cols)], axis=1)
    down_two = jnp.concatenate([down_w, swap_pair(after(down_w, queries))])
    bias_two = jnp.concatenate([up_b, swap_pair(after(up_b, queries))]).astype(f32)
    theirs = swap_pair(jnp.concatenate([queries, values], axis=1))
    keys_all = jnp.concatenate([queries, theirs[:, :channels]])
    values_all = jnp.concatenate([values, theirs[:, channels:]])
    cot_sent = after(cot_feat, conv_out).reshape(slots, piece, channels)
    cot_pixels = to_pixels(cot_sent, odd_z, odd_pair).reshape(pixels, channels)
    grad_res = cot_pixels.astype(f32) + jnp.dot(grad_rgb, rgb_full, precision=HIGH)
    branch = grad_res.astype(bf16)
    branch_rows = spread(branch)
    quarter = kernel_bank.shape[0] // 4
    bank_quarter = lax.dynamic_slice_in_dim(kernel_bank, plane * quarter, quarter, 0)
    bank_quarter = after(bank_quarter, up_cols)
    bank_quarter = lax.ppermute(bank_quarter, "batch", [(i, i ^ 4) for i in range(8)])
    attended = attend(queries, keys_all, values_all)
    after_self = hidden + product(attended, out_full)
    self_low = after_self.astype(bf16)

    in_head = (jnp.arange(channels)[None, :] // HEAD_DIM == jnp.arange(head_count)[:, None])[None]

    def by_head(rows):
        return jnp.where(in_head, rows[:, None, :], 0).astype(bf16).reshape(tokens * head_count, channels)

    key_blocks, value_blocks = by_head(cross_kv[:, :channels]), by_head(cross_kv[:, channels:])
    cross_scale = HEAD_DIM ** (-0.5)
    cross_q = product(self_low, cq_full).astype(bf16)

    def per_token(x):
        return [x[:, i * head_count : (i + 1) * head_count] for i in range(tokens)]

    cross_s = per_token(contract(cross_q, key_blocks, ((1,), (1,))) * cross_scale)
    top = jnp.maximum(jnp.maximum(cross_s[0], cross_s[1]), jnp.maximum(cross_s[2], cross_s[3]))
    raised = [jnp.exp(x - top) for x in cross_s]
    whole = raised[0] + raised[1] + raised[2] + raised[3]
    cross_p = [x / whole for x in raised]
    cross_plow = jnp.concatenate(cross_p, axis=1).astype(bf16)
    cross_o = product(cross_plow, value_blocks).astype(bf16)
    cross_o = after(cross_o, up_two, down_two, branch_rows)
    after_cross = after_self + product(cross_o, co_full)
    cross_low = after_cross.astype(bf16)

    cross_rows = after(spread(cross_low), bank_quarter)
    bank_other = gather(after(bank_quarter, cross_rows), "rows")

    def of_pair(x, step, width, axis):
        return lax.dynamic_slice_in_dim(x, (pair ^ step) * width, width, axis)

    inward = after(jnp.stack([cross_o, self_low, attended, hidden_low]), cross_rows)
    inward = [of_pair(inward, 0, 2 * slim, 2)] + [
        to_pair(of_pair(inward, step, 2 * slim, 2), step) for step in range(1, 4)
    ]
    inner = product(cross_rows, up_two) + bias_two
    activated, gelu_pull = jax.vjp(jax.nn.gelu, inner)
    act_low = activated.astype(bf16)
    (grad_inner,) = gelu_pull(contract(branch_rows, down_two, ((1,), (1,))))
    inner_low = grad_inner.astype(bf16)
    over_rows = ((0,), (0,))

    def pair_sum(x, axis):
        half = x.shape[axis] // 2
        kept = lax.dynamic_slice_in_dim(x, member * half, half, axis)
        sent = lax.dynamic_slice_in_dim(x, (1 - member) * half, half, axis)
        return kept + swap_pair(sent.astype(bf16)).astype(f32)

    def own_sum(x):
        half = x.shape[0] // 2
        return x[:half] + swap_pair(x[half:].astype(bf16)).astype(f32)

    cross_sums = contract(inner_low, up_two, ((1,), (1,))).reshape(4, pixels, channels)
    grad_cross = grad_res + member_sum(cross_sums)
    grad_down = own_sum(contract(act_low, branch_rows, over_rows)).astype(bf16)
    grad_upb = own_sum(jnp.sum(inner_low.astype(f32), axis=0))
    relative = pair ^ jnp.arange(4, dtype=jnp.int32)
    grad_up = contract(cross_rows, inner_low, over_rows).reshape(4, 2, slim, 2 * units)
    kept = lax.dynamic_index_in_dim(grad_up, member, 1, keepdims=False)
    sent = lax.dynamic_index_in_dim(grad_up, 1 - member, 1, keepdims=False).astype(bf16)
    sent = swap_pair(jnp.concatenate([sent[:, :, units:], sent[:, :, :units]], axis=2))
    ups = (kept + sent.astype(f32)).astype(bf16)
    ups = [lax.dynamic_index_in_dim(ups, pair ^ step, 0, keepdims=False) for step in range(4)]
    ups = [ups[0]] + [to_pair(ups[step], step) for step in range(1, 4)]

    cbranch = grad_cross.astype(bf16)
    grad_co = contract(cbranch, co_full, ((1,), (1,))).astype(bf16)
    grad_cp = per_token(contract(grad_co, value_blocks, ((1,), (1,))))
    mean = grad_cp[0] * cross_p[0] + grad_cp[1] * cross_p[1] + grad_cp[2] * cross_p[2] + grad_cp[3] * cross_p[3]
    grad_cs = jnp.concatenate([p * (g - mean) for p, g in zip(cross_p, grad_cp)], axis=1).astype(bf16)
    grad_cq = (product(grad_cs, key_blocks) * cross_scale).astype(bf16)

    def from_heads(blocks):
        return jnp.sum(jnp.where(in_head, blocks.reshape(tokens, head_count, channels), 0.0), axis=1)

    grad_kv = jnp.concatenate(
        [
            from_heads(contract(grad_cs, cross_q, over_rows)) * cross_scale,
            from_heads(contract(cross_plow, grad_co, over_rows)),
        ],
        axis=1,
    )
    grad_kv = (grad_kv + swap_pair(grad_kv)).astype(bf16)
    grad_self = grad_cross + contract(grad_cq, cq_full, ((1,), (1,)))

    sbranch = grad_self.astype(bf16)

    outward = jnp.concatenate([cbranch, grad_cq, sbranch], axis=1)
    few = jnp.pad(grad_kv.reshape(-1), (0, outward.shape[1] * 16 - grad_kv.size)).reshape(16, -1)
    outward = jnp.concatenate([outward, few])
    outward = exchange(outward)
    grad_att = contract(sbranch, out_full, ((1,), (1,))).astype(bf16)
    mlp_grads = jnp.concatenate([grad_down.reshape(4, -1, channels)] + [x[None] for x in ups])
    mlp_grads, grad_att = lax.optimization_barrier((mlp_grads, grad_att))
    grad_qloc, grad_kall, grad_vall = attend_back(queries, keys_all, values_all, grad_att)
    mlp_grads = lax.psum(after(mlp_grads, bank_other, grad_qloc), "rows")
    theirs = swap_pair(jnp.concatenate([grad_kall[pixels:], grad_vall[pixels:]], axis=1))
    grad_q = (grad_qloc + (grad_kall[:pixels] + theirs[:, :channels])).astype(bf16)
    grad_v = (grad_vall[:pixels] + theirs[:, channels:]).astype(bf16)
    grad_hidden = grad_self + contract(grad_q, qk_full, ((1,), (1,))) + contract(grad_v, val_full, ((1,), (1,)))
    grad_pre = grad_hidden * jnp.where(pre_act > 0, 1.0, SLOPE)
    grad_conv = (grad_pre * demodulate).astype(bf16)

    steps = [grad_conv] + [
        lax.ppermute(grad_conv, "rows", [(z, (z + k) % 4) for z in range(4)]) for k in range(1, 4)
    ]
    grad_cols = trade(jnp.transpose(grad_conv.reshape(pixels, 8, slim), (1, 0, 2)))
    conv_all = gather(jnp.stack(lax.optimization_barrier((*steps, grad_cols))[:4])[None], "batch")
    late = exchange(after(jnp.concatenate([grad_q, grad_v], axis=1), grad_cols))
    grad_maps = grad_cols.reshape(held, sides * sides, slim)
    coef_cols = jnp.square(demod_cols) * jnp.sum(grad_maps.astype(f32) * conv_cols, axis=1)
    all_taps = pool_matrix(jnp.arange(9, dtype=jnp.int32), sides)
    shifted = jnp.einsum(
        "tlp,spo->tslo", all_taps, grad_maps, preferred_element_type=f32
    )
    shifted = shifted.astype(bf16).reshape(9, held * lows, slim)
    grad_low = lax.dot_general(
        shifted, bank_cols[0], (((0, 2), (0, 2)), ((), ())), preferred_element_type=f32
    ).reshape(held, lows, channels)
    grad_low_other = lax.dot_general(
        shifted, bank_cols[1], (((0, 2), (0, 2)), ((), ())), preferred_element_type=f32
    ).reshape(held, lows, channels)
    mod_low = own_mod.astype(f32)
    select_taps = jnp.stack(
        [jnp.sum(mod_low * grad_low, axis=(1, 2)), jnp.sum(mod_low * grad_low_other, axis=(1, 2))], axis=1
    )
    low_partial = own_select[:, 0, None, None] * grad_low + own_select[:, 1, None, None] * grad_low_other
    low_parts = trade(low_partial.astype(bf16).reshape(8, lows // 2, channels))
    low_total = jnp.sum(low_parts.astype(f32), axis=0)

    held_back = lax.optimization_barrier((act_low, low_partial, *inward, *outward))
    act_low = held_back[0]
    inward, outward = jnp.stack(held_back[2:6]), jnp.stack(held_back[6:])
    result = product(act_low, down_two).reshape(4, pixels, channels)
    result = (after_cross + member_sum(result)).astype(bf16)
    colour = contract(rgb_full.astype(bf16), result, ((1,), (1,)))
    grad_rgb_w = contract(grad_rgb, result.astype(f32), ((0,), (0,)), HIGH)
    context_cols = jnp.take(context_cols.reshape(held, -1), relative, axis=0).reshape(held * tokens, slim)
    kv_all = outward[:, pixels:].reshape(held, -1)[:, : grad_kv.size].reshape(held * tokens, 2 * channels)
    grad_ck_w = contract(context_cols, kv_all[:, :channels], over_rows).astype(bf16)
    grad_cv_w = contract(context_cols, kv_all[:, channels:], over_rows).astype(bf16)
    grad_context = contract(kv_all[:, :channels], ck_w, ((1,), (1,))) + contract(kv_all[:, channels:], cv_w, ((1,), (1,)))
    grad_context = jnp.take(grad_context.reshape(held, -1), relative, axis=0)
    to_channel = [contract(coef_cols, x, ((1,), (1,)), HIGH) for x in products]
    first_share, other_share = own_select[:, :1], own_select[:, 1:]
    scale_term = -own_scales * (
        first_share * first_share * to_channel[0]
        + 2.0 * first_share * other_share * to_channel[1]
        + other_share * other_share * to_channel[2]
    )
    square_scales = jnp.square(own_scales)
    energy = [jnp.sum(square_scales * x, axis=1, keepdims=True) for x in to_channel]
    select_term = jnp.concatenate(
        [
            first_share * energy[0] + other_share * energy[1],
            first_share * energy[1] + other_share * energy[2],
        ],
        axis=1,
    )
    select_partial = select_taps - select_term

    member_scales = lax.dynamic_index_in_dim(own_scales, pair, 0, keepdims=False)
    feat_own = feat_all.reshape(total * lows, channels)
    feat_own = lax.dynamic_slice_in_dim(feat_own, first * lows + device * (lows // 2), lows // 2, 0).astype(f32)
    grad_input_rows = low_total * member_scales
    square_sum = jnp.sum(jnp.square(grad_input_rows))

    outward = outward[:, :pixels]

    def weight_gradients(picks, grads):
        parts = []
        for order, pick in enumerate(picks):
            right = grads[:, :, order * channels : (order + 1) * channels]
            parts.append(contract(inward[:, pick], right, ((0, 1), (0, 1))))
        parts = pair_sum(jnp.stack(parts).reshape(len(picks), 2 * slim, channels), 1)
        return parts.astype(bf16)

    grads_three = weight_gradients((0, 1, 2), outward)
    late = jnp.stack(lax.optimization_barrier((*late, low_total))[:4])
    grads_two = weight_gradients((3, 3), late)

    mids = jnp.concatenate([grads_three, grad_ck_w[None], grad_cv_w[None], grads_two])

    grad_hidden_sums = jnp.stack([jnp.sum(grad_pre, axis=0), jnp.sum(grad_pre * noise_col, axis=0)])
    singles = jnp.concatenate([select_partial.reshape(-1), square_sum[None], jnp.zeros((127 - 2 * held,), f32)])
    singles = jnp.concatenate([coef_cols.reshape(-1), singles])
    last_sent = jnp.concatenate(
        [
            grad_hidden_sums,
            grad_rgb_w,
            grad_context.reshape(-1, channels),
            jnp.sum(low_total * feat_own, axis=0)[None],
            scale_term,
            jnp.pad(singles, (0, channels - singles.shape[0]))[None],
        ]
    )
    last_sent, mids = lax.optimization_barrier((last_sent, mids, mlp_grads, bank_other))[:2]
    mids = lax.psum(mids, "rows")
    last_all = gather(last_sent[None], "batch")
    col_sums = jnp.sum(lax.dynamic_slice_in_dim(last_all[:, :5], device * slim, slim, 2), axis=0)
    context_grads = jnp.transpose(last_all[:, 5:7].reshape(8, held * tokens, slim), (1, 0, 2)).reshape(held, -1)
    table_cols = class_table.shape[1]
    context_grads = lax.dynamic_slice_in_dim(context_grads, device * table_cols, table_cols, 1)
    grad_scales = jnp.sum(last_all[:, 7].reshape(held, 2, channels), axis=1) + jnp.sum(last_all[:, 8 : 8 + held], axis=0)
    singles = last_all[:, 8 + held]
    coef_plane = jnp.transpose(singles[:, : held * slim].reshape(8, held, slim), (1, 0, 2)).reshape(-1)
    singles = jnp.sum(singles[:, held * slim : held * slim + 128], axis=0)
    pieces = [coef_plane, context_grads.reshape(-1), grad_scales.reshape(-1), col_sums.reshape(-1), grad_upb, singles]
    ends = []
    for x in pieces:
        ends.append(x.shape[0] + (ends[-1] if ends else 0))
    rows_all = gather(jnp.concatenate(pieces).reshape(1, -1, 128), "rows").reshape(4, -1)
    coef = rows_all[:, : ends[0]].reshape(total, channels)
    context_grads = rows_all[:, ends[0] : ends[1]].reshape(total, table_cols)
    grad_scales = rows_all[:, ends[1] : ends[2]].reshape(total, channels)
    rows_total = jnp.sum(rows_all[:, ends[2] : ends[4]], axis=0)
    sum_bias, sum_gain = rows_total[:slim], rows_total[slim : 2 * slim]
    sum_rgb = rows_total[2 * slim : 5 * slim].reshape(3, slim)
    sum_upb = rows_total[5 * slim :]
    singles = rows_all[:, ends[4] :]
    grad_select = singles[:, : 2 * held].reshape(total, 2)
    square_sum = jnp.sum(singles[:, 2 * held])
    classes = class_table.shape[0]
    one_hot = (labels_all[:, None] == jnp.arange(classes)[None, :]).astype(f32)
    sum_table = contract(one_hot, context_grads, over_rows, HIGH)
    entries = float(total * 4 * in_rows * in_cols * channels)
    r1_value = square_sum / entries
    style_f32 = style_own.astype(f32)
    grad_logits = select * (grad_select - jnp.sum(grad_select * select, axis=-1, keepdims=True))
    sum_mod = contract(style_f32, grad_scales, over_rows, HIGH)
    sum_sel = contract(style_f32, grad_logits, over_rows, HIGH)

    first_tap = 2 * (device % 4)
    matrix = pool_matrix(first_tap + jnp.arange(3, dtype=jnp.int32), sides)
    order = (plane - jnp.arange(4, dtype=jnp.int32)) % 4
    shifted_all = pool_samples(order, matrix, conv_all.reshape(4, 2, 4, pixels, channels))
    square_all = jnp.square(scales)
    blocks = (device % 4) * 9 + jnp.arange(9, dtype=jnp.int32)
    bank_total = bank_gradient(
        blocks // 4 - first_tap,
        blocks % 4,
        left,
        shifted_all.reshape(3, total * lows, channels),
        kernel_bank,
        bank_other,
        split_terms(own_share * own_share * square_all, True),
        split_terms(own_share * share_other * square_all, True),
        split_terms(coef, False),
    )

    mids, mlp_grads = after(mids, bank_total).astype(f32), after(mlp_grads, low_total).astype(f32)
    sum_down = mlp_grads[:4].reshape(units, channels)
    ordered = [lax.dynamic_index_in_dim(mlp_grads, 4 + (pair ^ c), 0, keepdims=False) for c in range(4)]
    swapped = [jnp.concatenate([x[:, units:], x[:, :units]], axis=1) for x in ordered]
    sum_up = jnp.where(member == 0, jnp.concatenate(ordered, axis=1), jnp.concatenate(swapped, axis=1))
    sum_co, sum_cq, sum_out, sum_ck, sum_cv, sum_qk, sum_val = [mids[i] for i in range(7)]

    feat_out = from_pixels(result.reshape(2, piece, channels), odd_z, odd_pair)
    feat_out = feat_out.reshape(slots, 2 * in_rows, sides, channels)
    colour_sent = jnp.transpose(colour.reshape(3, 2, piece), (1, 0, 2)).reshape(2, 1, 3 * piece)
    colour_sent = jnp.pad(colour_sent, ((0, 0), (0, 0), (0, channels - 3 * piece)))
    low_sent = jnp.concatenate([grad_input_rows.reshape(2, lows // 4, channels), colour_sent], axis=1)
    low_back = from_pixels(low_sent, odd_z, odd_pair)
    rgb_out = low_back[:, lows // 4, : 3 * piece].reshape(slots, 3, 2 * in_rows, sides)
    grad_input = low_back[:, : lows // 4].reshape(slots, in_rows, in_cols, channels)
    return (
        feat_out,
        rgb_out,
        grad_input,
        r1_value,
        sum_mod,
        sum_sel,
        bank_total,
        sum_bias,
        sum_gain,
        sum_qk,
        sum_val,
        sum_out,
        sum_cq,
        sum_ck,
        sum_cv,
        sum_co,
        sum_up,
        sum_upb,
        sum_down,
        sum_table,
        sum_rgb,
    )


def solution(mesh):
    split = mesh.shape["batch"] == 8 and mesh.shape["rows"] == 4
    return jax.shard_map(
        by_planes if split else per_device,
        mesh=mesh,
        in_specs=(
            P("batch", "rows", None, None),
            P("batch", None),
            P("batch"),
            P("batch", "rows", None),
            P("batch", "rows", None, None),
            P("batch", None, "rows", None),
            P("batch", None),
            P("batch", None),
            P("batch", None),
            P("batch"),
            P("batch"),
            P("batch", None),
            P("batch", None),
            P("batch", None),
            P("batch", None),
            P("batch", None),
            P("batch", None),
            P("batch", None),
            P("batch", None),
            P("batch"),
            P("batch", None),
            P(None, "batch"),
            P(None, "batch"),
        ),
        out_specs=(
            P("batch", "rows", None, None),
            P("batch", None, "rows", None),
            P("batch", "rows", None, None),
            P(),
            P("batch", None),
            P("batch", None),
            P("batch", None),
            P("batch"),
            P("batch"),
            P("batch", None),
            P("batch", None),
            P("batch", None),
            P("batch", None),
            P("batch", None),
            P("batch", None),
            P("batch", None),
            P("batch", None),
            P("batch"),
            P("batch", None),
            P(None, "batch"),
            P(None, "batch"),
        ),
        check_vma=False,
    )
```

```python
import jax
import jax.numpy as jnp
from jax import lax
from jax.experimental import pallas as pl
from jax.experimental.pallas import tpu as pltpu
from jax.sharding import PartitionSpec as P

HEAD_DIM = 64


HIGH = lax.Precision.HIGHEST
EPSILON = 1e-08
SLOPE = 0.2


def with_halo(cells, sides, width):
    for axis, dim in sides:
        count = lax.axis_size(axis)
        ends = count - 1
        head = lax.slice_in_dim(cells, 0, width, axis=dim)
        tail = lax.slice_in_dim(cells, cells.shape[dim] - width, cells.shape[dim], axis=dim)
        cells = jnp.concatenate(
            [
                lax.ppermute(tail, axis, [(i, (i + 1) % count) for i in range(ends)]),
                cells,
                lax.ppermute(head, axis, [((i + 1) % count, i) for i in range(ends)]),
            ],
            axis=dim,
        )
    return cells


def product(left, right):
    return jnp.dot(left, right, preferred_element_type=jnp.float32)


def kernel_mix(bank_split, select_row):
    mixed_kernel = select_row[0] * bank_split[0].astype(jnp.float32)
    mixed_kernel = mixed_kernel + select_row[1] * bank_split[1].astype(jnp.float32)
    return mixed_kernel


def gather_taps(padded, out_rows, out_cols, flipped):
    pieces = []
    for row_off in range(3):
        for col_off in range(3):
            if flipped:
                pieces.append(
                    padded[
                        :,
                        2 - row_off : 2 - row_off + out_rows,
                        2 - col_off : 2 - col_off + out_cols,
                    ]
                )
            else:
                pieces.append(padded[:, row_off : row_off + out_rows, col_off : col_off + out_cols])
    return jnp.concatenate(pieces, axis=-1)


def per_device(
    feat_in,
    style_vec,
    labels,
    noise_map,
    cot_feat,
    cot_rgb,
    mod_w,
    sel_w,
    kernel_bank,
    conv_bias,
    noise_gain,
    qk_w,
    val_w,
    out_w,
    cq_w,
    ck_w,
    cv_w,
    co_w,
    up_w,
    up_b,
    down_w,
    class_table,
    rgb_w,
):
    f32 = jnp.float32
    bf16 = jnp.bfloat16
    (
        mod_full,
        sel_full,
        bias_full,
        gain_full,
        qk_full,
        val_full,
        out_full,
        cq_full,
        ck_full,
        cv_full,
        co_full,
        up_full,
        upb_full,
        down_full,
        table_full,
        rgb_full,
    ) = (
        lax.all_gather(mod_w, "batch", axis=0, tiled=True),
        lax.all_gather(sel_w, "batch", axis=0, tiled=True),
        lax.all_gather(conv_bias, "batch", axis=0, tiled=True),
        lax.all_gather(noise_gain, "batch", axis=0, tiled=True),
        lax.all_gather(qk_w, "batch", axis=0, tiled=True),
        lax.all_gather(val_w, "batch", axis=0, tiled=True),
        lax.all_gather(out_w, "batch", axis=0, tiled=True),
        lax.all_gather(cq_w, "batch", axis=0, tiled=True),
        lax.all_gather(ck_w, "batch", axis=0, tiled=True),
        lax.all_gather(cv_w, "batch", axis=0, tiled=True),
        lax.all_gather(co_w, "batch", axis=0, tiled=True),
        lax.all_gather(up_w, "batch", axis=0, tiled=True),
        lax.all_gather(up_b, "batch", axis=0, tiled=True),
        lax.all_gather(down_w, "batch", axis=0, tiled=True),
        lax.all_gather(class_table, "batch", axis=1, tiled=True),
        lax.all_gather(rgb_w, "batch", axis=1, tiled=True),
    )
    bank_full = lax.all_gather(kernel_bank, "batch", axis=0, tiled=True)
    samples, in_rows, in_cols, channels = feat_in.shape
    out_rows = 2 * in_rows
    out_cols = 2 * in_cols
    pixels = out_rows * out_cols
    span = 9 * channels
    kernels = bank_full.shape[0] // span
    head_dim = HEAD_DIM
    head_count = channels // head_dim
    bank_split = bank_full.reshape(kernels, span, channels)
    scales = 1.0 + product(style_vec, mod_full)
    select = jax.nn.softmax(product(style_vec, sel_full), axis=-1)
    scale_tiled = jnp.tile(scales, (1, 9))
    upsampled = jnp.repeat(jnp.repeat(feat_in, 2, axis=1), 2, axis=2)
    modulated = (upsampled.astype(f32) * scales[:, None, None, :]).astype(bf16)
    with_rim = with_halo(modulated, (("rows", 1),), 1)
    padded = jnp.pad(with_rim, ((0, 0), (0, 0), (1, 1), (0, 0)))
    patches = gather_taps(padded, out_rows, out_cols, False).reshape(samples, pixels, span)

    def conv_forward(sample_item):
        patch_row, select_row, scale_row = sample_item
        mixed_kernel = kernel_mix(bank_split, select_row)
        demod_row = lax.rsqrt(
            jnp.sum(jnp.square(mixed_kernel * scale_row[:, None]), axis=0) + EPSILON
        )
        return (product(patch_row, mixed_kernel.astype(bf16)), demod_row, mixed_kernel)

    conv_out, demodulate, mixed_all = lax.map(conv_forward, (patches, select, scale_tiled))
    noise_flat = noise_map.reshape(samples, pixels, 1)
    pre_act = (
        conv_out * demodulate[:, None, :]
        + gain_full.astype(f32) * noise_flat
        + bias_full.astype(f32)
    )
    hidden = jnp.where(pre_act > 0, pre_act, SLOPE * pre_act)
    hidden_low = hidden.astype(bf16)
    queries = product(hidden_low, qk_full).astype(bf16)
    values = product(hidden_low, val_full).astype(bf16)
    all_queries, all_values = (
        lax.all_gather(queries, "rows", axis=1, tiled=True),
        lax.all_gather(values, "rows", axis=1, tiled=True),
    )
    query_h = queries.reshape(samples, pixels, head_count, head_dim)
    key_h = all_queries.reshape(samples, -1, head_count, head_dim)
    value_h = all_values.reshape(samples, -1, head_count, head_dim)
    key_f32 = key_h.astype(f32)
    key_norm = jnp.transpose(jnp.sum(jnp.square(key_f32), axis=-1), (0, 2, 1))[:, :, None, :]
    l2_scale = 0.5 * head_dim ** (-0.5)

    def self_scores():
        inner_dots = jnp.einsum("bqhd,bkhd->bhqk", query_h, key_h, preferred_element_type=f32)
        return l2_scale * (2.0 * inner_dots - key_norm)

    scores = self_scores()
    row_max = jnp.max(scores, axis=-1, keepdims=True)
    log_total = row_max + jnp.log(jnp.sum(jnp.exp(scores - row_max), axis=-1, keepdims=True))
    probs_low = jnp.exp(scores - log_total).astype(bf16)
    attended = (
        jnp.einsum("bhqk,bkhd->bqhd", probs_low, value_h, preferred_element_type=f32)
        .reshape(samples, pixels, channels)
        .astype(bf16)
    )
    after_self = hidden + product(attended, out_full)
    self_low = after_self.astype(bf16)
    cross_q = product(self_low, cq_full).astype(bf16).reshape(samples, pixels, head_count, head_dim)
    classes = table_full.shape[0]
    one_hot = (labels[:, None] == jnp.arange(classes)[None, :]).astype(bf16)
    contexts = table_full.shape[1] // channels
    context = product(one_hot, table_full).astype(bf16).reshape(samples, contexts, channels)
    cross_k = jnp.einsum("bjc,cd->bjd", context, ck_full, preferred_element_type=f32).astype(bf16)
    cross_v = jnp.einsum("bjc,cd->bjd", context, cv_full, preferred_element_type=f32).astype(bf16)
    key_cross = cross_k.reshape(samples, contexts, head_count, head_dim)
    value_cross = cross_v.reshape(samples, contexts, head_count, head_dim)
    cross_scale = head_dim ** (-0.5)
    cross_s = (
        jnp.einsum("bqhd,bjhd->bhqj", cross_q, key_cross, preferred_element_type=f32) * cross_scale
    )
    cross_p = jax.nn.softmax(cross_s, axis=-1)
    cross_plow = cross_p.astype(bf16)
    cross_o = (
        jnp.einsum("bhqj,bjhd->bqhd", cross_plow, value_cross, preferred_element_type=f32)
        .reshape(samples, pixels, channels)
        .astype(bf16)
    )
    after_cross = after_self + product(cross_o, co_full)
    cross_low = after_cross.astype(bf16)
    inner = product(cross_low, up_full) + upb_full.astype(f32)
    activated, gelu_pull = jax.vjp(jax.nn.gelu, inner)
    act_low = activated.astype(bf16)
    after_mlp = after_cross + product(act_low, down_full)
    result = after_mlp.astype(bf16)
    colour = product(result, rgb_full.T)
    rgb_out = jnp.transpose(colour, (0, 2, 1)).reshape(samples, 3, out_rows, out_cols)
    grad_rgb = jnp.transpose(cot_rgb.reshape(samples, 3, pixels), (0, 2, 1))
    grad_res = cot_feat.reshape(samples, pixels, channels).astype(f32) + jnp.dot(
        grad_rgb, rgb_full.astype(f32), precision=HIGH
    )
    grad_rgb_w = jnp.einsum("bpk,bpc->kc", grad_rgb, result.astype(f32), precision=HIGH)
    branch = grad_res.astype(bf16)
    grad_down_w = jnp.einsum("bpf,bpc->fc", act_low, branch, preferred_element_type=f32)
    (grad_inner,) = gelu_pull(product(branch, down_full.T))
    inner_low = grad_inner.astype(bf16)
    grad_up_b = jnp.sum(inner_low.astype(f32), axis=(0, 1))
    grad_up_w = jnp.einsum("bpc,bpf->cf", cross_low, inner_low, preferred_element_type=f32)
    grad_cross = grad_res + product(inner_low, up_full.T)
    cbranch = grad_cross.astype(bf16)
    grad_co_w = jnp.einsum("bpc,bpd->cd", cross_o, cbranch, preferred_element_type=f32)
    grad_co = (
        product(cbranch, co_full.T).astype(bf16).reshape(samples, pixels, head_count, head_dim)
    )
    grad_cp = jnp.einsum("bqhd,bjhd->bhqj", grad_co, value_cross, preferred_element_type=f32)
    grad_cv = (
        jnp.einsum("bhqj,bqhd->bjhd", cross_plow, grad_co, preferred_element_type=f32)
        .astype(bf16)
        .reshape(samples, contexts, channels)
    )
    grad_cs = (cross_p * (grad_cp - jnp.sum(grad_cp * cross_p, axis=-1, keepdims=True))).astype(
        bf16
    )
    grad_cq = (
        (
            jnp.einsum("bhqj,bjhd->bqhd", grad_cs, key_cross, preferred_element_type=f32)
            * cross_scale
        )
        .astype(bf16)
        .reshape(samples, pixels, channels)
    )
    grad_ck = (
        (jnp.einsum("bhqj,bqhd->bjhd", grad_cs, cross_q, preferred_element_type=f32) * cross_scale)
        .astype(bf16)
        .reshape(samples, contexts, channels)
    )
    grad_cq_w = jnp.einsum("bpc,bpd->cd", self_low, grad_cq, preferred_element_type=f32)
    grad_ck_w = jnp.einsum("bjc,bjd->cd", context, grad_ck, preferred_element_type=f32)
    grad_cv_w = jnp.einsum("bjc,bjd->cd", context, grad_cv, preferred_element_type=f32)
    grad_context = jnp.einsum(
        "bjd,cd->bjc", grad_ck, ck_full, preferred_element_type=f32
    ) + jnp.einsum("bjd,cd->bjc", grad_cv, cv_full, preferred_element_type=f32)
    grad_table = jnp.dot(
        one_hot.astype(f32).T, grad_context.reshape(samples, contexts * channels), precision=HIGH
    )
    grad_self = grad_cross + product(grad_cq, cq_full.T)
    sbranch = grad_self.astype(bf16)
    grad_out_w = jnp.einsum("bpc,bpd->cd", attended, sbranch, preferred_element_type=f32)
    grad_att = (
        product(sbranch, out_full.T).astype(bf16).reshape(samples, pixels, head_count, head_dim)
    )
    probs = jnp.exp(self_scores() - log_total)
    probs_again = probs.astype(bf16)
    grad_probs = jnp.einsum("bqhd,bkhd->bhqk", grad_att, value_h, preferred_element_type=f32)
    grad_vall = jnp.einsum("bhqk,bqhd->bkhd", probs_again, grad_att, preferred_element_type=f32)
    grad_s = (probs * (grad_probs - jnp.sum(grad_probs * probs, axis=-1, keepdims=True))).astype(
        bf16
    )
    grad_qloc = (
        2.0 * l2_scale * jnp.einsum("bhqk,bkhd->bqhd", grad_s, key_h, preferred_element_type=f32)
    )
    col_total = jnp.transpose(jnp.sum(grad_s.astype(f32), axis=2), (0, 2, 1))[:, :, :, None]
    grad_kall = (
        2.0
        * l2_scale
        * (
            jnp.einsum("bhqk,bqhd->bkhd", grad_s, query_h, preferred_element_type=f32)
            - key_f32 * col_total
        )
    )
    back_keys, back_values = (
        lax.psum_scatter(
            grad_kall.reshape(samples, -1, channels).astype(jnp.bfloat16),
            "rows",
            scatter_dimension=1,
            tiled=True,
        ).astype(jnp.float32),
        lax.psum_scatter(
            grad_vall.reshape(samples, -1, channels).astype(jnp.bfloat16),
            "rows",
            scatter_dimension=1,
            tiled=True,
        ).astype(jnp.float32),
    )
    grad_q = (grad_qloc.reshape(samples, pixels, channels) + back_keys).astype(bf16)
    grad_v = back_values.astype(bf16)
    grad_qk_w = jnp.einsum("bpc,bpd->cd", hidden_low, grad_q, preferred_element_type=f32)
    grad_val_w = jnp.einsum("bpc,bpd->cd", hidden_low, grad_v, preferred_element_type=f32)
    grad_hidden = grad_self + product(grad_q, qk_full.T) + product(grad_v, val_full.T)
    grad_pre = grad_hidden * jnp.where(pre_act > 0, 1.0, SLOPE)
    grad_gain = jnp.sum(grad_pre * noise_flat, axis=(0, 1))
    grad_bias = jnp.sum(grad_pre, axis=(0, 1))
    grad_demod = jnp.sum(grad_pre * conv_out, axis=1)
    demod_coef = demodulate**3 * grad_demod
    grad_conv = (grad_pre * demodulate[:, None, :]).astype(bf16)
    grad_rim = with_halo(
        grad_conv.reshape(samples, out_rows, out_cols, channels), (("rows", 1),), 1
    )
    grad_pad = jnp.pad(grad_rim, ((0, 0), (0, 0), (1, 1), (0, 0)))
    grad_patches = gather_taps(grad_pad, out_rows, out_cols, True).reshape(samples, pixels, span)

    def conv_backward(sample_item):
        gpatch_row, mixed_kernel, scale_row, coef_row = sample_item
        taps_low = mixed_kernel.astype(bf16).reshape(9, channels, channels)
        grad_mod = jnp.einsum(
            "pto,tio->pi",
            gpatch_row.reshape(pixels, 9, channels),
            taps_low,
            preferred_element_type=f32,
        )
        scale_term = -scale_row[:channels] * jnp.sum(
            (jnp.square(mixed_kernel) * coef_row[None, :]).reshape(9, channels, channels),
            axis=(0, 2),
        )
        return (grad_mod, scale_term)

    grad_mod, scale_term = lax.map(
        conv_backward, (grad_patches, mixed_all, scale_tiled, demod_coef)
    )
    block_rows = span // 8

    def tap_block(index, carry):
        bank_acc, select_acc = carry
        tap_row = index * block_rows
        patch_cols = lax.dynamic_slice_in_dim(patches, tap_row, block_rows, 2)
        grad_taps = jnp.einsum("bpt,bpo->bto", patch_cols, grad_conv, preferred_element_type=f32)
        bank_rows = lax.dynamic_slice_in_dim(bank_split, tap_row, block_rows, 1).astype(f32)
        mixed_rows = lax.dynamic_slice_in_dim(mixed_all, tap_row, block_rows, 1)
        scale_rows = lax.dynamic_slice_in_dim(scale_tiled, tap_row, block_rows, 1)
        grad_mixed = (
            grad_taps - mixed_rows * jnp.square(scale_rows)[:, :, None] * demod_coef[:, None, :]
        )
        select_acc = select_acc + jnp.einsum("kto,bto->bk", bank_rows, grad_mixed, precision=HIGH)
        bank_piece = jnp.einsum("bk,bto->kto", select, grad_mixed, precision=HIGH)
        bank_acc = lax.dynamic_update_slice_in_dim(bank_acc, bank_piece, tap_row, 1)
        return (bank_acc, select_acc)

    bank_acc, grad_select = lax.fori_loop(
        0,
        8,
        tap_block,
        (jnp.zeros((kernels, span, channels), f32), jnp.zeros((samples, kernels), f32)),
    )
    bank_flat = bank_acc.reshape(kernels * span, channels)
    grad_mod = grad_mod.reshape(samples, out_rows, out_cols, channels)
    grad_scales = jnp.sum(grad_mod * upsampled.astype(f32), axis=(1, 2)) + scale_term
    grad_up = grad_mod * scales[:, None, None, :]
    grad_input = grad_up.reshape(samples, in_rows, 2, in_cols, 2, channels).sum(axis=(2, 4))
    grad_logits = select * (grad_select - jnp.sum(grad_select * select, axis=-1, keepdims=True))
    style_f32 = style_vec.astype(f32)
    grad_mod_w = jnp.dot(style_f32.T, grad_scales, precision=HIGH)
    grad_sel_w = jnp.dot(style_f32.T, grad_logits, precision=HIGH)
    (
        sum_mod,
        sum_sel,
        sum_bias,
        sum_gain,
        sum_qk,
        sum_val,
        sum_out,
        sum_cq,
        sum_ck,
        sum_cv,
        sum_co,
        sum_up,
        sum_upb,
        sum_down,
        sum_table,
        sum_rgb,
    ) = (
        lax.psum_scatter(grad_mod_w, "batch", scatter_dimension=0, tiled=True),
        lax.psum_scatter(grad_sel_w, "batch", scatter_dimension=0, tiled=True),
        lax.psum_scatter(grad_bias, "batch", scatter_dimension=0, tiled=True),
        lax.psum_scatter(grad_gain, "batch", scatter_dimension=0, tiled=True),
        lax.psum_scatter(grad_qk_w, "batch", scatter_dimension=0, tiled=True),
        lax.psum_scatter(grad_val_w, "batch", scatter_dimension=0, tiled=True),
        lax.psum_scatter(grad_out_w, "batch", scatter_dimension=0, tiled=True),
        lax.psum_scatter(grad_cq_w, "batch", scatter_dimension=0, tiled=True),
        lax.psum_scatter(grad_ck_w, "batch", scatter_dimension=0, tiled=True),
        lax.psum_scatter(grad_cv_w, "batch", scatter_dimension=0, tiled=True),
        lax.psum_scatter(grad_co_w, "batch", scatter_dimension=0, tiled=True),
        lax.psum_scatter(grad_up_w, "batch", scatter_dimension=0, tiled=True),
        lax.psum_scatter(grad_up_b, "batch", scatter_dimension=0, tiled=True),
        lax.psum_scatter(grad_down_w, "batch", scatter_dimension=0, tiled=True),
        lax.psum_scatter(grad_table, "batch", scatter_dimension=1, tiled=True),
        lax.psum_scatter(grad_rgb_w, "batch", scatter_dimension=1, tiled=True),
    )
    bank_part = lax.psum_scatter(bank_flat, "batch", scatter_dimension=0, tiled=True)
    (
        sum_mod,
        sum_sel,
        sum_bias,
        sum_gain,
        sum_qk,
        sum_val,
        sum_out,
        sum_cq,
        sum_ck,
        sum_cv,
        sum_co,
        sum_up,
        sum_upb,
        sum_down,
        sum_table,
        sum_rgb,
        bank_total,
    ) = (
        lax.psum(sum_mod.astype(jnp.bfloat16), "rows").astype(jnp.float32),
        lax.psum(sum_sel.astype(jnp.bfloat16), "rows").astype(jnp.float32),
        lax.psum(sum_bias.astype(jnp.bfloat16), "rows").astype(jnp.float32),
        lax.psum(sum_gain.astype(jnp.bfloat16), "rows").astype(jnp.float32),
        lax.psum(sum_qk.astype(jnp.bfloat16), "rows").astype(jnp.float32),
        lax.psum(sum_val.astype(jnp.bfloat16), "rows").astype(jnp.float32),
        lax.psum(sum_out.astype(jnp.bfloat16), "rows").astype(jnp.float32),
        lax.psum(sum_cq.astype(jnp.bfloat16), "rows").astype(jnp.float32),
        lax.psum(sum_ck.astype(jnp.bfloat16), "rows").astype(jnp.float32),
        lax.psum(sum_cv.astype(jnp.bfloat16), "rows").astype(jnp.float32),
        lax.psum(sum_co.astype(jnp.bfloat16), "rows").astype(jnp.float32),
        lax.psum(sum_up.astype(jnp.bfloat16), "rows").astype(jnp.float32),
        lax.psum(sum_upb.astype(jnp.bfloat16), "rows").astype(jnp.float32),
        lax.psum(sum_down.astype(jnp.bfloat16), "rows").astype(jnp.float32),
        lax.psum(sum_table.astype(jnp.bfloat16), "rows").astype(jnp.float32),
        lax.psum(sum_rgb.astype(jnp.bfloat16), "rows").astype(jnp.float32),
        lax.psum(bank_part.astype(jnp.bfloat16), "rows").astype(jnp.float32),
    )
    entry_count = float(
        samples * lax.axis_size("batch") * in_rows * lax.axis_size("rows") * in_cols * channels
    )
    r1_value = lax.psum(jnp.sum(jnp.square(grad_input)), ("batch", "rows")) / entry_count
    feat_out = result.reshape(samples, out_rows, out_cols, channels)
    return (
        feat_out,
        rgb_out,
        grad_input,
        r1_value,
        sum_mod,
        sum_sel,
        bank_total,
        sum_bias,
        sum_gain,
        sum_qk,
        sum_val,
        sum_out,
        sum_cq,
        sum_ck,
        sum_cv,
        sum_co,
        sum_up,
        sum_upb,
        sum_down,
        sum_table,
        sum_rgb,
    )


def gather(x, axis_name, axis=0):
    return lax.all_gather(x, axis_name, axis=axis, tiled=True)


def trade(x):
    return lax.all_to_all(x, "batch", 0, 0, tiled=True)


def to_pair(x, step):
    return lax.ppermute(x, "batch", [(i, i ^ (2 * step)) for i in range(8)])


def spread(x):
    return jnp.concatenate([x] + [to_pair(x, step) for step in range(1, 4)])


def exchange(x):
    return [x] + [to_pair(x, step) for step in range(1, 4)]


def member_sum(parts):
    total = parts[0].astype(jnp.float32)
    for step in range(1, 4):
        total = total + to_pair(parts[step].astype(jnp.bfloat16), step).astype(jnp.float32)
    return total


def after(x, *earlier):
    return lax.optimization_barrier((x,) + earlier)[0]


def behind(x, earlier):
    nothing = jnp.minimum(jnp.abs(earlier[(0,) * earlier.ndim].astype(jnp.float32)), 0.0)
    return x + nothing.astype(x.dtype)


def swap_pair(x):
    return lax.ppermute(x, "batch", [(i, i ^ 1) for i in range(8)])


def move_table(turn):
    table = []
    for d in range(8):
        for z in range(4):
            slot = (z % 2) ^ turn
            pair = 2 * (d % 2) + slot
            table.append((4 * d + z, 4 * (2 * pair + z // 2) + d // 2))
    return table


def to_pixels(x, odd_z, odd_pair):
    sent = jnp.where(odd_z, x[::-1], x)
    first = lax.ppermute(sent[0], ("batch", "rows"), move_table(0))
    second = lax.ppermute(sent[1], ("batch", "rows"), move_table(1))
    return jnp.where(odd_pair, jnp.stack([second, first]), jnp.stack([first, second]))


def from_pixels(x, odd_z, odd_pair):
    sent = jnp.where(odd_pair, x[::-1], x)
    back = [[(b, a) for a, b in move_table(turn)] for turn in range(2)]
    first = lax.ppermute(sent[0], ("batch", "rows"), back[0])
    second = lax.ppermute(sent[1], ("batch", "rows"), back[1])
    return jnp.where(odd_z, jnp.stack([second, first]), jnp.stack([first, second]))


def contract(left, right, dims, precision=None):
    return lax.dot_general(
        left, right, (dims, ((), ())), precision=precision, preferred_element_type=jnp.float32
    )


def conv_kernel(
    select_ref, patch_ref, bank_ref, scale_ref, out_ref, square_ref, product_ref, acc_ref, sum_ref
):
    col, row = pl.program_id(0), pl.program_id(1)
    start = jnp.logical_and(col == 0, row == 0)
    last = jnp.logical_and(col == 2, row == 2)

    @pl.when(start)
    def _():
        acc_ref[...] = jnp.zeros_like(acc_ref)
        sum_ref[...] = jnp.zeros_like(sum_ref)
        product_ref[...] = jnp.zeros_like(product_ref)

    first = bank_ref[0, 0].astype(jnp.float32)
    second = bank_ref[1, 0].astype(jnp.float32)
    product_ref[0] += first * first
    product_ref[1] += first * second
    product_ref[2] += second * second
    for b in range(4):
        mixed = select_ref[b, 0] * first + select_ref[b, 1] * second
        scaled = mixed * scale_ref[b]
        sum_ref[b] += jnp.sum(jnp.square(scaled).reshape(-1, 8, 128), axis=0)
        begin = pl.multiple_of(row * 16, 16)
        left = patch_ref[b, 0, pl.ds(begin, 256), :]
        acc_ref[b] += jnp.dot(left, mixed.astype(jnp.bfloat16), preferred_element_type=jnp.float32)

    @pl.when(last)
    def _():
        out_ref[...] = acc_ref[...]
        square_ref[...] = sum_ref[...]


def conv_forward_plane(select, patch_cols, bank_cols, scale_cols):
    samples, _, _, width = patch_cols.shape
    cols = bank_cols.shape[-1]
    f32 = jnp.float32
    return pl.pallas_call(
        conv_kernel,
        grid=(3, 3),
        in_specs=[
            pl.BlockSpec(memory_space=pltpu.SMEM),
            pl.BlockSpec((samples, 1, 288, width), lambda c, a: (0, c, 0, 0)),
            pl.BlockSpec((2, 1, width, cols), lambda c, a: (0, 3 * a + c, 0, 0)),
            pl.BlockSpec((samples, width, cols), lambda c, a: (0, 0, 0)),
        ],
        out_specs=[
            pl.BlockSpec((samples, 256, cols), lambda c, a: (0, 0, 0)),
            pl.BlockSpec((samples, 8, cols), lambda c, a: (0, 0, 0)),
            pl.BlockSpec((3, width, cols), lambda c, a: (0, 0, 0)),
        ],
        out_shape=[
            jax.ShapeDtypeStruct((samples, 256, cols), f32),
            jax.ShapeDtypeStruct((samples, 8, cols), f32),
            jax.ShapeDtypeStruct((3, width, cols), f32),
        ],
        scratch_shapes=[
            pltpu.VMEM((samples, 256, cols), f32),
            pltpu.VMEM((samples, 8, cols), f32),
        ],
        compiler_params=pltpu.CompilerParams(vmem_limit_bytes=40 << 20),
        cost_estimate=pl.CostEstimate(
            flops=2 * samples * 256 * 9 * width * cols, bytes_accessed=20 << 20, transcendentals=0
        ),
        name="conv_plane",
    )(select, patch_cols, bank_cols, scale_cols)


def head_scores(query, key):
    squares = jnp.square(key.astype(jnp.float32))
    upper = squares.astype(jnp.bfloat16)
    lower = (squares - upper.astype(jnp.float32)).astype(jnp.bfloat16)
    ones = jnp.ones((8, HEAD_DIM), jnp.bfloat16)
    over_last = ((1,), (1,))
    norms = contract(ones, upper, over_last) + contract(ones, lower, over_last)
    scale = 0.5 * HEAD_DIM ** (-0.5)
    return scale * (2.0 * contract(query, key, over_last) - norms[0:1])


def head_softmax(scores):
    raised = jnp.exp(scores - jnp.max(scores, axis=-1, keepdims=True))
    return raised * (1.0 / jnp.sum(raised, axis=-1, keepdims=True))


def attend_kernel(query_ref, key_ref, value_ref, out_ref):
    for h in range(query_ref.shape[1] // HEAD_DIM):
        part = slice(h * HEAD_DIM, (h + 1) * HEAD_DIM)
        probs = head_softmax(head_scores(query_ref[:, part], key_ref[:, part]))
        out_ref[:, part] = jnp.dot(
            probs.astype(jnp.bfloat16), value_ref[:, part], preferred_element_type=jnp.float32
        ).astype(jnp.bfloat16)


def attend(query, key, value):
    pixels, width = query.shape
    everything = key.shape[0]
    pair = 4 * HEAD_DIM
    return pl.pallas_call(
        attend_kernel,
        grid=(width // pair,),
        in_specs=[
            pl.BlockSpec((pixels, pair), lambda i: (0, i)),
            pl.BlockSpec((everything, pair), lambda i: (0, i)),
            pl.BlockSpec((everything, pair), lambda i: (0, i)),
        ],
        out_specs=pl.BlockSpec((pixels, pair), lambda i: (0, i)),
        out_shape=jax.ShapeDtypeStruct((pixels, width), jnp.bfloat16),
        cost_estimate=pl.CostEstimate(
            flops=4 * pixels * everything * width, bytes_accessed=3 << 20, transcendentals=1 << 19
        ),
        name="attend",
    )(query, key, value)


def attend_back_kernel(query_ref, key_ref, value_ref, grad_ref, gq_ref, gk_ref, gv_ref):
    bf16 = jnp.bfloat16
    twice = 2.0 * (0.5 * HEAD_DIM ** (-0.5))
    for h in range(query_ref.shape[1] // HEAD_DIM):
        part = slice(h * HEAD_DIM, (h + 1) * HEAD_DIM)
        query, key, value, grad = query_ref[:, part], key_ref[:, part], value_ref[:, part], grad_ref[:, part]
        probs = head_softmax(head_scores(query, key))
        grad_probs = contract(grad, value, ((1,), (1,)))
        mean = jnp.sum(grad_probs * probs, axis=-1, keepdims=True)
        grad_s = (probs * (grad_probs - mean)).astype(bf16)
        gv_ref[:, part] = contract(probs.astype(bf16), grad, ((0,), (0,)))
        gq_ref[:, part] = twice * jnp.dot(grad_s, key, preferred_element_type=jnp.float32)
        both = jnp.concatenate([query, jnp.ones_like(query)], axis=1)
        sums = contract(grad_s, both, ((0,), (0,)))
        gk_ref[:, part] = twice * (
            sums[:, :HEAD_DIM] - key.astype(jnp.float32) * sums[:, HEAD_DIM:]
        )


def attend_back(query, key, value, grad):
    pixels, width = query.shape
    everything = key.shape[0]
    pair = 4 * HEAD_DIM
    few = pl.BlockSpec((pixels, pair), lambda i: (0, i))
    many = pl.BlockSpec((everything, pair), lambda i: (0, i))
    f32 = jnp.float32
    return pl.pallas_call(
        attend_back_kernel,
        grid=(width // pair,),
        in_specs=[few, many, many, few],
        out_specs=[few, many, many],
        out_shape=[
            jax.ShapeDtypeStruct((pixels, width), f32),
            jax.ShapeDtypeStruct((everything, width), f32),
            jax.ShapeDtypeStruct((everything, width), f32),
        ],
        cost_estimate=pl.CostEstimate(
            flops=14 * pixels * everything * width, bytes_accessed=5 << 20, transcendentals=1 << 19
        ),
        name="attend_back",
    )(query, key, value, grad)


def split_terms(x, left):
    upper = x.astype(jnp.bfloat16)
    lower = (x - upper.astype(jnp.float32)).astype(jnp.bfloat16)
    return jnp.concatenate([upper, upper, lower] if left else [upper, lower, upper])


def bank_kernel(tap_ref, part_ref, left_ref, right_ref, own_ref, other_ref, same_ref, cross_ref, coef_ref, out_ref):
    del tap_ref, part_ref
    first = ((0,), (0,))
    out_ref[...] = (
        jnp.dot(left_ref[...], right_ref[0], preferred_element_type=jnp.float32)
        - own_ref[...].astype(jnp.float32) * contract(same_ref[...], coef_ref[...], first)
        - other_ref[...].astype(jnp.float32) * contract(cross_ref[...], coef_ref[...], first)
    )


def bank_gradient(taps, parts, left, right, own, other, same, cross, coef):
    lows = left.shape[1]
    count = taps.shape[0]
    rows = own.shape[0] // count
    out_cols = own.shape[1]
    terms = coef.shape[0]
    return pl.pallas_call(
        bank_kernel,
        grid_spec=pltpu.PrefetchScalarGridSpec(
            num_scalar_prefetch=2,
            grid=(count,),
            in_specs=[
                pl.BlockSpec((rows, lows), lambda m, t, q: (q[m], 0)),
                pl.BlockSpec((1, lows, out_cols), lambda m, t, q: (t[m], 0, 0)),
                pl.BlockSpec((rows, out_cols), lambda m, t, q: (m, 0)),
                pl.BlockSpec((rows, out_cols), lambda m, t, q: (m, 0)),
                pl.BlockSpec((terms, rows), lambda m, t, q: (0, q[m])),
                pl.BlockSpec((terms, rows), lambda m, t, q: (0, q[m])),
                pl.BlockSpec((terms, out_cols), lambda m, t, q: (0, 0)),
            ],
            out_specs=pl.BlockSpec((rows, out_cols), lambda m, t, q: (m, 0)),
        ),
        out_shape=jax.ShapeDtypeStruct((own.shape[0], out_cols), jnp.float32),
        compiler_params=pltpu.CompilerParams(vmem_limit_bytes=40 << 20),
        cost_estimate=pl.CostEstimate(
            flops=2 * lows * own.shape[0] * out_cols, bytes_accessed=32 << 20, transcendentals=0
        ),
        name="bank_gradient",
    )(taps, parts, left, right, own, other, same, cross, coef)


def pool_matrix(taps, side):
    half = side // 2
    shape = (taps.shape[0], half * half, side * side)
    block = lax.broadcasted_iota(jnp.int32, shape, 1)
    pixel = lax.broadcasted_iota(jnp.int32, shape, 2)
    tap = taps[:, None, None]
    row = pixel // side + tap // 3 - 1 - 2 * (block // half)
    col = pixel % side + tap % 3 - 1 - 2 * (block % half)
    inside = (row >= 0) & (row < 2) & (col >= 0) & (col < 2)
    return inside.astype(jnp.bfloat16)


def patch_matrix(low):
    side = 2 * low
    shape = (3 * (side + 2) * side, low * low)
    place = lax.broadcasted_iota(jnp.int32, shape, 0)
    source = lax.broadcasted_iota(jnp.int32, shape, 1)
    offset, place = place // ((side + 2) * side), place % ((side + 2) * side)
    row, col = place // side - 1, place % side + offset - 1
    inside = (row >= 0) & (row < side) & (col >= 0) & (col < side)
    return (inside & (source == (row // 2) * low + col // 2)).astype(jnp.bfloat16)


def pool_kernel(order_ref, matrix_ref, map_ref, out_ref):
    del order_ref
    pixels = matrix_ref.shape[1]
    taps, _, lows, width = out_ref.shape
    grid = map_ref[...].reshape(pixels, width)
    pooled = jnp.dot(matrix_ref[...], grid, preferred_element_type=jnp.float32)
    out_ref[...] = pooled.astype(jnp.bfloat16).reshape(taps, 1, lows, width)


def pool_samples(order, matrix, maps, piece):
    taps, lows, pixels = matrix.shape
    pairs, members, steps, _, width = maps.shape
    return pl.pallas_call(
        pool_kernel,
        grid_spec=pltpu.PrefetchScalarGridSpec(
            num_scalar_prefetch=1,
            grid=(steps, pairs),
            in_specs=[
                pl.BlockSpec((taps * lows, pixels), lambda k, c, o: (0, 0)),
                pl.BlockSpec((1, members, 1, piece, width), lambda k, c, o: (c, 0, k, 0, 0)),
            ],
            out_specs=pl.BlockSpec((taps, 1, lows, width), lambda k, c, o: (0, o[k] * pairs + c, 0, 0)),
        ),
        out_shape=jax.ShapeDtypeStruct((taps, steps * pairs, lows, width), jnp.bfloat16),
        compiler_params=pltpu.CompilerParams(vmem_limit_bytes=40 << 20),
        cost_estimate=pl.CostEstimate(
            flops=2 * taps * lows * pixels * width * steps * pairs, bytes_accessed=14 << 20, transcendentals=0
        ),
        name="pool_samples",
    )(order, matrix.reshape(taps * lows, pixels), maps)


def by_planes(
    feat_in,
    style_vec,
    labels,
    noise_map,
    cot_feat,
    cot_rgb,
    mod_w,
    sel_w,
    kernel_bank,
    conv_bias,
    noise_gain,
    qk_w,
    val_w,
    out_w,
    cq_w,
    ck_w,
    cv_w,
    co_w,
    up_w,
    up_b,
    down_w,
    class_table,
    rgb_w,
):
    f32, bf16 = jnp.float32, jnp.bfloat16
    device, plane = lax.axis_index("batch"), lax.axis_index("rows")
    pair, member = device // 2, device % 2
    odd_z, odd_pair = plane % 2 == 1, pair % 2 == 1
    slots, in_rows, in_cols, channels = feat_in.shape
    total = 8 * slots
    held = total // 4
    piece = 2 * in_rows * 2 * in_cols
    pixels = 2 * piece
    lows = 4 * in_rows * in_cols
    style_width = style_vec.shape[1]
    own_style = style_width // 8
    slim = channels // 8
    head_count = channels // HEAD_DIM

    point_maps = jnp.concatenate(
        [noise_map.reshape(slots, 1, piece), cot_rgb.reshape(slots, 3, piece)], axis=1
    )
    point_maps = to_pixels(point_maps, odd_z, odd_pair)
    point_cols = jnp.transpose(point_maps, (0, 2, 1)).reshape(pixels, 4)
    noise_col, grad_rgb = point_cols[:, :1], point_cols[:, 1:]

    packed = jnp.concatenate(
        [
            feat_in.reshape(-1, 128),
            style_vec.reshape(-1, 128),
            conv_bias.reshape(-1, 128),
            noise_gain.reshape(-1, 128),
            rgb_w.reshape(-1, 128),
            jnp.pad(jnp.stack([labels // 32, labels % 32]).astype(bf16), ((0, 0), (0, 128 - slots))),
        ]
    )
    bank_sent = jnp.transpose(kernel_bank.reshape(-1, 8, slim), (1, 0, 2))
    smalls = gather(after(packed, bank_sent, point_cols)[None], "batch")
    feat_rows = feat_in.size // 128
    style_rows = style_vec.size // 128
    at = feat_rows + style_rows
    feat_part = smalls[:, :feat_rows].reshape(total, in_rows * in_cols, channels)
    style_all = smalls[:, feat_rows:at].reshape(total, style_width)
    bias_full = smalls[:, at].astype(f32).reshape(channels)
    gain_full = smalls[:, at + 1].astype(f32).reshape(channels)
    rgb_full = jnp.transpose(smalls[:, at + 2 : at + 5], (1, 0, 2)).astype(f32).reshape(3, channels)
    label_parts = smalls[:, at + 5 : at + 7, :slots].astype(jnp.int32)
    labels_all = (32 * label_parts[:, 0] + label_parts[:, 1]).reshape(total)

    style_own = lax.dynamic_slice_in_dim(style_all, device * own_style, own_style, 1)
    context_own = jnp.take(class_table, labels_all, axis=0)
    partial_styles = jnp.concatenate(
        [
            product(style_own, mod_w),
            jnp.pad(product(style_own, sel_w), ((0, 0), (0, 126))),
            context_own.astype(f32),
        ],
        axis=1,
    )
    styles = gather(partial_styles[None], "batch")
    sums = jnp.sum(styles[:, :, : channels + 128], axis=0)
    scales = 1.0 + sums[:, :channels]
    select = jax.nn.softmax(sums[:, channels : channels + 2], axis=-1)
    context_all = jnp.transpose(styles[:, :, channels + 128 :], (1, 0, 2)).reshape(total, -1).astype(bf16)
    feat_all = gather(feat_part[None], "rows")
    feat_all = jnp.transpose(feat_all, (1, 0, 2, 3)).reshape(total, lows, channels)

    kernels = 2
    bank_cols = trade(after(bank_sent, styles)).reshape(kernels, 9, channels, slim)

    squares = jnp.stack(lax.optimization_barrier((qk_w, val_w, out_w, cq_w, co_w, styles))[:5])
    weights = gather(squares, "batch", 1)
    qk_full, val_full, out_full, cq_full, co_full = [weights[i] for i in range(5)]


    first = held * plane
    tokens = context_all.shape[1] // channels
    modulated = (feat_all.astype(f32) * scales[:, None, :]).astype(bf16)
    own_mod = lax.dynamic_slice_in_dim(modulated, first, held, 0)
    own_scales = lax.dynamic_slice_in_dim(scales, first, held, 0)
    own_select = lax.dynamic_slice_in_dim(select, first, held, 0)
    sides = 2 * in_cols
    patch_cols = jnp.einsum(
        "srl,slc->src",
        jnp.broadcast_to(patch_matrix(in_cols)[None], (held, 3 * (sides + 2) * sides, lows)),
        own_mod,
        preferred_element_type=f32,
    )
    patch_cols = patch_cols.astype(bf16).reshape(held, 3, (sides + 2) * sides, channels)
    kernel_id = device // 4
    own_share = lax.dynamic_index_in_dim(select, kernel_id, 1)
    share_other = lax.dynamic_index_in_dim(select, 1 - kernel_id, 1)
    left = (own_share[:, :, None] * modulated.astype(f32)).astype(bf16)
    left = jnp.transpose(left.reshape(total * lows, channels))
    scale_cols = jnp.broadcast_to(own_scales[:, :, None], (held, channels, slim))
    own_context = lax.dynamic_slice_in_dim(context_all, first, held, 0).reshape(held * tokens, channels)
    context_cols = lax.dynamic_slice_in_dim(own_context, device * slim, slim, 1)
    cross_partial = product(context_cols, jnp.concatenate([ck_w, cv_w], axis=1)).reshape(held, -1, slim)
    cross_partial = jnp.repeat(cross_partial, 2, axis=0)
    bank_cols, patch_cols, left, scale_cols, cross_partial = lax.optimization_barrier(
        (bank_cols, patch_cols, left, scale_cols, cross_partial)
    )
    quarter = kernel_bank.shape[0] // 4
    bank_quarter = lax.dynamic_slice_in_dim(kernel_bank, plane * quarter, quarter, 0)
    across = [[i, i + 4] for i in range(4)]
    bank_quarter = lax.all_gather(after(bank_quarter, bank_cols), "batch", axis_index_groups=across)
    bank_quarter = lax.dynamic_index_in_dim(bank_quarter, 1 - device // 4, 0, keepdims=False)

    conv_cols, square_cols, products = conv_forward_plane(own_select, patch_cols, bank_cols, scale_cols)

    demod_cols = lax.rsqrt(jnp.sum(square_cols, axis=1) + EPSILON)
    extra = jnp.broadcast_to(jnp.repeat(demod_cols, 2, axis=0)[:, None, :], (8, 8, slim))
    sent = jnp.concatenate([conv_cols.reshape(8, pixels, slim), extra, cross_partial], axis=1)
    back = trade(sent)
    cross_kv = jnp.sum(back[:, pixels + 8 :], axis=0).reshape(tokens, 2 * channels).astype(bf16)
    back = jnp.transpose(back[:, : pixels + 8], (1, 0, 2)).reshape(pixels + 8, channels)
    conv_out, demodulate = back[:pixels], back[pixels]

    pre_act = conv_out * demodulate + gain_full * noise_col + bias_full
    hidden = jnp.where(pre_act > 0, pre_act, SLOPE * pre_act)
    hidden_low = hidden.astype(bf16)

    queries = product(hidden_low, qk_full).astype(bf16)
    values = product(hidden_low, val_full).astype(bf16)
    up_sent = jnp.transpose(up_w.reshape(slim, 8, -1), (1, 0, 2))
    up_cols = trade(after(up_sent, queries)).reshape(channels, -1)
    units = up_cols.shape[1]
    up_two = jnp.concatenate([up_cols, swap_pair(up_cols)], axis=1)
    down_two = jnp.concatenate([down_w, swap_pair(after(down_w, queries))])
    bias_two = jnp.concatenate([up_b, swap_pair(after(up_b, queries))]).astype(f32)
    theirs = swap_pair(jnp.concatenate([queries, values], axis=1))
    keys_all = jnp.concatenate([queries, theirs[:, :channels]])
    values_all = jnp.concatenate([values, theirs[:, channels:]])
    cot_sent = after(cot_feat, conv_cols).reshape(slots, piece, channels)
    cot_pixels = to_pixels(cot_sent, odd_z, odd_pair).reshape(pixels, channels)
    grad_res = cot_pixels.astype(f32) + jnp.dot(grad_rgb, rgb_full, precision=HIGH)
    branch = grad_res.astype(bf16)
    branch_rows = spread(branch)
    attended = attend(queries, keys_all, values_all)
    after_self = hidden + product(attended, out_full)
    self_low = after_self.astype(bf16)

    in_head = (jnp.arange(channels)[None, :] // HEAD_DIM == jnp.arange(head_count)[:, None])[None]

    def by_head(rows):
        return jnp.where(in_head, rows[:, None, :], 0).astype(bf16).reshape(tokens * head_count, channels)

    key_blocks, value_blocks = by_head(cross_kv[:, :channels]), by_head(cross_kv[:, channels:])
    cross_scale = HEAD_DIM ** (-0.5)
    cross_q = product(self_low, cq_full).astype(bf16)

    def per_token(x):
        return [x[:, i * head_count : (i + 1) * head_count] for i in range(tokens)]

    cross_s = per_token(contract(cross_q, key_blocks, ((1,), (1,))) * cross_scale)
    top = jnp.maximum(jnp.maximum(cross_s[0], cross_s[1]), jnp.maximum(cross_s[2], cross_s[3]))
    raised = [jnp.exp(x - top) for x in cross_s]
    whole = raised[0] + raised[1] + raised[2] + raised[3]
    cross_p = [x / whole for x in raised]
    cross_plow = jnp.concatenate(cross_p, axis=1).astype(bf16)
    cross_o = product(cross_plow, value_blocks).astype(bf16)
    cross_o = after(cross_o, up_two, down_two, branch_rows)
    after_cross = after_self + product(cross_o, co_full)
    cross_low = after_cross.astype(bf16)

    bank_other = gather(after(bank_quarter, cross_low), "rows")
    cross_rows = spread(cross_low)

    def of_pair(x, step, width, axis):
        return lax.dynamic_slice_in_dim(x, (pair ^ step) * width, width, axis)

    inward = after(jnp.stack([cross_o, self_low, attended, hidden_low]), cross_rows)
    inward = [of_pair(inward, 0, 2 * slim, 2)] + [
        to_pair(of_pair(inward, step, 2 * slim, 2), step) for step in range(1, 4)
    ]
    inner = product(cross_rows, up_two) + bias_two
    activated, gelu_pull = jax.vjp(jax.nn.gelu, inner)
    act_low = activated.astype(bf16)
    (grad_inner,) = gelu_pull(contract(branch_rows, down_two, ((1,), (1,))))
    inner_low = grad_inner.astype(bf16)
    over_rows = ((0,), (0,))

    def pair_sum(x, axis):
        half = x.shape[axis] // 2
        kept = lax.dynamic_slice_in_dim(x, member * half, half, axis)
        sent = lax.dynamic_slice_in_dim(x, (1 - member) * half, half, axis)
        return kept + swap_pair(sent.astype(bf16)).astype(f32)

    def own_sum(x):
        half = x.shape[0] // 2
        return x[:half] + swap_pair(x[half:].astype(bf16)).astype(f32)

    cross_sums = contract(inner_low, up_two, ((1,), (1,))).reshape(4, pixels, channels)
    grad_cross = grad_res + member_sum(cross_sums)
    grad_down = own_sum(contract(act_low, branch_rows, over_rows)).astype(bf16)
    grad_upb = own_sum(jnp.sum(inner_low.astype(f32), axis=0))
    relative = pair ^ jnp.arange(4, dtype=jnp.int32)
    grad_up = contract(cross_rows, inner_low, over_rows).reshape(4, 2, slim, 2 * units)
    kept = lax.dynamic_index_in_dim(grad_up, member, 1, keepdims=False)
    sent = lax.dynamic_index_in_dim(grad_up, 1 - member, 1, keepdims=False).astype(bf16)
    sent = swap_pair(jnp.concatenate([sent[:, :, units:], sent[:, :, :units]], axis=2))
    ups = (kept + sent.astype(f32)).astype(bf16)
    ups = [lax.dynamic_index_in_dim(ups, pair ^ step, 0, keepdims=False) for step in range(4)]
    ups = [ups[0]] + [to_pair(ups[step], step) for step in range(1, 4)]

    cbranch = grad_cross.astype(bf16)
    grad_co = contract(cbranch, co_full, ((1,), (1,))).astype(bf16)
    grad_cp = per_token(contract(grad_co, value_blocks, ((1,), (1,))))
    mean = grad_cp[0] * cross_p[0] + grad_cp[1] * cross_p[1] + grad_cp[2] * cross_p[2] + grad_cp[3] * cross_p[3]
    grad_cs = jnp.concatenate([p * (g - mean) for p, g in zip(cross_p, grad_cp)], axis=1).astype(bf16)
    grad_cq = (product(grad_cs, key_blocks) * cross_scale).astype(bf16)

    def from_heads(blocks):
        return jnp.sum(jnp.where(in_head, blocks.reshape(tokens, head_count, channels), 0.0), axis=1)

    grad_kv = jnp.concatenate(
        [
            from_heads(contract(grad_cs, cross_q, over_rows)) * cross_scale,
            from_heads(contract(cross_plow, grad_co, over_rows)),
        ],
        axis=1,
    )
    grad_kv = (grad_kv + swap_pair(grad_kv)).astype(bf16)
    grad_self = grad_cross + contract(grad_cq, cq_full, ((1,), (1,)))

    sbranch = grad_self.astype(bf16)

    token_rows = jnp.pad(grad_kv.reshape(2 * tokens, channels), ((0, 16 - 2 * tokens), (0, 0)))
    out_first = exchange(cbranch)
    out_second = exchange(jnp.concatenate([grad_cq, token_rows]))
    out_third = exchange(sbranch)
    sbranch = after(sbranch, *out_first)
    grad_att = contract(sbranch, out_full, ((1,), (1,))).astype(bf16)
    mlp_grads = jnp.concatenate([grad_down.reshape(4, -1, channels)] + [x[None] for x in ups])
    mlp_grads, grad_att = lax.optimization_barrier((mlp_grads, grad_att, bank_other, *out_second))[:2]
    mlp_grads = lax.psum(mlp_grads, "rows")
    grad_qloc, grad_kall, grad_vall = attend_back(queries, keys_all, values_all, grad_att)
    theirs = jnp.concatenate([grad_kall[pixels:], grad_vall[pixels:]], axis=1)
    theirs = swap_pair(after(theirs, *out_third))
    grad_q = (grad_qloc + (grad_kall[:pixels] + theirs[:, :channels])).astype(bf16)
    grad_v = (grad_vall[:pixels] + theirs[:, channels:]).astype(bf16)
    grad_hidden = grad_self + contract(grad_q, qk_full, ((1,), (1,))) + contract(grad_v, val_full, ((1,), (1,)))
    grad_pre = grad_hidden * jnp.where(pre_act > 0, 1.0, SLOPE)
    grad_conv = (grad_pre * demodulate).astype(bf16)

    with_tokens = jnp.concatenate([grad_conv, token_rows])
    steps = [with_tokens] + [
        lax.ppermute(with_tokens, "rows", [(z, (z + k) % 4) for z in range(4)]) for k in range(1, 4)
    ]
    grad_cols = trade(jnp.transpose(grad_conv.reshape(pixels, 8, slim), (1, 0, 2)))
    conv_all = gather(jnp.stack(lax.optimization_barrier((*steps, grad_cols))[:4])[None], "batch")
    late = exchange(after(jnp.concatenate([grad_q, grad_v], axis=1), grad_cols))
    grad_maps = grad_cols.reshape(held, sides * sides, slim)
    coef_cols = jnp.square(demod_cols) * jnp.sum(grad_maps.astype(f32) * conv_cols, axis=1)
    all_taps = pool_matrix(jnp.arange(9, dtype=jnp.int32), sides)
    shifted = jnp.einsum(
        "tlp,spo->tslo", all_taps, grad_maps, preferred_element_type=f32
    )
    shifted = shifted.astype(bf16).reshape(9, held * lows, slim)
    grad_low = lax.dot_general(
        shifted, bank_cols[0], (((0, 2), (0, 2)), ((), ())), preferred_element_type=f32
    ).reshape(held, lows, channels)
    grad_low_other = lax.dot_general(
        shifted, bank_cols[1], (((0, 2), (0, 2)), ((), ())), preferred_element_type=f32
    ).reshape(held, lows, channels)
    mod_low = own_mod.astype(f32)
    select_taps = jnp.stack(
        [jnp.sum(mod_low * grad_low, axis=(1, 2)), jnp.sum(mod_low * grad_low_other, axis=(1, 2))], axis=1
    )
    low_partial = own_select[:, 0, None, None] * grad_low + own_select[:, 1, None, None] * grad_low_other
    low_parts = trade(low_partial.astype(bf16).reshape(8, lows // 2, channels))
    low_total = jnp.sum(low_parts.astype(f32), axis=0)

    held_back = lax.optimization_barrier((act_low, low_partial, *inward, *out_first, *out_second, *out_third))
    act_low, inward = held_back[0], jnp.stack(held_back[2:6])
    out_first, out_second, out_third = [jnp.stack(held_back[6 + 4 * i : 10 + 4 * i]) for i in range(3)]
    result = product(act_low, down_two).reshape(4, pixels, channels)
    result = (after_cross + member_sum(result)).astype(bf16)
    colour = contract(rgb_full.astype(bf16), result, ((1,), (1,)))
    grad_rgb_w = contract(grad_rgb, result.astype(f32), ((0,), (0,)), HIGH)
    kv_all = out_second[:, pixels:].reshape(held, -1)[:, : grad_kv.size].reshape(held * tokens, 2 * channels)
    grad_context = contract(kv_all[:, :channels], ck_w, ((1,), (1,))) + contract(kv_all[:, channels:], cv_w, ((1,), (1,)))
    grad_context = jnp.take(grad_context.reshape(held, -1), relative, axis=0)
    to_channel = [contract(coef_cols, x, ((1,), (1,)), HIGH) for x in products]
    first_share, other_share = own_select[:, :1], own_select[:, 1:]
    scale_term = -own_scales * (
        first_share * first_share * to_channel[0]
        + 2.0 * first_share * other_share * to_channel[1]
        + other_share * other_share * to_channel[2]
    )
    square_scales = jnp.square(own_scales)
    energy = [jnp.sum(square_scales * x, axis=1, keepdims=True) for x in to_channel]
    select_term = jnp.concatenate(
        [
            first_share * energy[0] + other_share * energy[1],
            first_share * energy[1] + other_share * energy[2],
        ],
        axis=1,
    )
    select_partial = select_taps - select_term

    member_scales = lax.dynamic_index_in_dim(own_scales, pair, 0, keepdims=False)
    feat_own = feat_all.reshape(total * lows, channels)
    feat_own = lax.dynamic_slice_in_dim(feat_own, first * lows + device * (lows // 2), lows // 2, 0).astype(f32)
    grad_input_rows = low_total * member_scales
    square_sum = jnp.sum(jnp.square(grad_input_rows))


    def weight_gradients(pairs):
        parts = [contract(inward[:, pick], right, ((0, 1), (0, 1))) for pick, right in pairs]
        parts = pair_sum(jnp.stack(parts).reshape(len(parts), 2 * slim, channels), 1)
        return parts.astype(bf16)

    grads_three = weight_gradients([(0, out_first), (1, out_second[:, :pixels]), (2, out_third)])
    grad_hidden_sums = jnp.stack([jnp.sum(grad_pre, axis=0), jnp.sum(grad_pre * noise_col, axis=0)])
    singles = jnp.concatenate([select_partial.reshape(-1), square_sum[None], jnp.zeros((127 - 2 * held,), f32)])
    singles = jnp.concatenate([coef_cols.reshape(-1), singles])
    last_sent = jnp.concatenate(
        [
            grad_hidden_sums,
            grad_rgb_w,
            grad_context.reshape(-1, channels),
            jnp.sum(low_total * feat_own, axis=0)[None],
            scale_term,
            jnp.pad(singles, (0, channels - singles.shape[0]))[None],
        ]
    )
    last_all = gather(last_sent[None], "batch")
    col_sums = jnp.sum(lax.dynamic_slice_in_dim(last_all[:, :5], device * slim, slim, 2), axis=0)
    context_grads = jnp.transpose(last_all[:, 5:7].reshape(8, held * tokens, slim), (1, 0, 2)).reshape(held, -1)
    table_cols = class_table.shape[1]
    context_grads = lax.dynamic_slice_in_dim(context_grads, device * table_cols, table_cols, 1)
    grad_scales = jnp.sum(last_all[:, 7].reshape(held, 2, channels), axis=1) + jnp.sum(last_all[:, 8 : 8 + held], axis=0)
    singles = last_all[:, 8 + held]
    coef_plane = jnp.transpose(singles[:, : held * slim].reshape(8, held, slim), (1, 0, 2)).reshape(-1)
    singles = jnp.sum(singles[:, held * slim : held * slim + 128], axis=0)
    pieces = [coef_plane, context_grads.reshape(-1), grad_scales.reshape(-1), col_sums.reshape(-1), grad_upb, singles]
    ends = []
    for x in pieces:
        ends.append(x.shape[0] + (ends[-1] if ends else 0))
    rows_all = gather(jnp.concatenate(pieces).reshape(1, -1, 128), "rows").reshape(4, -1)
    late = jnp.stack(lax.optimization_barrier((*late, last_all))[:4])
    grads_two = weight_gradients([(3, late[:, :, :channels]), (3, late[:, :, channels:])])

    mids = jnp.concatenate([grads_three, grads_two])
    mids = lax.psum(after(mids, mlp_grads), "rows")
    coef = rows_all[:, : ends[0]].reshape(total, channels)
    context_grads = rows_all[:, ends[0] : ends[1]].reshape(total, table_cols)
    grad_scales = rows_all[:, ends[1] : ends[2]].reshape(total, channels)
    rows_total = jnp.sum(rows_all[:, ends[2] : ends[4]], axis=0)
    sum_bias, sum_gain = rows_total[:slim], rows_total[slim : 2 * slim]
    sum_rgb = rows_total[2 * slim : 5 * slim].reshape(3, slim)
    sum_upb = rows_total[5 * slim :]
    singles = rows_all[:, ends[4] :]
    grad_select = singles[:, : 2 * held].reshape(total, 2)
    square_sum = jnp.sum(singles[:, 2 * held])
    classes = class_table.shape[0]
    one_hot = (labels_all[:, None] == jnp.arange(classes)[None, :]).astype(f32)
    sum_table = contract(one_hot, context_grads, over_rows, HIGH)
    entries = float(total * 4 * in_rows * in_cols * channels)
    r1_value = square_sum / entries
    style_f32 = style_own.astype(f32)
    grad_logits = select * (grad_select - jnp.sum(grad_select * select, axis=-1, keepdims=True))
    sum_mod = contract(style_f32, grad_scales, over_rows, HIGH)
    sum_sel = contract(style_f32, grad_logits, over_rows, HIGH)

    first_tap = 2 * (device % 4)
    matrix = pool_matrix(first_tap + jnp.arange(3, dtype=jnp.int32), sides)
    order = (plane - jnp.arange(4, dtype=jnp.int32)) % 4
    shifted_all = pool_samples(order, matrix, conv_all.reshape(4, 2, 4, pixels + 16, channels), pixels)
    kv_every = jnp.transpose(conv_all[::2, :, pixels : pixels + 2 * tokens], (1, 0, 2, 3))
    kv_every = kv_every.reshape(total * tokens, 2 * channels)
    context_every = lax.dynamic_slice_in_dim(after(context_all, low_total).reshape(4, held * tokens, channels), device * slim, slim, 2)
    context_every = jnp.take(context_every, order, axis=0).reshape(total * tokens, slim)
    sum_ck = contract(context_every, kv_every[:, :channels], over_rows)
    sum_cv = contract(context_every, kv_every[:, channels:], over_rows)
    square_all = jnp.square(scales)
    blocks = (device % 4) * 9 + jnp.arange(9, dtype=jnp.int32)
    bank_total = bank_gradient(
        blocks // 4 - first_tap,
        blocks % 4,
        left,
        shifted_all.reshape(3, total * lows, channels),
        kernel_bank,
        bank_other,
        split_terms(own_share * own_share * square_all, True),
        split_terms(own_share * share_other * square_all, True),
        split_terms(coef, False),
    )

    mids, mlp_grads = after(mids, bank_total).astype(f32), after(mlp_grads, low_total).astype(f32)
    sum_down = mlp_grads[:4].reshape(units, channels)
    ordered = [lax.dynamic_index_in_dim(mlp_grads, 4 + (pair ^ c), 0, keepdims=False) for c in range(4)]
    swapped = [jnp.concatenate([x[:, units:], x[:, :units]], axis=1) for x in ordered]
    sum_up = jnp.where(member == 0, jnp.concatenate(ordered, axis=1), jnp.concatenate(swapped, axis=1))
    sum_co, sum_cq, sum_out, sum_qk, sum_val = [mids[i] for i in range(5)]

    feat_out = from_pixels(after(result, rows_all).reshape(2, piece, channels), odd_z, odd_pair)
    feat_out = feat_out.reshape(slots, 2 * in_rows, sides, channels)
    colour_sent = jnp.transpose(colour.reshape(3, 2, piece), (1, 0, 2)).reshape(2, 1, 3 * piece)
    colour_sent = jnp.pad(colour_sent, ((0, 0), (0, 0), (0, channels - 3 * piece)))
    low_sent = jnp.concatenate([grad_input_rows.reshape(2, lows // 4, channels), colour_sent], axis=1)
    low_back = from_pixels(after(low_sent, rows_all), odd_z, odd_pair)
    rgb_out = low_back[:, lows // 4, : 3 * piece].reshape(slots, 3, 2 * in_rows, sides)
    grad_input = low_back[:, : lows // 4].reshape(slots, in_rows, in_cols, channels)
    return (
        feat_out,
        rgb_out,
        grad_input,
        r1_value,
        sum_mod,
        sum_sel,
        bank_total,
        sum_bias,
        sum_gain,
        sum_qk,
        sum_val,
        sum_out,
        sum_cq,
        sum_ck,
        sum_cv,
        sum_co,
        sum_up,
        sum_upb,
        sum_down,
        sum_table,
        sum_rgb,
    )


def solution(mesh):
    split = mesh.shape["batch"] == 8 and mesh.shape["rows"] == 4
    return jax.shard_map(
        by_planes if split else per_device,
        mesh=mesh,
        in_specs=(
            P("batch", "rows", None, None),
            P("batch", None),
            P("batch"),
            P("batch", "rows", None),
            P("batch", "rows", None, None),
            P("batch", None, "rows", None),
            P("batch", None),
            P("batch", None),
            P("batch", None),
            P("batch"),
            P("batch"),
            P("batch", None),
            P("batch", None),
            P("batch", None),
            P("batch", None),
            P("batch", None),
            P("batch", None),
            P("batch", None),
            P("batch", None),
            P("batch"),
            P("batch", None),
            P(None, "batch"),
            P(None, "batch"),
        ),
        out_specs=(
            P("batch", "rows", None, None),
            P("batch", None, "rows", None),
            P("batch", "rows", None, None),
            P(),
            P("batch", None),
            P("batch", None),
            P("batch", None),
            P("batch"),
            P("batch"),
            P("batch", None),
            P("batch", None),
            P("batch", None),
            P("batch", None),
            P("batch", None),
            P("batch", None),
            P("batch", None),
            P("batch", None),
            P("batch"),
            P("batch", None),
            P(None, "batch"),
            P(None, "batch"),
        ),
        check_vma=False,
    )
```

```python
import jax
import jax.numpy as jnp
from jax import lax
from jax.experimental import pallas as pl
from jax.experimental.pallas import tpu as pltpu
from jax.sharding import PartitionSpec as P

HEAD_DIM = 64


HIGH = lax.Precision.HIGHEST
EPSILON = 1e-08
SLOPE = 0.2


def with_halo(cells, sides, width):
    for axis, dim in sides:
        count = lax.axis_size(axis)
        ends = count - 1
        head = lax.slice_in_dim(cells, 0, width, axis=dim)
        tail = lax.slice_in_dim(cells, cells.shape[dim] - width, cells.shape[dim], axis=dim)
        cells = jnp.concatenate(
            [
                lax.ppermute(tail, axis, [(i, (i + 1) % count) for i in range(ends)]),
                cells,
                lax.ppermute(head, axis, [((i + 1) % count, i) for i in range(ends)]),
            ],
            axis=dim,
        )
    return cells


def product(left, right):
    return jnp.dot(left, right, preferred_element_type=jnp.float32)


def kernel_mix(bank_split, select_row):
    mixed_kernel = select_row[0] * bank_split[0].astype(jnp.float32)
    mixed_kernel = mixed_kernel + select_row[1] * bank_split[1].astype(jnp.float32)
    return mixed_kernel


def gather_taps(padded, out_rows, out_cols, flipped):
    pieces = []
    for row_off in range(3):
        for col_off in range(3):
            if flipped:
                pieces.append(
                    padded[
                        :,
                        2 - row_off : 2 - row_off + out_rows,
                        2 - col_off : 2 - col_off + out_cols,
                    ]
                )
            else:
                pieces.append(padded[:, row_off : row_off + out_rows, col_off : col_off + out_cols])
    return jnp.concatenate(pieces, axis=-1)


def per_device(
    feat_in,
    style_vec,
    labels,
    noise_map,
    cot_feat,
    cot_rgb,
    mod_w,
    sel_w,
    kernel_bank,
    conv_bias,
    noise_gain,
    qk_w,
    val_w,
    out_w,
    cq_w,
    ck_w,
    cv_w,
    co_w,
    up_w,
    up_b,
    down_w,
    class_table,
    rgb_w,
):
    f32 = jnp.float32
    bf16 = jnp.bfloat16
    (
        mod_full,
        sel_full,
        bias_full,
        gain_full,
        qk_full,
        val_full,
        out_full,
        cq_full,
        ck_full,
        cv_full,
        co_full,
        up_full,
        upb_full,
        down_full,
        table_full,
        rgb_full,
    ) = (
        lax.all_gather(mod_w, "batch", axis=0, tiled=True),
        lax.all_gather(sel_w, "batch", axis=0, tiled=True),
        lax.all_gather(conv_bias, "batch", axis=0, tiled=True),
        lax.all_gather(noise_gain, "batch", axis=0, tiled=True),
        lax.all_gather(qk_w, "batch", axis=0, tiled=True),
        lax.all_gather(val_w, "batch", axis=0, tiled=True),
        lax.all_gather(out_w, "batch", axis=0, tiled=True),
        lax.all_gather(cq_w, "batch", axis=0, tiled=True),
        lax.all_gather(ck_w, "batch", axis=0, tiled=True),
        lax.all_gather(cv_w, "batch", axis=0, tiled=True),
        lax.all_gather(co_w, "batch", axis=0, tiled=True),
        lax.all_gather(up_w, "batch", axis=0, tiled=True),
        lax.all_gather(up_b, "batch", axis=0, tiled=True),
        lax.all_gather(down_w, "batch", axis=0, tiled=True),
        lax.all_gather(class_table, "batch", axis=1, tiled=True),
        lax.all_gather(rgb_w, "batch", axis=1, tiled=True),
    )
    bank_full = lax.all_gather(kernel_bank, "batch", axis=0, tiled=True)
    samples, in_rows, in_cols, channels = feat_in.shape
    out_rows = 2 * in_rows
    out_cols = 2 * in_cols
    pixels = out_rows * out_cols
    span = 9 * channels
    kernels = bank_full.shape[0] // span
    head_dim = HEAD_DIM
    head_count = channels // head_dim
    bank_split = bank_full.reshape(kernels, span, channels)
    scales = 1.0 + product(style_vec, mod_full)
    select = jax.nn.softmax(product(style_vec, sel_full), axis=-1)
    scale_tiled = jnp.tile(scales, (1, 9))
    upsampled = jnp.repeat(jnp.repeat(feat_in, 2, axis=1), 2, axis=2)
    modulated = (upsampled.astype(f32) * scales[:, None, None, :]).astype(bf16)
    with_rim = with_halo(modulated, (("rows", 1),), 1)
    padded = jnp.pad(with_rim, ((0, 0), (0, 0), (1, 1), (0, 0)))
    patches = gather_taps(padded, out_rows, out_cols, False).reshape(samples, pixels, span)

    def conv_forward(sample_item):
        patch_row, select_row, scale_row = sample_item
        mixed_kernel = kernel_mix(bank_split, select_row)
        demod_row = lax.rsqrt(
            jnp.sum(jnp.square(mixed_kernel * scale_row[:, None]), axis=0) + EPSILON
        )
        return (product(patch_row, mixed_kernel.astype(bf16)), demod_row, mixed_kernel)

    conv_out, demodulate, mixed_all = lax.map(conv_forward, (patches, select, scale_tiled))
    noise_flat = noise_map.reshape(samples, pixels, 1)
    pre_act = (
        conv_out * demodulate[:, None, :]
        + gain_full.astype(f32) * noise_flat
        + bias_full.astype(f32)
    )
    hidden = jnp.where(pre_act > 0, pre_act, SLOPE * pre_act)
    hidden_low = hidden.astype(bf16)
    queries = product(hidden_low, qk_full).astype(bf16)
    values = product(hidden_low, val_full).astype(bf16)
    all_queries, all_values = (
        lax.all_gather(queries, "rows", axis=1, tiled=True),
        lax.all_gather(values, "rows", axis=1, tiled=True),
    )
    query_h = queries.reshape(samples, pixels, head_count, head_dim)
    key_h = all_queries.reshape(samples, -1, head_count, head_dim)
    value_h = all_values.reshape(samples, -1, head_count, head_dim)
    key_f32 = key_h.astype(f32)
    key_norm = jnp.transpose(jnp.sum(jnp.square(key_f32), axis=-1), (0, 2, 1))[:, :, None, :]
    l2_scale = 0.5 * head_dim ** (-0.5)

    def self_scores():
        inner_dots = jnp.einsum("bqhd,bkhd->bhqk", query_h, key_h, preferred_element_type=f32)
        return l2_scale * (2.0 * inner_dots - key_norm)

    scores = self_scores()
    row_max = jnp.max(scores, axis=-1, keepdims=True)
    log_total = row_max + jnp.log(jnp.sum(jnp.exp(scores - row_max), axis=-1, keepdims=True))
    probs_low = jnp.exp(scores - log_total).astype(bf16)
    attended = (
        jnp.einsum("bhqk,bkhd->bqhd", probs_low, value_h, preferred_element_type=f32)
        .reshape(samples, pixels, channels)
        .astype(bf16)
    )
    after_self = hidden + product(attended, out_full)
    self_low = after_self.astype(bf16)
    cross_q = product(self_low, cq_full).astype(bf16).reshape(samples, pixels, head_count, head_dim)
    classes = table_full.shape[0]
    one_hot = (labels[:, None] == jnp.arange(classes)[None, :]).astype(bf16)
    contexts = table_full.shape[1] // channels
    context = product(one_hot, table_full).astype(bf16).reshape(samples, contexts, channels)
    cross_k = jnp.einsum("bjc,cd->bjd", context, ck_full, preferred_element_type=f32).astype(bf16)
    cross_v = jnp.einsum("bjc,cd->bjd", context, cv_full, preferred_element_type=f32).astype(bf16)
    key_cross = cross_k.reshape(samples, contexts, head_count, head_dim)
    value_cross = cross_v.reshape(samples, contexts, head_count, head_dim)
    cross_scale = head_dim ** (-0.5)
    cross_s = (
        jnp.einsum("bqhd,bjhd->bhqj", cross_q, key_cross, preferred_element_type=f32) * cross_scale
    )
    cross_p = jax.nn.softmax(cross_s, axis=-1)
    cross_plow = cross_p.astype(bf16)
    cross_o = (
        jnp.einsum("bhqj,bjhd->bqhd", cross_plow, value_cross, preferred_element_type=f32)
        .reshape(samples, pixels, channels)
        .astype(bf16)
    )
    after_cross = after_self + product(cross_o, co_full)
    cross_low = after_cross.astype(bf16)
    inner = product(cross_low, up_full) + upb_full.astype(f32)
    activated, gelu_pull = jax.vjp(jax.nn.gelu, inner)
    act_low = activated.astype(bf16)
    after_mlp = after_cross + product(act_low, down_full)
    result = after_mlp.astype(bf16)
    colour = product(result, rgb_full.T)
    rgb_out = jnp.transpose(colour, (0, 2, 1)).reshape(samples, 3, out_rows, out_cols)
    grad_rgb = jnp.transpose(cot_rgb.reshape(samples, 3, pixels), (0, 2, 1))
    grad_res = cot_feat.reshape(samples, pixels, channels).astype(f32) + jnp.dot(
        grad_rgb, rgb_full.astype(f32), precision=HIGH
    )
    grad_rgb_w = jnp.einsum("bpk,bpc->kc", grad_rgb, result.astype(f32), precision=HIGH)
    branch = grad_res.astype(bf16)
    grad_down_w = jnp.einsum("bpf,bpc->fc", act_low, branch, preferred_element_type=f32)
    (grad_inner,) = gelu_pull(product(branch, down_full.T))
    inner_low = grad_inner.astype(bf16)
    grad_up_b = jnp.sum(inner_low.astype(f32), axis=(0, 1))
    grad_up_w = jnp.einsum("bpc,bpf->cf", cross_low, inner_low, preferred_element_type=f32)
    grad_cross = grad_res + product(inner_low, up_full.T)
    cbranch = grad_cross.astype(bf16)
    grad_co_w = jnp.einsum("bpc,bpd->cd", cross_o, cbranch, preferred_element_type=f32)
    grad_co = (
        product(cbranch, co_full.T).astype(bf16).reshape(samples, pixels, head_count, head_dim)
    )
    grad_cp = jnp.einsum("bqhd,bjhd->bhqj", grad_co, value_cross, preferred_element_type=f32)
    grad_cv = (
        jnp.einsum("bhqj,bqhd->bjhd", cross_plow, grad_co, preferred_element_type=f32)
        .astype(bf16)
        .reshape(samples, contexts, channels)
    )
    grad_cs = (cross_p * (grad_cp - jnp.sum(grad_cp * cross_p, axis=-1, keepdims=True))).astype(
        bf16
    )
    grad_cq = (
        (
            jnp.einsum("bhqj,bjhd->bqhd", grad_cs, key_cross, preferred_element_type=f32)
            * cross_scale
        )
        .astype(bf16)
        .reshape(samples, pixels, channels)
    )
    grad_ck = (
        (jnp.einsum("bhqj,bqhd->bjhd", grad_cs, cross_q, preferred_element_type=f32) * cross_scale)
        .astype(bf16)
        .reshape(samples, contexts, channels)
    )
    grad_cq_w = jnp.einsum("bpc,bpd->cd", self_low, grad_cq, preferred_element_type=f32)
    grad_ck_w = jnp.einsum("bjc,bjd->cd", context, grad_ck, preferred_element_type=f32)
    grad_cv_w = jnp.einsum("bjc,bjd->cd", context, grad_cv, preferred_element_type=f32)
    grad_context = jnp.einsum(
        "bjd,cd->bjc", grad_ck, ck_full, preferred_element_type=f32
    ) + jnp.einsum("bjd,cd->bjc", grad_cv, cv_full, preferred_element_type=f32)
    grad_table = jnp.dot(
        one_hot.astype(f32).T, grad_context.reshape(samples, contexts * channels), precision=HIGH
    )
    grad_self = grad_cross + product(grad_cq, cq_full.T)
    sbranch = grad_self.astype(bf16)
    grad_out_w = jnp.einsum("bpc,bpd->cd", attended, sbranch, preferred_element_type=f32)
    grad_att = (
        product(sbranch, out_full.T).astype(bf16).reshape(samples, pixels, head_count, head_dim)
    )
    probs = jnp.exp(self_scores() - log_total)
    probs_again = probs.astype(bf16)
    grad_probs = jnp.einsum("bqhd,bkhd->bhqk", grad_att, value_h, preferred_element_type=f32)
    grad_vall = jnp.einsum("bhqk,bqhd->bkhd", probs_again, grad_att, preferred_element_type=f32)
    grad_s = (probs * (grad_probs - jnp.sum(grad_probs * probs, axis=-1, keepdims=True))).astype(
        bf16
    )
    grad_qloc = (
        2.0 * l2_scale * jnp.einsum("bhqk,bkhd->bqhd", grad_s, key_h, preferred_element_type=f32)
    )
    col_total = jnp.transpose(jnp.sum(grad_s.astype(f32), axis=2), (0, 2, 1))[:, :, :, None]
    grad_kall = (
        2.0
        * l2_scale
        * (
            jnp.einsum("bhqk,bqhd->bkhd", grad_s, query_h, preferred_element_type=f32)
            - key_f32 * col_total
        )
    )
    back_keys, back_values = (
        lax.psum_scatter(
            grad_kall.reshape(samples, -1, channels).astype(jnp.bfloat16),
            "rows",
            scatter_dimension=1,
            tiled=True,
        ).astype(jnp.float32),
        lax.psum_scatter(
            grad_vall.reshape(samples, -1, channels).astype(jnp.bfloat16),
            "rows",
            scatter_dimension=1,
            tiled=True,
        ).astype(jnp.float32),
    )
    grad_q = (grad_qloc.reshape(samples, pixels, channels) + back_keys).astype(bf16)
    grad_v = back_values.astype(bf16)
    grad_qk_w = jnp.einsum("bpc,bpd->cd", hidden_low, grad_q, preferred_element_type=f32)
    grad_val_w = jnp.einsum("bpc,bpd->cd", hidden_low, grad_v, preferred_element_type=f32)
    grad_hidden = grad_self + product(grad_q, qk_full.T) + product(grad_v, val_full.T)
    grad_pre = grad_hidden * jnp.where(pre_act > 0, 1.0, SLOPE)
    grad_gain = jnp.sum(grad_pre * noise_flat, axis=(0, 1))
    grad_bias = jnp.sum(grad_pre, axis=(0, 1))
    grad_demod = jnp.sum(grad_pre * conv_out, axis=1)
    demod_coef = demodulate**3 * grad_demod
    grad_conv = (grad_pre * demodulate[:, None, :]).astype(bf16)
    grad_rim = with_halo(
        grad_conv.reshape(samples, out_rows, out_cols, channels), (("rows", 1),), 1
    )
    grad_pad = jnp.pad(grad_rim, ((0, 0), (0, 0), (1, 1), (0, 0)))
    grad_patches = gather_taps(grad_pad, out_rows, out_cols, True).reshape(samples, pixels, span)

    def conv_backward(sample_item):
        gpatch_row, mixed_kernel, scale_row, coef_row = sample_item
        taps_low = mixed_kernel.astype(bf16).reshape(9, channels, channels)
        grad_mod = jnp.einsum(
            "pto,tio->pi",
            gpatch_row.reshape(pixels, 9, channels),
            taps_low,
            preferred_element_type=f32,
        )
        scale_term = -scale_row[:channels] * jnp.sum(
            (jnp.square(mixed_kernel) * coef_row[None, :]).reshape(9, channels, channels),
            axis=(0, 2),
        )
        return (grad_mod, scale_term)

    grad_mod, scale_term = lax.map(
        conv_backward, (grad_patches, mixed_all, scale_tiled, demod_coef)
    )
    block_rows = span // 8

    def tap_block(index, carry):
        bank_acc, select_acc = carry
        tap_row = index * block_rows
        patch_cols = lax.dynamic_slice_in_dim(patches, tap_row, block_rows, 2)
        grad_taps = jnp.einsum("bpt,bpo->bto", patch_cols, grad_conv, preferred_element_type=f32)
        bank_rows = lax.dynamic_slice_in_dim(bank_split, tap_row, block_rows, 1).astype(f32)
        mixed_rows = lax.dynamic_slice_in_dim(mixed_all, tap_row, block_rows, 1)
        scale_rows = lax.dynamic_slice_in_dim(scale_tiled, tap_row, block_rows, 1)
        grad_mixed = (
            grad_taps - mixed_rows * jnp.square(scale_rows)[:, :, None] * demod_coef[:, None, :]
        )
        select_acc = select_acc + jnp.einsum("kto,bto->bk", bank_rows, grad_mixed, precision=HIGH)
        bank_piece = jnp.einsum("bk,bto->kto", select, grad_mixed, precision=HIGH)
        bank_acc = lax.dynamic_update_slice_in_dim(bank_acc, bank_piece, tap_row, 1)
        return (bank_acc, select_acc)

    bank_acc, grad_select = lax.fori_loop(
        0,
        8,
        tap_block,
        (jnp.zeros((kernels, span, channels), f32), jnp.zeros((samples, kernels), f32)),
    )
    bank_flat = bank_acc.reshape(kernels * span, channels)
    grad_mod = grad_mod.reshape(samples, out_rows, out_cols, channels)
    grad_scales = jnp.sum(grad_mod * upsampled.astype(f32), axis=(1, 2)) + scale_term
    grad_up = grad_mod * scales[:, None, None, :]
    grad_input = grad_up.reshape(samples, in_rows, 2, in_cols, 2, channels).sum(axis=(2, 4))
    grad_logits = select * (grad_select - jnp.sum(grad_select * select, axis=-1, keepdims=True))
    style_f32 = style_vec.astype(f32)
    grad_mod_w = jnp.dot(style_f32.T, grad_scales, precision=HIGH)
    grad_sel_w = jnp.dot(style_f32.T, grad_logits, precision=HIGH)
    (
        sum_mod,
        sum_sel,
        sum_bias,
        sum_gain,
        sum_qk,
        sum_val,
        sum_out,
        sum_cq,
        sum_ck,
        sum_cv,
        sum_co,
        sum_up,
        sum_upb,
        sum_down,
        sum_table,
        sum_rgb,
    ) = (
        lax.psum_scatter(grad_mod_w, "batch", scatter_dimension=0, tiled=True),
        lax.psum_scatter(grad_sel_w, "batch", scatter_dimension=0, tiled=True),
        lax.psum_scatter(grad_bias, "batch", scatter_dimension=0, tiled=True),
        lax.psum_scatter(grad_gain, "batch", scatter_dimension=0, tiled=True),
        lax.psum_scatter(grad_qk_w, "batch", scatter_dimension=0, tiled=True),
        lax.psum_scatter(grad_val_w, "batch", scatter_dimension=0, tiled=True),
        lax.psum_scatter(grad_out_w, "batch", scatter_dimension=0, tiled=True),
        lax.psum_scatter(grad_cq_w, "batch", scatter_dimension=0, tiled=True),
        lax.psum_scatter(grad_ck_w, "batch", scatter_dimension=0, tiled=True),
        lax.psum_scatter(grad_cv_w, "batch", scatter_dimension=0, tiled=True),
        lax.psum_scatter(grad_co_w, "batch", scatter_dimension=0, tiled=True),
        lax.psum_scatter(grad_up_w, "batch", scatter_dimension=0, tiled=True),
        lax.psum_scatter(grad_up_b, "batch", scatter_dimension=0, tiled=True),
        lax.psum_scatter(grad_down_w, "batch", scatter_dimension=0, tiled=True),
        lax.psum_scatter(grad_table, "batch", scatter_dimension=1, tiled=True),
        lax.psum_scatter(grad_rgb_w, "batch", scatter_dimension=1, tiled=True),
    )
    bank_part = lax.psum_scatter(bank_flat, "batch", scatter_dimension=0, tiled=True)
    (
        sum_mod,
        sum_sel,
        sum_bias,
        sum_gain,
        sum_qk,
        sum_val,
        sum_out,
        sum_cq,
        sum_ck,
        sum_cv,
        sum_co,
        sum_up,
        sum_upb,
        sum_down,
        sum_table,
        sum_rgb,
        bank_total,
    ) = (
        lax.psum(sum_mod.astype(jnp.bfloat16), "rows").astype(jnp.float32),
        lax.psum(sum_sel.astype(jnp.bfloat16), "rows").astype(jnp.float32),
        lax.psum(sum_bias.astype(jnp.bfloat16), "rows").astype(jnp.float32),
        lax.psum(sum_gain.astype(jnp.bfloat16), "rows").astype(jnp.float32),
        lax.psum(sum_qk.astype(jnp.bfloat16), "rows").astype(jnp.float32),
        lax.psum(sum_val.astype(jnp.bfloat16), "rows").astype(jnp.float32),
        lax.psum(sum_out.astype(jnp.bfloat16), "rows").astype(jnp.float32),
        lax.psum(sum_cq.astype(jnp.bfloat16), "rows").astype(jnp.float32),
        lax.psum(sum_ck.astype(jnp.bfloat16), "rows").astype(jnp.float32),
        lax.psum(sum_cv.astype(jnp.bfloat16), "rows").astype(jnp.float32),
        lax.psum(sum_co.astype(jnp.bfloat16), "rows").astype(jnp.float32),
        lax.psum(sum_up.astype(jnp.bfloat16), "rows").astype(jnp.float32),
        lax.psum(sum_upb.astype(jnp.bfloat16), "rows").astype(jnp.float32),
        lax.psum(sum_down.astype(jnp.bfloat16), "rows").astype(jnp.float32),
        lax.psum(sum_table.astype(jnp.bfloat16), "rows").astype(jnp.float32),
        lax.psum(sum_rgb.astype(jnp.bfloat16), "rows").astype(jnp.float32),
        lax.psum(bank_part.astype(jnp.bfloat16), "rows").astype(jnp.float32),
    )
    entry_count = float(
        samples * lax.axis_size("batch") * in_rows * lax.axis_size("rows") * in_cols * channels
    )
    r1_value = lax.psum(jnp.sum(jnp.square(grad_input)), ("batch", "rows")) / entry_count
    feat_out = result.reshape(samples, out_rows, out_cols, channels)
    return (
        feat_out,
        rgb_out,
        grad_input,
        r1_value,
        sum_mod,
        sum_sel,
        bank_total,
        sum_bias,
        sum_gain,
        sum_qk,
        sum_val,
        sum_out,
        sum_cq,
        sum_ck,
        sum_cv,
        sum_co,
        sum_up,
        sum_upb,
        sum_down,
        sum_table,
        sum_rgb,
    )


def gather(x, axis_name, axis=0):
    return lax.all_gather(x, axis_name, axis=axis, tiled=True)


def trade(x):
    return lax.all_to_all(x, "batch", 0, 0, tiled=True)


def to_pair(x, step):
    return lax.ppermute(x, "batch", [(i, i ^ (2 * step)) for i in range(8)])


def spread(x):
    return jnp.concatenate([x] + [to_pair(x, step) for step in range(1, 4)])


def exchange(x):
    return [x] + [to_pair(x, step) for step in range(1, 4)]


def member_sum(parts):
    total = parts[0].astype(jnp.float32)
    for step in range(1, 4):
        total = total + to_pair(parts[step].astype(jnp.bfloat16), step).astype(jnp.float32)
    return total


def after(x, *earlier):
    return lax.optimization_barrier((x,) + earlier)[0]


def behind(x, earlier):
    nothing = jnp.minimum(jnp.abs(earlier[(0,) * earlier.ndim].astype(jnp.float32)), 0.0)
    return x + nothing.astype(x.dtype)


def swap_pair(x):
    return lax.ppermute(x, "batch", [(i, i ^ 1) for i in range(8)])


def move_table(turn):
    table = []
    for d in range(8):
        for z in range(4):
            slot = (z % 2) ^ turn
            pair = 2 * (d % 2) + slot
            table.append((4 * d + z, 4 * (2 * pair + z // 2) + d // 2))
    return table


def to_pixels(x, odd_z, odd_pair):
    sent = jnp.where(odd_z, x[::-1], x)
    first = lax.ppermute(sent[0], ("batch", "rows"), move_table(0))
    second = lax.ppermute(sent[1], ("batch", "rows"), move_table(1))
    return jnp.where(odd_pair, jnp.stack([second, first]), jnp.stack([first, second]))


def from_pixels(x, odd_z, odd_pair):
    sent = jnp.where(odd_pair, x[::-1], x)
    back = [[(b, a) for a, b in move_table(turn)] for turn in range(2)]
    first = lax.ppermute(sent[0], ("batch", "rows"), back[0])
    second = lax.ppermute(sent[1], ("batch", "rows"), back[1])
    return jnp.where(odd_z, jnp.stack([second, first]), jnp.stack([first, second]))


def contract(left, right, dims, precision=None):
    return lax.dot_general(
        left, right, (dims, ((), ())), precision=precision, preferred_element_type=jnp.float32
    )


def conv_kernel(
    select_ref, patch_ref, bank_ref, scale_ref, out_ref, square_ref, product_ref, acc_ref, sum_ref
):
    col, row = pl.program_id(0), pl.program_id(1)
    start = jnp.logical_and(col == 0, row == 0)
    last = jnp.logical_and(col == 2, row == 2)

    @pl.when(start)
    def _():
        acc_ref[...] = jnp.zeros_like(acc_ref)
        sum_ref[...] = jnp.zeros_like(sum_ref)
        product_ref[...] = jnp.zeros_like(product_ref)

    first = bank_ref[0, 0].astype(jnp.float32)
    second = bank_ref[1, 0].astype(jnp.float32)
    product_ref[0] += first * first
    product_ref[1] += first * second
    product_ref[2] += second * second
    for b in range(4):
        mixed = select_ref[b, 0] * first + select_ref[b, 1] * second
        scaled = mixed * scale_ref[b]
        sum_ref[b] += jnp.sum(jnp.square(scaled).reshape(-1, 8, 128), axis=0)
        begin = pl.multiple_of(row * 16, 16)
        left = patch_ref[b, 0, pl.ds(begin, 256), :]
        acc_ref[b] += jnp.dot(left, mixed.astype(jnp.bfloat16), preferred_element_type=jnp.float32)

    @pl.when(last)
    def _():
        out_ref[...] = acc_ref[...]
        square_ref[...] = sum_ref[...]


def conv_forward_plane(select, patch_cols, bank_cols, scale_cols):
    samples, _, _, width = patch_cols.shape
    cols = bank_cols.shape[-1]
    f32 = jnp.float32
    return pl.pallas_call(
        conv_kernel,
        grid=(3, 3),
        in_specs=[
            pl.BlockSpec(memory_space=pltpu.SMEM),
            pl.BlockSpec((samples, 1, 288, width), lambda c, a: (0, c, 0, 0)),
            pl.BlockSpec((2, 1, width, cols), lambda c, a: (0, 3 * a + c, 0, 0)),
            pl.BlockSpec((samples, width, cols), lambda c, a: (0, 0, 0)),
        ],
        out_specs=[
            pl.BlockSpec((samples, 256, cols), lambda c, a: (0, 0, 0)),
            pl.BlockSpec((samples, 8, cols), lambda c, a: (0, 0, 0)),
            pl.BlockSpec((3, width, cols), lambda c, a: (0, 0, 0)),
        ],
        out_shape=[
            jax.ShapeDtypeStruct((samples, 256, cols), f32),
            jax.ShapeDtypeStruct((samples, 8, cols), f32),
            jax.ShapeDtypeStruct((3, width, cols), f32),
        ],
        scratch_shapes=[
            pltpu.VMEM((samples, 256, cols), f32),
            pltpu.VMEM((samples, 8, cols), f32),
        ],
        compiler_params=pltpu.CompilerParams(vmem_limit_bytes=40 << 20),
        cost_estimate=pl.CostEstimate(
            flops=2 * samples * 256 * 9 * width * cols, bytes_accessed=20 << 20, transcendentals=0
        ),
        name="conv_plane",
    )(select, patch_cols, bank_cols, scale_cols)


def head_scores(query, key):
    squares = jnp.square(key.astype(jnp.float32))
    upper = squares.astype(jnp.bfloat16)
    lower = (squares - upper.astype(jnp.float32)).astype(jnp.bfloat16)
    ones = jnp.ones((8, HEAD_DIM), jnp.bfloat16)
    over_last = ((1,), (1,))
    norms = contract(ones, upper, over_last) + contract(ones, lower, over_last)
    scale = 0.5 * HEAD_DIM ** (-0.5)
    return scale * (2.0 * contract(query, key, over_last) - norms[0:1])


def head_softmax(scores):
    raised = jnp.exp(scores - jnp.max(scores, axis=-1, keepdims=True))
    return raised * (1.0 / jnp.sum(raised, axis=-1, keepdims=True))


def attend_kernel(query_ref, key_ref, value_ref, out_ref):
    for h in range(query_ref.shape[1] // HEAD_DIM):
        part = slice(h * HEAD_DIM, (h + 1) * HEAD_DIM)
        probs = head_softmax(head_scores(query_ref[:, part], key_ref[:, part]))
        out_ref[:, part] = jnp.dot(
            probs.astype(jnp.bfloat16), value_ref[:, part], preferred_element_type=jnp.float32
        ).astype(jnp.bfloat16)


def attend(query, key, value):
    pixels, width = query.shape
    everything = key.shape[0]
    pair = 4 * HEAD_DIM
    return pl.pallas_call(
        attend_kernel,
        grid=(width // pair,),
        in_specs=[
            pl.BlockSpec((pixels, pair), lambda i: (0, i)),
            pl.BlockSpec((everything, pair), lambda i: (0, i)),
            pl.BlockSpec((everything, pair), lambda i: (0, i)),
        ],
        out_specs=pl.BlockSpec((pixels, pair), lambda i: (0, i)),
        out_shape=jax.ShapeDtypeStruct((pixels, width), jnp.bfloat16),
        cost_estimate=pl.CostEstimate(
            flops=4 * pixels * everything * width, bytes_accessed=3 << 20, transcendentals=1 << 19
        ),
        name="attend",
    )(query, key, value)


def attend_back_kernel(query_ref, key_ref, value_ref, grad_ref, gq_ref, gk_ref, gv_ref):
    bf16 = jnp.bfloat16
    twice = 2.0 * (0.5 * HEAD_DIM ** (-0.5))
    for h in range(query_ref.shape[1] // HEAD_DIM):
        part = slice(h * HEAD_DIM, (h + 1) * HEAD_DIM)
        query, key, value, grad = query_ref[:, part], key_ref[:, part], value_ref[:, part], grad_ref[:, part]
        probs = head_softmax(head_scores(query, key))
        grad_probs = contract(grad, value, ((1,), (1,)))
        mean = jnp.sum(grad_probs * probs, axis=-1, keepdims=True)
        grad_s = (probs * (grad_probs - mean)).astype(bf16)
        gv_ref[:, part] = contract(probs.astype(bf16), grad, ((0,), (0,)))
        gq_ref[:, part] = twice * jnp.dot(grad_s, key, preferred_element_type=jnp.float32)
        both = jnp.concatenate([query, jnp.ones_like(query)], axis=1)
        sums = contract(grad_s, both, ((0,), (0,)))
        gk_ref[:, part] = twice * (
            sums[:, :HEAD_DIM] - key.astype(jnp.float32) * sums[:, HEAD_DIM:]
        )


def attend_back(query, key, value, grad):
    pixels, width = query.shape
    everything = key.shape[0]
    pair = 4 * HEAD_DIM
    few = pl.BlockSpec((pixels, pair), lambda i: (0, i))
    many = pl.BlockSpec((everything, pair), lambda i: (0, i))
    f32 = jnp.float32
    return pl.pallas_call(
        attend_back_kernel,
        grid=(width // pair,),
        in_specs=[few, many, many, few],
        out_specs=[few, many, many],
        out_shape=[
            jax.ShapeDtypeStruct((pixels, width), f32),
            jax.ShapeDtypeStruct((everything, width), f32),
            jax.ShapeDtypeStruct((everything, width), f32),
        ],
        cost_estimate=pl.CostEstimate(
            flops=14 * pixels * everything * width, bytes_accessed=5 << 20, transcendentals=1 << 19
        ),
        name="attend_back",
    )(query, key, value, grad)


def split_terms(x, left):
    upper = x.astype(jnp.bfloat16)
    lower = (x - upper.astype(jnp.float32)).astype(jnp.bfloat16)
    return jnp.concatenate([upper, upper, lower] if left else [upper, lower, upper])


def bank_kernel(tap_ref, part_ref, left_ref, right_ref, own_ref, other_ref, same_ref, cross_ref, coef_ref, out_ref):
    del tap_ref, part_ref
    first = ((0,), (0,))
    out_ref[...] = (
        jnp.dot(left_ref[...], right_ref[0], preferred_element_type=jnp.float32)
        - own_ref[...].astype(jnp.float32) * contract(same_ref[...], coef_ref[...], first)
        - other_ref[...].astype(jnp.float32) * contract(cross_ref[...], coef_ref[...], first)
    )


def bank_gradient(taps, parts, left, right, own, other, same, cross, coef):
    lows = left.shape[1]
    count = taps.shape[0]
    rows = own.shape[0] // count
    out_cols = own.shape[1]
    terms = coef.shape[0]
    return pl.pallas_call(
        bank_kernel,
        grid_spec=pltpu.PrefetchScalarGridSpec(
            num_scalar_prefetch=2,
            grid=(count,),
            in_specs=[
                pl.BlockSpec((rows, lows), lambda m, t, q: (q[m], 0)),
                pl.BlockSpec((1, lows, out_cols), lambda m, t, q: (t[m], 0, 0)),
                pl.BlockSpec((rows, out_cols), lambda m, t, q: (m, 0)),
                pl.BlockSpec((rows, out_cols), lambda m, t, q: (m, 0)),
                pl.BlockSpec((terms, rows), lambda m, t, q: (0, q[m])),
                pl.BlockSpec((terms, rows), lambda m, t, q: (0, q[m])),
                pl.BlockSpec((terms, out_cols), lambda m, t, q: (0, 0)),
            ],
            out_specs=pl.BlockSpec((rows, out_cols), lambda m, t, q: (m, 0)),
        ),
        out_shape=jax.ShapeDtypeStruct((own.shape[0], out_cols), jnp.float32),
        compiler_params=pltpu.CompilerParams(vmem_limit_bytes=40 << 20),
        cost_estimate=pl.CostEstimate(
            flops=2 * lows * own.shape[0] * out_cols, bytes_accessed=32 << 20, transcendentals=0
        ),
        name="bank_gradient",
    )(taps, parts, left, right, own, other, same, cross, coef)


def pool_matrix(taps, side):
    half = side // 2
    shape = (taps.shape[0], half * half, side * side)
    block = lax.broadcasted_iota(jnp.int32, shape, 1)
    pixel = lax.broadcasted_iota(jnp.int32, shape, 2)
    tap = taps[:, None, None]
    row = pixel // side + tap // 3 - 1 - 2 * (block // half)
    col = pixel % side + tap % 3 - 1 - 2 * (block % half)
    inside = (row >= 0) & (row < 2) & (col >= 0) & (col < 2)
    return inside.astype(jnp.bfloat16)


def patch_matrix(low):
    side = 2 * low
    shape = (3 * (side + 2) * side, low * low)
    place = lax.broadcasted_iota(jnp.int32, shape, 0)
    source = lax.broadcasted_iota(jnp.int32, shape, 1)
    offset, place = place // ((side + 2) * side), place % ((side + 2) * side)
    row, col = place // side - 1, place % side + offset - 1
    inside = (row >= 0) & (row < side) & (col >= 0) & (col < side)
    return (inside & (source == (row // 2) * low + col // 2)).astype(jnp.bfloat16)


def pool_kernel(order_ref, matrix_ref, map_ref, out_ref):
    del order_ref
    pixels = matrix_ref.shape[1]
    taps, _, lows, width = out_ref.shape
    grid = map_ref[...].reshape(pixels, width)
    pooled = jnp.dot(matrix_ref[...], grid, preferred_element_type=jnp.float32)
    out_ref[...] = pooled.astype(jnp.bfloat16).reshape(taps, 1, lows, width)


def pool_samples(order, matrix, maps, piece):
    taps, lows, pixels = matrix.shape
    pairs, members, steps, _, width = maps.shape
    return pl.pallas_call(
        pool_kernel,
        grid_spec=pltpu.PrefetchScalarGridSpec(
            num_scalar_prefetch=1,
            grid=(steps, pairs),
            in_specs=[
                pl.BlockSpec((taps * lows, pixels), lambda k, c, o: (0, 0)),
                pl.BlockSpec((1, members, 1, piece, width), lambda k, c, o: (c, 0, k, 0, 0)),
            ],
            out_specs=pl.BlockSpec((taps, 1, lows, width), lambda k, c, o: (0, o[k] * pairs + c, 0, 0)),
        ),
        out_shape=jax.ShapeDtypeStruct((taps, steps * pairs, lows, width), jnp.bfloat16),
        compiler_params=pltpu.CompilerParams(vmem_limit_bytes=40 << 20),
        cost_estimate=pl.CostEstimate(
            flops=2 * taps * lows * pixels * width * steps * pairs, bytes_accessed=14 << 20, transcendentals=0
        ),
        name="pool_samples",
    )(order, matrix.reshape(taps * lows, pixels), maps)


def by_planes(
    feat_in,
    style_vec,
    labels,
    noise_map,
    cot_feat,
    cot_rgb,
    mod_w,
    sel_w,
    kernel_bank,
    conv_bias,
    noise_gain,
    qk_w,
    val_w,
    out_w,
    cq_w,
    ck_w,
    cv_w,
    co_w,
    up_w,
    up_b,
    down_w,
    class_table,
    rgb_w,
):
    f32, bf16 = jnp.float32, jnp.bfloat16
    device, plane = lax.axis_index("batch"), lax.axis_index("rows")
    pair, member = device // 2, device % 2
    odd_z, odd_pair = plane % 2 == 1, pair % 2 == 1
    slots, in_rows, in_cols, channels = feat_in.shape
    total = 8 * slots
    held = total // 4
    piece = 2 * in_rows * 2 * in_cols
    pixels = 2 * piece
    lows = 4 * in_rows * in_cols
    style_width = style_vec.shape[1]
    own_style = style_width // 8
    slim = channels // 8
    head_count = channels // HEAD_DIM

    point_maps = jnp.concatenate(
        [noise_map.reshape(slots, 1, piece), cot_rgb.reshape(slots, 3, piece)], axis=1
    )
    point_maps = to_pixels(point_maps, odd_z, odd_pair)
    point_cols = jnp.transpose(point_maps, (0, 2, 1)).reshape(pixels, 4)
    noise_col, grad_rgb = point_cols[:, :1], point_cols[:, 1:]

    packed = jnp.concatenate(
        [
            feat_in.reshape(-1, 128),
            style_vec.reshape(-1, 128),
            conv_bias.reshape(-1, 128),
            noise_gain.reshape(-1, 128),
            rgb_w.reshape(-1, 128),
            jnp.pad(jnp.stack([labels // 32, labels % 32]).astype(bf16), ((0, 0), (0, 128 - slots))),
        ]
    )
    bank_sent = jnp.transpose(kernel_bank.reshape(-1, 8, slim), (1, 0, 2))
    smalls = gather(after(packed, bank_sent, point_cols)[None], "batch")
    feat_rows = feat_in.size // 128
    style_rows = style_vec.size // 128
    at = feat_rows + style_rows
    feat_part = smalls[:, :feat_rows].reshape(total, in_rows * in_cols, channels)
    style_all = smalls[:, feat_rows:at].reshape(total, style_width)
    bias_full = smalls[:, at].astype(f32).reshape(channels)
    gain_full = smalls[:, at + 1].astype(f32).reshape(channels)
    rgb_full = jnp.transpose(smalls[:, at + 2 : at + 5], (1, 0, 2)).astype(f32).reshape(3, channels)
    label_parts = smalls[:, at + 5 : at + 7, :slots].astype(jnp.int32)
    labels_all = (32 * label_parts[:, 0] + label_parts[:, 1]).reshape(total)

    style_own = lax.dynamic_slice_in_dim(style_all, device * own_style, own_style, 1)
    context_own = jnp.take(class_table, labels_all, axis=0)
    partial_styles = jnp.concatenate(
        [
            product(style_own, mod_w),
            jnp.pad(product(style_own, sel_w), ((0, 0), (0, 126))),
            context_own.astype(f32),
        ],
        axis=1,
    )
    styles = gather(partial_styles[None], "batch")
    sums = jnp.sum(styles[:, :, : channels + 128], axis=0)
    scales = 1.0 + sums[:, :channels]
    select = jax.nn.softmax(sums[:, channels : channels + 2], axis=-1)
    context_all = jnp.transpose(styles[:, :, channels + 128 :], (1, 0, 2)).reshape(total, -1).astype(bf16)
    feat_all = gather(feat_part[None], "rows")
    feat_all = jnp.transpose(feat_all, (1, 0, 2, 3)).reshape(total, lows, channels)

    kernels = 2
    bank_cols = trade(after(bank_sent, styles)).reshape(kernels, 9, channels, slim)

    squares = jnp.stack(lax.optimization_barrier((qk_w, val_w, out_w, cq_w, co_w, styles))[:5])
    weights = gather(squares, "batch", 1)
    qk_full, val_full, out_full, cq_full, co_full = [weights[i] for i in range(5)]


    first = held * plane
    tokens = context_all.shape[1] // channels
    modulated = (feat_all.astype(f32) * scales[:, None, :]).astype(bf16)
    own_mod = lax.dynamic_slice_in_dim(modulated, first, held, 0)
    own_scales = lax.dynamic_slice_in_dim(scales, first, held, 0)
    own_select = lax.dynamic_slice_in_dim(select, first, held, 0)
    sides = 2 * in_cols
    patch_cols = jnp.einsum(
        "srl,slc->src",
        jnp.broadcast_to(patch_matrix(in_cols)[None], (held, 3 * (sides + 2) * sides, lows)),
        own_mod,
        preferred_element_type=f32,
    )
    patch_cols = patch_cols.astype(bf16).reshape(held, 3, (sides + 2) * sides, channels)
    kernel_id = device // 4
    own_share = lax.dynamic_index_in_dim(select, kernel_id, 1)
    share_other = lax.dynamic_index_in_dim(select, 1 - kernel_id, 1)
    left = (own_share[:, :, None] * modulated.astype(f32)).astype(bf16)
    left = jnp.transpose(left.reshape(total * lows, channels))
    scale_cols = jnp.broadcast_to(own_scales[:, :, None], (held, channels, slim))
    own_context = lax.dynamic_slice_in_dim(context_all, first, held, 0).reshape(held * tokens, channels)
    context_cols = lax.dynamic_slice_in_dim(own_context, device * slim, slim, 1)
    cross_partial = product(context_cols, jnp.concatenate([ck_w, cv_w], axis=1)).reshape(held, -1, slim)
    cross_partial = jnp.repeat(cross_partial, 2, axis=0)
    bank_cols, patch_cols, left, scale_cols, cross_partial = lax.optimization_barrier(
        (bank_cols, patch_cols, left, scale_cols, cross_partial)
    )

    conv_cols, square_cols, products = conv_forward_plane(own_select, patch_cols, bank_cols, scale_cols)

    demod_cols = lax.rsqrt(jnp.sum(square_cols, axis=1) + EPSILON)
    extra = jnp.broadcast_to(jnp.repeat(demod_cols, 2, axis=0)[:, None, :], (8, 8, slim))
    sent = jnp.concatenate([conv_cols.reshape(8, pixels, slim), extra, cross_partial], axis=1)
    back = trade(sent)
    cross_kv = jnp.sum(back[:, pixels + 8 :], axis=0).reshape(tokens, 2 * channels).astype(bf16)
    back = jnp.transpose(back[:, : pixels + 8], (1, 0, 2)).reshape(pixels + 8, channels)
    conv_out, demodulate = back[:pixels], back[pixels]

    pre_act = conv_out * demodulate + gain_full * noise_col + bias_full
    hidden = jnp.where(pre_act > 0, pre_act, SLOPE * pre_act)
    hidden_low = hidden.astype(bf16)

    queries = product(hidden_low, qk_full).astype(bf16)
    values = product(hidden_low, val_full).astype(bf16)
    quarter = kernel_bank.shape[0] // 4
    bank_quarter = lax.dynamic_slice_in_dim(kernel_bank, plane * quarter, quarter, 0)
    across = [[i, i + 4] for i in range(4)]
    bank_quarter = lax.all_gather(after(bank_quarter, queries), "batch", axis_index_groups=across)
    bank_quarter = lax.dynamic_index_in_dim(bank_quarter, 1 - device // 4, 0, keepdims=False)
    up_sent = jnp.transpose(up_w.reshape(slim, 8, -1), (1, 0, 2))
    up_cols = trade(after(up_sent, queries)).reshape(channels, -1)
    units = up_cols.shape[1]
    up_two = jnp.concatenate([up_cols, swap_pair(up_cols)], axis=1)
    down_two = jnp.concatenate([down_w, swap_pair(after(down_w, queries))])
    bias_two = jnp.concatenate([up_b, swap_pair(after(up_b, queries))]).astype(f32)
    theirs = swap_pair(jnp.concatenate([queries, values], axis=1))
    keys_all = jnp.concatenate([queries, theirs[:, :channels]])
    values_all = jnp.concatenate([values, theirs[:, channels:]])
    cot_sent = after(cot_feat, queries).reshape(slots, piece, channels)
    cot_pixels = to_pixels(cot_sent, odd_z, odd_pair).reshape(pixels, channels)
    attended = attend(queries, keys_all, values_all)
    grad_res = after(cot_pixels, attended).astype(f32) + jnp.dot(grad_rgb, rgb_full, precision=HIGH)
    branch = grad_res.astype(bf16)
    branch_rows = spread(branch)
    after_self = hidden + product(attended, out_full)
    self_low = after_self.astype(bf16)

    in_head = (jnp.arange(channels)[None, :] // HEAD_DIM == jnp.arange(head_count)[:, None])[None]

    def by_head(rows):
        return jnp.where(in_head, rows[:, None, :], 0).astype(bf16).reshape(tokens * head_count, channels)

    key_blocks, value_blocks = by_head(cross_kv[:, :channels]), by_head(cross_kv[:, channels:])
    cross_scale = HEAD_DIM ** (-0.5)
    cross_q = product(self_low, cq_full).astype(bf16)

    def per_token(x):
        return [x[:, i * head_count : (i + 1) * head_count] for i in range(tokens)]

    cross_s = per_token(contract(cross_q, key_blocks, ((1,), (1,))) * cross_scale)
    top = jnp.maximum(jnp.maximum(cross_s[0], cross_s[1]), jnp.maximum(cross_s[2], cross_s[3]))
    raised = [jnp.exp(x - top) for x in cross_s]
    whole = raised[0] + raised[1] + raised[2] + raised[3]
    cross_p = [x / whole for x in raised]
    cross_plow = jnp.concatenate(cross_p, axis=1).astype(bf16)
    cross_o = product(cross_plow, value_blocks).astype(bf16)
    cross_o = after(cross_o, up_two, down_two, branch_rows)
    after_cross = after_self + product(cross_o, co_full)
    cross_low = after_cross.astype(bf16)

    cross_rows, bank_quarter = lax.optimization_barrier((spread(cross_low), bank_quarter))
    bank_other = gather(bank_quarter, "rows")

    def of_pair(x, step, width, axis):
        return lax.dynamic_slice_in_dim(x, (pair ^ step) * width, width, axis)

    inward = after(jnp.stack([cross_o, self_low, attended, hidden_low]), cross_rows)
    inward = [of_pair(inward, 0, 2 * slim, 2)] + [
        to_pair(of_pair(inward, step, 2 * slim, 2), step) for step in range(1, 4)
    ]
    inner = product(cross_rows, up_two) + bias_two
    activated, gelu_pull = jax.vjp(jax.nn.gelu, inner)
    act_low = activated.astype(bf16)
    (grad_inner,) = gelu_pull(contract(branch_rows, down_two, ((1,), (1,))))
    inner_low = grad_inner.astype(bf16)
    over_rows = ((0,), (0,))

    def pair_sum(x, axis):
        half = x.shape[axis] // 2
        kept = lax.dynamic_slice_in_dim(x, member * half, half, axis)
        sent = lax.dynamic_slice_in_dim(x, (1 - member) * half, half, axis)
        return kept + swap_pair(sent.astype(bf16)).astype(f32)

    def own_sum(x):
        half = x.shape[0] // 2
        return x[:half] + swap_pair(x[half:].astype(bf16)).astype(f32)

    cross_sums = contract(inner_low, up_two, ((1,), (1,))).reshape(4, pixels, channels)
    grad_cross = grad_res + member_sum(cross_sums)
    grad_down = own_sum(contract(act_low, branch_rows, over_rows)).astype(bf16)
    grad_upb = own_sum(jnp.sum(inner_low.astype(f32), axis=0))
    relative = pair ^ jnp.arange(4, dtype=jnp.int32)
    grad_up = contract(cross_rows, inner_low, over_rows).reshape(4, 2, slim, 2 * units)
    kept = lax.dynamic_index_in_dim(grad_up, member, 1, keepdims=False)
    sent = lax.dynamic_index_in_dim(grad_up, 1 - member, 1, keepdims=False).astype(bf16)
    sent = swap_pair(jnp.concatenate([sent[:, :, units:], sent[:, :, :units]], axis=2))
    ups = (kept + sent.astype(f32)).astype(bf16)
    ups = [lax.dynamic_index_in_dim(ups, pair ^ step, 0, keepdims=False) for step in range(4)]
    ups = [ups[0]] + [to_pair(ups[step], step) for step in range(1, 4)]

    cbranch = grad_cross.astype(bf16)
    grad_co = contract(cbranch, co_full, ((1,), (1,))).astype(bf16)
    grad_cp = per_token(contract(grad_co, value_blocks, ((1,), (1,))))
    mean = grad_cp[0] * cross_p[0] + grad_cp[1] * cross_p[1] + grad_cp[2] * cross_p[2] + grad_cp[3] * cross_p[3]
    grad_cs = jnp.concatenate([p * (g - mean) for p, g in zip(cross_p, grad_cp)], axis=1).astype(bf16)
    grad_cq = (product(grad_cs, key_blocks) * cross_scale).astype(bf16)

    def from_heads(blocks):
        return jnp.sum(jnp.where(in_head, blocks.reshape(tokens, head_count, channels), 0.0), axis=1)

    grad_kv = jnp.concatenate(
        [
            from_heads(contract(grad_cs, cross_q, over_rows)) * cross_scale,
            from_heads(contract(cross_plow, grad_co, over_rows)),
        ],
        axis=1,
    )
    grad_kv = (grad_kv + swap_pair(grad_kv)).astype(bf16)
    grad_self = grad_cross + contract(grad_cq, cq_full, ((1,), (1,)))

    sbranch = grad_self.astype(bf16)

    token_rows = jnp.pad(grad_kv.reshape(2 * tokens, channels), ((0, 16 - 2 * tokens), (0, 0)))
    out_first = exchange(cbranch)
    out_second = exchange(jnp.concatenate([grad_cq, token_rows]))
    out_third = exchange(sbranch)
    sbranch = after(sbranch, *out_first, *inward)
    grad_att = contract(sbranch, out_full, ((1,), (1,))).astype(bf16)
    mlp_grads = jnp.concatenate([grad_down.reshape(4, -1, channels)] + [x[None] for x in ups])
    grad_att = after(grad_att, mlp_grads, *out_second)
    grad_qloc, grad_kall, grad_vall = attend_back(queries, keys_all, values_all, grad_att)
    theirs = jnp.concatenate([grad_kall[pixels:], grad_vall[pixels:]], axis=1)
    theirs, mlp_grads = lax.optimization_barrier((theirs, mlp_grads, bank_other, *out_third))[:2]
    mlp_grads = lax.psum(mlp_grads, "rows")
    theirs = swap_pair(theirs)
    grad_q = (grad_qloc + (grad_kall[:pixels] + theirs[:, :channels])).astype(bf16)
    grad_v = (grad_vall[:pixels] + theirs[:, channels:]).astype(bf16)
    grad_hidden = grad_self + contract(grad_q, qk_full, ((1,), (1,))) + contract(grad_v, val_full, ((1,), (1,)))
    grad_pre = grad_hidden * jnp.where(pre_act > 0, 1.0, SLOPE)
    grad_conv = (grad_pre * demodulate).astype(bf16)

    with_tokens = jnp.concatenate([grad_conv, token_rows])
    steps = [with_tokens] + [
        lax.ppermute(with_tokens, "rows", [(z, (z + k) % 4) for z in range(4)]) for k in range(1, 4)
    ]
    grad_cols = trade(jnp.transpose(grad_conv.reshape(pixels, 8, slim), (1, 0, 2)))
    grad_maps = grad_cols.reshape(held, sides * sides, slim)
    coef_cols = jnp.square(demod_cols) * jnp.sum(grad_maps.astype(f32) * conv_cols, axis=1)
    all_taps = pool_matrix(jnp.arange(9, dtype=jnp.int32), sides)
    shifted = jnp.einsum(
        "tlp,spo->tslo", all_taps, grad_maps, preferred_element_type=f32
    )
    shifted = shifted.astype(bf16).reshape(9, held * lows, slim)
    grad_low = lax.dot_general(
        shifted, bank_cols[0], (((0, 2), (0, 2)), ((), ())), preferred_element_type=f32
    ).reshape(held, lows, channels)
    grad_low_other = lax.dot_general(
        shifted, bank_cols[1], (((0, 2), (0, 2)), ((), ())), preferred_element_type=f32
    ).reshape(held, lows, channels)
    mod_low = own_mod.astype(f32)
    select_taps = jnp.stack(
        [jnp.sum(mod_low * grad_low, axis=(1, 2)), jnp.sum(mod_low * grad_low_other, axis=(1, 2))], axis=1
    )
    low_partial = own_select[:, 0, None, None] * grad_low + own_select[:, 1, None, None] * grad_low_other
    conv_all = gather(jnp.stack(lax.optimization_barrier((*steps, low_partial))[:4])[None], "batch")
    late = exchange(after(jnp.concatenate([grad_q, grad_v], axis=1), grad_maps))
    low_partial = after(low_partial, *late)
    low_parts = trade(low_partial.astype(bf16).reshape(8, lows // 2, channels))
    low_total = jnp.sum(low_parts.astype(f32), axis=0)

    held_back = lax.optimization_barrier((act_low, low_partial, *inward, *out_first, *out_second, *out_third))
    act_low, inward = held_back[0], jnp.stack(held_back[2:6])
    out_first, out_second, out_third = [jnp.stack(held_back[6 + 4 * i : 10 + 4 * i]) for i in range(3)]
    result = product(act_low, down_two).reshape(4, pixels, channels)
    result = (after_cross + member_sum(result)).astype(bf16)
    colour = contract(rgb_full.astype(bf16), result, ((1,), (1,)))
    grad_rgb_w = contract(grad_rgb, result.astype(f32), ((0,), (0,)), HIGH)
    kv_all = out_second[:, pixels:].reshape(held, -1)[:, : grad_kv.size].reshape(held * tokens, 2 * channels)
    grad_context = contract(kv_all[:, :channels], ck_w, ((1,), (1,))) + contract(kv_all[:, channels:], cv_w, ((1,), (1,)))
    grad_context = jnp.take(grad_context.reshape(held, -1), relative, axis=0)
    to_channel = [contract(coef_cols, x, ((1,), (1,)), HIGH) for x in products]
    first_share, other_share = own_select[:, :1], own_select[:, 1:]
    scale_term = -own_scales * (
        first_share * first_share * to_channel[0]
        + 2.0 * first_share * other_share * to_channel[1]
        + other_share * other_share * to_channel[2]
    )
    square_scales = jnp.square(own_scales)
    energy = [jnp.sum(square_scales * x, axis=1, keepdims=True) for x in to_channel]
    select_term = jnp.concatenate(
        [
            first_share * energy[0] + other_share * energy[1],
            first_share * energy[1] + other_share * energy[2],
        ],
        axis=1,
    )
    select_partial = select_taps - select_term

    member_scales = lax.dynamic_index_in_dim(own_scales, pair, 0, keepdims=False)
    feat_own = feat_all.reshape(total * lows, channels)
    feat_own = lax.dynamic_slice_in_dim(feat_own, first * lows + device * (lows // 2), lows // 2, 0).astype(f32)
    grad_input_rows = low_total * member_scales
    square_sum = jnp.sum(jnp.square(grad_input_rows))


    def weight_gradients(pairs):
        parts = [contract(inward[:, pick], right, ((0, 1), (0, 1))) for pick, right in pairs]
        parts = pair_sum(jnp.stack(parts).reshape(len(parts), 2 * slim, channels), 1)
        return parts.astype(bf16)

    grads_three = weight_gradients([(0, out_first), (1, out_second[:, :pixels]), (2, out_third)])
    grad_hidden_sums = jnp.stack([jnp.sum(grad_pre, axis=0), jnp.sum(grad_pre * noise_col, axis=0)])
    singles = jnp.concatenate([select_partial.reshape(-1), square_sum[None], jnp.zeros((127 - 2 * held,), f32)])
    singles = jnp.concatenate([coef_cols.reshape(-1), singles])
    last_sent = jnp.concatenate(
        [
            grad_hidden_sums,
            grad_rgb_w,
            grad_context.reshape(-1, channels),
            jnp.sum(low_total * feat_own, axis=0)[None],
            scale_term,
            jnp.pad(singles, (0, channels - singles.shape[0]))[None],
        ]
    )
    last_all = gather(last_sent[None], "batch")
    col_sums = jnp.sum(lax.dynamic_slice_in_dim(last_all[:, :5], device * slim, slim, 2), axis=0)
    context_grads = jnp.transpose(last_all[:, 5:7].reshape(8, held * tokens, slim), (1, 0, 2)).reshape(held, -1)
    table_cols = class_table.shape[1]
    context_grads = lax.dynamic_slice_in_dim(context_grads, device * table_cols, table_cols, 1)
    grad_scales = jnp.sum(last_all[:, 7].reshape(held, 2, channels), axis=1) + jnp.sum(last_all[:, 8 : 8 + held], axis=0)
    singles = last_all[:, 8 + held]
    coef_plane = jnp.transpose(singles[:, : held * slim].reshape(8, held, slim), (1, 0, 2)).reshape(-1)
    singles = jnp.sum(singles[:, held * slim : held * slim + 128], axis=0)
    pieces = [coef_plane, context_grads.reshape(-1), grad_scales.reshape(-1), col_sums.reshape(-1), grad_upb, singles]
    ends = []
    for x in pieces:
        ends.append(x.shape[0] + (ends[-1] if ends else 0))
    rows_all = gather(jnp.concatenate(pieces).reshape(1, -1, 128), "rows").reshape(4, -1)
    late = jnp.stack(late)
    grads_two = weight_gradients([(3, late[:, :, :channels]), (3, late[:, :, channels:])])

    mids = jnp.concatenate([grads_three, grads_two])
    mids = lax.psum(after(mids, mlp_grads), "rows")
    coef = rows_all[:, : ends[0]].reshape(total, channels)
    first_tap = 2 * (device % 4)
    matrix = pool_matrix(first_tap + jnp.arange(3, dtype=jnp.int32), sides)
    order = (plane - jnp.arange(4, dtype=jnp.int32)) % 4
    shifted_all = pool_samples(order, matrix, conv_all.reshape(4, 2, 4, pixels + 16, channels), pixels)
    kv_every = jnp.transpose(conv_all[::2, :, pixels : pixels + 2 * tokens], (1, 0, 2, 3))
    kv_every = kv_every.reshape(total * tokens, 2 * channels)
    context_every = lax.dynamic_slice_in_dim(after(context_all, low_total).reshape(4, held * tokens, channels), device * slim, slim, 2)
    context_every = jnp.take(context_every, order, axis=0).reshape(total * tokens, slim)
    sum_ck = contract(context_every, kv_every[:, :channels], over_rows)
    sum_cv = contract(context_every, kv_every[:, channels:], over_rows)
    square_all = jnp.square(scales)
    blocks = (device % 4) * 9 + jnp.arange(9, dtype=jnp.int32)
    bank_total = bank_gradient(
        blocks // 4 - first_tap,
        blocks % 4,
        left,
        shifted_all.reshape(3, total * lows, channels),
        kernel_bank,
        bank_other,
        split_terms(own_share * own_share * square_all, True),
        split_terms(own_share * share_other * square_all, True),
        split_terms(coef, False),
    )

    mlp_grads = after(mlp_grads, bank_total).astype(f32)
    sum_down = mlp_grads[:4].reshape(units, channels)
    ordered = [lax.dynamic_index_in_dim(mlp_grads, 4 + (pair ^ c), 0, keepdims=False) for c in range(4)]
    swapped = [jnp.concatenate([x[:, units:], x[:, :units]], axis=1) for x in ordered]
    sum_up = jnp.where(member == 0, jnp.concatenate(ordered, axis=1), jnp.concatenate(swapped, axis=1))

    rows_late = after(rows_all, bank_total)
    context_grads = rows_late[:, ends[0] : ends[1]].reshape(total, table_cols)
    grad_scales = rows_late[:, ends[1] : ends[2]].reshape(total, channels)
    rows_total = jnp.sum(rows_late[:, ends[2] : ends[4]], axis=0)
    sum_bias, sum_gain = rows_total[:slim], rows_total[slim : 2 * slim]
    sum_rgb = rows_total[2 * slim : 5 * slim].reshape(3, slim)
    sum_upb = rows_total[5 * slim :]
    singles = rows_late[:, ends[4] :]
    grad_select = singles[:, : 2 * held].reshape(total, 2)
    square_sum = jnp.sum(singles[:, 2 * held])
    classes = class_table.shape[0]
    one_hot = (labels_all[:, None] == jnp.arange(classes)[None, :]).astype(f32)
    sum_table = contract(one_hot, context_grads, over_rows, HIGH)
    entries = float(total * 4 * in_rows * in_cols * channels)
    r1_value = square_sum / entries
    style_f32 = style_own.astype(f32)
    grad_logits = select * (grad_select - jnp.sum(grad_select * select, axis=-1, keepdims=True))
    sum_mod = contract(style_f32, grad_scales, over_rows, HIGH)
    sum_sel = contract(style_f32, grad_logits, over_rows, HIGH)

    feat_out = from_pixels(after(result, coef).reshape(2, piece, channels), odd_z, odd_pair)
    feat_out = feat_out.reshape(slots, 2 * in_rows, sides, channels)
    colour_sent = jnp.transpose(colour.reshape(3, 2, piece), (1, 0, 2)).reshape(2, 1, 3 * piece)
    colour_sent = jnp.pad(colour_sent, ((0, 0), (0, 0), (0, channels - 3 * piece)))
    low_sent = jnp.concatenate([grad_input_rows.reshape(2, lows // 4, channels), colour_sent], axis=1)
    low_back = from_pixels(after(low_sent, coef), odd_z, odd_pair)
    rgb_out = low_back[:, lows // 4, : 3 * piece].reshape(slots, 3, 2 * in_rows, sides)
    grad_input = low_back[:, : lows // 4].reshape(slots, in_rows, in_cols, channels)
    mids = after(mids, feat_out, low_back, sum_up, sum_down, sum_table, sum_mod, sum_ck, sum_cv, sum_rgb)
    sum_co, sum_cq, sum_out, sum_qk, sum_val = [mids[i].astype(f32) for i in range(5)]
    return (
        feat_out,
        rgb_out,
        grad_input,
        r1_value,
        sum_mod,
        sum_sel,
        bank_total,
        sum_bias,
        sum_gain,
        sum_qk,
        sum_val,
        sum_out,
        sum_cq,
        sum_ck,
        sum_cv,
        sum_co,
        sum_up,
        sum_upb,
        sum_down,
        sum_table,
        sum_rgb,
    )


def solution(mesh):
    split = mesh.shape["batch"] == 8 and mesh.shape["rows"] == 4
    return jax.shard_map(
        by_planes if split else per_device,
        mesh=mesh,
        in_specs=(
            P("batch", "rows", None, None),
            P("batch", None),
            P("batch"),
            P("batch", "rows", None),
            P("batch", "rows", None, None),
            P("batch", None, "rows", None),
            P("batch", None),
            P("batch", None),
            P("batch", None),
            P("batch"),
            P("batch"),
            P("batch", None),
            P("batch", None),
            P("batch", None),
            P("batch", None),
            P("batch", None),
            P("batch", None),
            P("batch", None),
            P("batch", None),
            P("batch"),
            P("batch", None),
            P(None, "batch"),
            P(None, "batch"),
        ),
        out_specs=(
            P("batch", "rows", None, None),
            P("batch", None, "rows", None),
            P("batch", "rows", None, None),
            P(),
            P("batch", None),
            P("batch", None),
            P("batch", None),
            P("batch"),
            P("batch"),
            P("batch", None),
            P("batch", None),
            P("batch", None),
            P("batch", None),
            P("batch", None),
            P("batch", None),
            P("batch", None),
            P("batch", None),
            P("batch"),
            P("batch", None),
            P(None, "batch"),
            P(None, "batch"),
        ),
        check_vma=False,
    )
```

```python
import jax
import jax.numpy as jnp
from jax import lax
from jax.experimental import pallas as pl
from jax.experimental.pallas import tpu as pltpu
from jax.sharding import PartitionSpec as P

HEAD_DIM = 64


HIGH = lax.Precision.HIGHEST
EPSILON = 1e-08
SLOPE = 0.2


def with_halo(cells, sides, width):
    for axis, dim in sides:
        count = lax.axis_size(axis)
        ends = count - 1
        head = lax.slice_in_dim(cells, 0, width, axis=dim)
        tail = lax.slice_in_dim(cells, cells.shape[dim] - width, cells.shape[dim], axis=dim)
        cells = jnp.concatenate(
            [
                lax.ppermute(tail, axis, [(i, (i + 1) % count) for i in range(ends)]),
                cells,
                lax.ppermute(head, axis, [((i + 1) % count, i) for i in range(ends)]),
            ],
            axis=dim,
        )
    return cells


def product(left, right):
    return jnp.dot(left, right, preferred_element_type=jnp.float32)


def kernel_mix(bank_split, select_row):
    mixed_kernel = select_row[0] * bank_split[0].astype(jnp.float32)
    mixed_kernel = mixed_kernel + select_row[1] * bank_split[1].astype(jnp.float32)
    return mixed_kernel


def gather_taps(padded, out_rows, out_cols, flipped):
    pieces = []
    for row_off in range(3):
        for col_off in range(3):
            if flipped:
                pieces.append(
                    padded[
                        :,
                        2 - row_off : 2 - row_off + out_rows,
                        2 - col_off : 2 - col_off + out_cols,
                    ]
                )
            else:
                pieces.append(padded[:, row_off : row_off + out_rows, col_off : col_off + out_cols])
    return jnp.concatenate(pieces, axis=-1)


def per_device(
    feat_in,
    style_vec,
    labels,
    noise_map,
    cot_feat,
    cot_rgb,
    mod_w,
    sel_w,
    kernel_bank,
    conv_bias,
    noise_gain,
    qk_w,
    val_w,
    out_w,
    cq_w,
    ck_w,
    cv_w,
    co_w,
    up_w,
    up_b,
    down_w,
    class_table,
    rgb_w,
):
    f32 = jnp.float32
    bf16 = jnp.bfloat16
    (
        mod_full,
        sel_full,
        bias_full,
        gain_full,
        qk_full,
        val_full,
        out_full,
        cq_full,
        ck_full,
        cv_full,
        co_full,
        up_full,
        upb_full,
        down_full,
        table_full,
        rgb_full,
    ) = (
        lax.all_gather(mod_w, "batch", axis=0, tiled=True),
        lax.all_gather(sel_w, "batch", axis=0, tiled=True),
        lax.all_gather(conv_bias, "batch", axis=0, tiled=True),
        lax.all_gather(noise_gain, "batch", axis=0, tiled=True),
        lax.all_gather(qk_w, "batch", axis=0, tiled=True),
        lax.all_gather(val_w, "batch", axis=0, tiled=True),
        lax.all_gather(out_w, "batch", axis=0, tiled=True),
        lax.all_gather(cq_w, "batch", axis=0, tiled=True),
        lax.all_gather(ck_w, "batch", axis=0, tiled=True),
        lax.all_gather(cv_w, "batch", axis=0, tiled=True),
        lax.all_gather(co_w, "batch", axis=0, tiled=True),
        lax.all_gather(up_w, "batch", axis=0, tiled=True),
        lax.all_gather(up_b, "batch", axis=0, tiled=True),
        lax.all_gather(down_w, "batch", axis=0, tiled=True),
        lax.all_gather(class_table, "batch", axis=1, tiled=True),
        lax.all_gather(rgb_w, "batch", axis=1, tiled=True),
    )
    bank_full = lax.all_gather(kernel_bank, "batch", axis=0, tiled=True)
    samples, in_rows, in_cols, channels = feat_in.shape
    out_rows = 2 * in_rows
    out_cols = 2 * in_cols
    pixels = out_rows * out_cols
    span = 9 * channels
    kernels = bank_full.shape[0] // span
    head_dim = HEAD_DIM
    head_count = channels // head_dim
    bank_split = bank_full.reshape(kernels, span, channels)
    scales = 1.0 + product(style_vec, mod_full)
    select = jax.nn.softmax(product(style_vec, sel_full), axis=-1)
    scale_tiled = jnp.tile(scales, (1, 9))
    upsampled = jnp.repeat(jnp.repeat(feat_in, 2, axis=1), 2, axis=2)
    modulated = (upsampled.astype(f32) * scales[:, None, None, :]).astype(bf16)
    with_rim = with_halo(modulated, (("rows", 1),), 1)
    padded = jnp.pad(with_rim, ((0, 0), (0, 0), (1, 1), (0, 0)))
    patches = gather_taps(padded, out_rows, out_cols, False).reshape(samples, pixels, span)

    def conv_forward(sample_item):
        patch_row, select_row, scale_row = sample_item
        mixed_kernel = kernel_mix(bank_split, select_row)
        demod_row = lax.rsqrt(
            jnp.sum(jnp.square(mixed_kernel * scale_row[:, None]), axis=0) + EPSILON
        )
        return (product(patch_row, mixed_kernel.astype(bf16)), demod_row, mixed_kernel)

    conv_out, demodulate, mixed_all = lax.map(conv_forward, (patches, select, scale_tiled))
    noise_flat = noise_map.reshape(samples, pixels, 1)
    pre_act = (
        conv_out * demodulate[:, None, :]
        + gain_full.astype(f32) * noise_flat
        + bias_full.astype(f32)
    )
    hidden = jnp.where(pre_act > 0, pre_act, SLOPE * pre_act)
    hidden_low = hidden.astype(bf16)
    queries = product(hidden_low, qk_full).astype(bf16)
    values = product(hidden_low, val_full).astype(bf16)
    all_queries, all_values = (
        lax.all_gather(queries, "rows", axis=1, tiled=True),
        lax.all_gather(values, "rows", axis=1, tiled=True),
    )
    query_h = queries.reshape(samples, pixels, head_count, head_dim)
    key_h = all_queries.reshape(samples, -1, head_count, head_dim)
    value_h = all_values.reshape(samples, -1, head_count, head_dim)
    key_f32 = key_h.astype(f32)
    key_norm = jnp.transpose(jnp.sum(jnp.square(key_f32), axis=-1), (0, 2, 1))[:, :, None, :]
    l2_scale = 0.5 * head_dim ** (-0.5)

    def self_scores():
        inner_dots = jnp.einsum("bqhd,bkhd->bhqk", query_h, key_h, preferred_element_type=f32)
        return l2_scale * (2.0 * inner_dots - key_norm)

    scores = self_scores()
    row_max = jnp.max(scores, axis=-1, keepdims=True)
    log_total = row_max + jnp.log(jnp.sum(jnp.exp(scores - row_max), axis=-1, keepdims=True))
    probs_low = jnp.exp(scores - log_total).astype(bf16)
    attended = (
        jnp.einsum("bhqk,bkhd->bqhd", probs_low, value_h, preferred_element_type=f32)
        .reshape(samples, pixels, channels)
        .astype(bf16)
    )
    after_self = hidden + product(attended, out_full)
    self_low = after_self.astype(bf16)
    cross_q = product(self_low, cq_full).astype(bf16).reshape(samples, pixels, head_count, head_dim)
    classes = table_full.shape[0]
    one_hot = (labels[:, None] == jnp.arange(classes)[None, :]).astype(bf16)
    contexts = table_full.shape[1] // channels
    context = product(one_hot, table_full).astype(bf16).reshape(samples, contexts, channels)
    cross_k = jnp.einsum("bjc,cd->bjd", context, ck_full, preferred_element_type=f32).astype(bf16)
    cross_v = jnp.einsum("bjc,cd->bjd", context, cv_full, preferred_element_type=f32).astype(bf16)
    key_cross = cross_k.reshape(samples, contexts, head_count, head_dim)
    value_cross = cross_v.reshape(samples, contexts, head_count, head_dim)
    cross_scale = head_dim ** (-0.5)
    cross_s = (
        jnp.einsum("bqhd,bjhd->bhqj", cross_q, key_cross, preferred_element_type=f32) * cross_scale
    )
    cross_p = jax.nn.softmax(cross_s, axis=-1)
    cross_plow = cross_p.astype(bf16)
    cross_o = (
        jnp.einsum("bhqj,bjhd->bqhd", cross_plow, value_cross, preferred_element_type=f32)
        .reshape(samples, pixels, channels)
        .astype(bf16)
    )
    after_cross = after_self + product(cross_o, co_full)
    cross_low = after_cross.astype(bf16)
    inner = product(cross_low, up_full) + upb_full.astype(f32)
    activated, gelu_pull = jax.vjp(jax.nn.gelu, inner)
    act_low = activated.astype(bf16)
    after_mlp = after_cross + product(act_low, down_full)
    result = after_mlp.astype(bf16)
    colour = product(result, rgb_full.T)
    rgb_out = jnp.transpose(colour, (0, 2, 1)).reshape(samples, 3, out_rows, out_cols)
    grad_rgb = jnp.transpose(cot_rgb.reshape(samples, 3, pixels), (0, 2, 1))
    grad_res = cot_feat.reshape(samples, pixels, channels).astype(f32) + jnp.dot(
        grad_rgb, rgb_full.astype(f32), precision=HIGH
    )
    grad_rgb_w = jnp.einsum("bpk,bpc->kc", grad_rgb, result.astype(f32), precision=HIGH)
    branch = grad_res.astype(bf16)
    grad_down_w = jnp.einsum("bpf,bpc->fc", act_low, branch, preferred_element_type=f32)
    (grad_inner,) = gelu_pull(product(branch, down_full.T))
    inner_low = grad_inner.astype(bf16)
    grad_up_b = jnp.sum(inner_low.astype(f32), axis=(0, 1))
    grad_up_w = jnp.einsum("bpc,bpf->cf", cross_low, inner_low, preferred_element_type=f32)
    grad_cross = grad_res + product(inner_low, up_full.T)
    cbranch = grad_cross.astype(bf16)
    grad_co_w = jnp.einsum("bpc,bpd->cd", cross_o, cbranch, preferred_element_type=f32)
    grad_co = (
        product(cbranch, co_full.T).astype(bf16).reshape(samples, pixels, head_count, head_dim)
    )
    grad_cp = jnp.einsum("bqhd,bjhd->bhqj", grad_co, value_cross, preferred_element_type=f32)
    grad_cv = (
        jnp.einsum("bhqj,bqhd->bjhd", cross_plow, grad_co, preferred_element_type=f32)
        .astype(bf16)
        .reshape(samples, contexts, channels)
    )
    grad_cs = (cross_p * (grad_cp - jnp.sum(grad_cp * cross_p, axis=-1, keepdims=True))).astype(
        bf16
    )
    grad_cq = (
        (
            jnp.einsum("bhqj,bjhd->bqhd", grad_cs, key_cross, preferred_element_type=f32)
            * cross_scale
        )
        .astype(bf16)
        .reshape(samples, pixels, channels)
    )
    grad_ck = (
        (jnp.einsum("bhqj,bqhd->bjhd", grad_cs, cross_q, preferred_element_type=f32) * cross_scale)
        .astype(bf16)
        .reshape(samples, contexts, channels)
    )
    grad_cq_w = jnp.einsum("bpc,bpd->cd", self_low, grad_cq, preferred_element_type=f32)
    grad_ck_w = jnp.einsum("bjc,bjd->cd", context, grad_ck, preferred_element_type=f32)
    grad_cv_w = jnp.einsum("bjc,bjd->cd", context, grad_cv, preferred_element_type=f32)
    grad_context = jnp.einsum(
        "bjd,cd->bjc", grad_ck, ck_full, preferred_element_type=f32
    ) + jnp.einsum("bjd,cd->bjc", grad_cv, cv_full, preferred_element_type=f32)
    grad_table = jnp.dot(
        one_hot.astype(f32).T, grad_context.reshape(samples, contexts * channels), precision=HIGH
    )
    grad_self = grad_cross + product(grad_cq, cq_full.T)
    sbranch = grad_self.astype(bf16)
    grad_out_w = jnp.einsum("bpc,bpd->cd", attended, sbranch, preferred_element_type=f32)
    grad_att = (
        product(sbranch, out_full.T).astype(bf16).reshape(samples, pixels, head_count, head_dim)
    )
    probs = jnp.exp(self_scores() - log_total)
    probs_again = probs.astype(bf16)
    grad_probs = jnp.einsum("bqhd,bkhd->bhqk", grad_att, value_h, preferred_element_type=f32)
    grad_vall = jnp.einsum("bhqk,bqhd->bkhd", probs_again, grad_att, preferred_element_type=f32)
    grad_s = (probs * (grad_probs - jnp.sum(grad_probs * probs, axis=-1, keepdims=True))).astype(
        bf16
    )
    grad_qloc = (
        2.0 * l2_scale * jnp.einsum("bhqk,bkhd->bqhd", grad_s, key_h, preferred_element_type=f32)
    )
    col_total = jnp.transpose(jnp.sum(grad_s.astype(f32), axis=2), (0, 2, 1))[:, :, :, None]
    grad_kall = (
        2.0
        * l2_scale
        * (
            jnp.einsum("bhqk,bqhd->bkhd", grad_s, query_h, preferred_element_type=f32)
            - key_f32 * col_total
        )
    )
    back_keys, back_values = (
        lax.psum_scatter(
            grad_kall.reshape(samples, -1, channels).astype(jnp.bfloat16),
            "rows",
            scatter_dimension=1,
            tiled=True,
        ).astype(jnp.float32),
        lax.psum_scatter(
            grad_vall.reshape(samples, -1, channels).astype(jnp.bfloat16),
            "rows",
            scatter_dimension=1,
            tiled=True,
        ).astype(jnp.float32),
    )
    grad_q = (grad_qloc.reshape(samples, pixels, channels) + back_keys).astype(bf16)
    grad_v = back_values.astype(bf16)
    grad_qk_w = jnp.einsum("bpc,bpd->cd", hidden_low, grad_q, preferred_element_type=f32)
    grad_val_w = jnp.einsum("bpc,bpd->cd", hidden_low, grad_v, preferred_element_type=f32)
    grad_hidden = grad_self + product(grad_q, qk_full.T) + product(grad_v, val_full.T)
    grad_pre = grad_hidden * jnp.where(pre_act > 0, 1.0, SLOPE)
    grad_gain = jnp.sum(grad_pre * noise_flat, axis=(0, 1))
    grad_bias = jnp.sum(grad_pre, axis=(0, 1))
    grad_demod = jnp.sum(grad_pre * conv_out, axis=1)
    demod_coef = demodulate**3 * grad_demod
    grad_conv = (grad_pre * demodulate[:, None, :]).astype(bf16)
    grad_rim = with_halo(
        grad_conv.reshape(samples, out_rows, out_cols, channels), (("rows", 1),), 1
    )
    grad_pad = jnp.pad(grad_rim, ((0, 0), (0, 0), (1, 1), (0, 0)))
    grad_patches = gather_taps(grad_pad, out_rows, out_cols, True).reshape(samples, pixels, span)

    def conv_backward(sample_item):
        gpatch_row, mixed_kernel, scale_row, coef_row = sample_item
        taps_low = mixed_kernel.astype(bf16).reshape(9, channels, channels)
        grad_mod = jnp.einsum(
            "pto,tio->pi",
            gpatch_row.reshape(pixels, 9, channels),
            taps_low,
            preferred_element_type=f32,
        )
        scale_term = -scale_row[:channels] * jnp.sum(
            (jnp.square(mixed_kernel) * coef_row[None, :]).reshape(9, channels, channels),
            axis=(0, 2),
        )
        return (grad_mod, scale_term)

    grad_mod, scale_term = lax.map(
        conv_backward, (grad_patches, mixed_all, scale_tiled, demod_coef)
    )
    block_rows = span // 8

    def tap_block(index, carry):
        bank_acc, select_acc = carry
        tap_row = index * block_rows
        patch_cols = lax.dynamic_slice_in_dim(patches, tap_row, block_rows, 2)
        grad_taps = jnp.einsum("bpt,bpo->bto", patch_cols, grad_conv, preferred_element_type=f32)
        bank_rows = lax.dynamic_slice_in_dim(bank_split, tap_row, block_rows, 1).astype(f32)
        mixed_rows = lax.dynamic_slice_in_dim(mixed_all, tap_row, block_rows, 1)
        scale_rows = lax.dynamic_slice_in_dim(scale_tiled, tap_row, block_rows, 1)
        grad_mixed = (
            grad_taps - mixed_rows * jnp.square(scale_rows)[:, :, None] * demod_coef[:, None, :]
        )
        select_acc = select_acc + jnp.einsum("kto,bto->bk", bank_rows, grad_mixed, precision=HIGH)
        bank_piece = jnp.einsum("bk,bto->kto", select, grad_mixed, precision=HIGH)
        bank_acc = lax.dynamic_update_slice_in_dim(bank_acc, bank_piece, tap_row, 1)
        return (bank_acc, select_acc)

    bank_acc, grad_select = lax.fori_loop(
        0,
        8,
        tap_block,
        (jnp.zeros((kernels, span, channels), f32), jnp.zeros((samples, kernels), f32)),
    )
    bank_flat = bank_acc.reshape(kernels * span, channels)
    grad_mod = grad_mod.reshape(samples, out_rows, out_cols, channels)
    grad_scales = jnp.sum(grad_mod * upsampled.astype(f32), axis=(1, 2)) + scale_term
    grad_up = grad_mod * scales[:, None, None, :]
    grad_input = grad_up.reshape(samples, in_rows, 2, in_cols, 2, channels).sum(axis=(2, 4))
    grad_logits = select * (grad_select - jnp.sum(grad_select * select, axis=-1, keepdims=True))
    style_f32 = style_vec.astype(f32)
    grad_mod_w = jnp.dot(style_f32.T, grad_scales, precision=HIGH)
    grad_sel_w = jnp.dot(style_f32.T, grad_logits, precision=HIGH)
    (
        sum_mod,
        sum_sel,
        sum_bias,
        sum_gain,
        sum_qk,
        sum_val,
        sum_out,
        sum_cq,
        sum_ck,
        sum_cv,
        sum_co,
        sum_up,
        sum_upb,
        sum_down,
        sum_table,
        sum_rgb,
    ) = (
        lax.psum_scatter(grad_mod_w, "batch", scatter_dimension=0, tiled=True),
        lax.psum_scatter(grad_sel_w, "batch", scatter_dimension=0, tiled=True),
        lax.psum_scatter(grad_bias, "batch", scatter_dimension=0, tiled=True),
        lax.psum_scatter(grad_gain, "batch", scatter_dimension=0, tiled=True),
        lax.psum_scatter(grad_qk_w, "batch", scatter_dimension=0, tiled=True),
        lax.psum_scatter(grad_val_w, "batch", scatter_dimension=0, tiled=True),
        lax.psum_scatter(grad_out_w, "batch", scatter_dimension=0, tiled=True),
        lax.psum_scatter(grad_cq_w, "batch", scatter_dimension=0, tiled=True),
        lax.psum_scatter(grad_ck_w, "batch", scatter_dimension=0, tiled=True),
        lax.psum_scatter(grad_cv_w, "batch", scatter_dimension=0, tiled=True),
        lax.psum_scatter(grad_co_w, "batch", scatter_dimension=0, tiled=True),
        lax.psum_scatter(grad_up_w, "batch", scatter_dimension=0, tiled=True),
        lax.psum_scatter(grad_up_b, "batch", scatter_dimension=0, tiled=True),
        lax.psum_scatter(grad_down_w, "batch", scatter_dimension=0, tiled=True),
        lax.psum_scatter(grad_table, "batch", scatter_dimension=1, tiled=True),
        lax.psum_scatter(grad_rgb_w, "batch", scatter_dimension=1, tiled=True),
    )
    bank_part = lax.psum_scatter(bank_flat, "batch", scatter_dimension=0, tiled=True)
    (
        sum_mod,
        sum_sel,
        sum_bias,
        sum_gain,
        sum_qk,
        sum_val,
        sum_out,
        sum_cq,
        sum_ck,
        sum_cv,
        sum_co,
        sum_up,
        sum_upb,
        sum_down,
        sum_table,
        sum_rgb,
        bank_total,
    ) = (
        lax.psum(sum_mod.astype(jnp.bfloat16), "rows").astype(jnp.float32),
        lax.psum(sum_sel.astype(jnp.bfloat16), "rows").astype(jnp.float32),
        lax.psum(sum_bias.astype(jnp.bfloat16), "rows").astype(jnp.float32),
        lax.psum(sum_gain.astype(jnp.bfloat16), "rows").astype(jnp.float32),
        lax.psum(sum_qk.astype(jnp.bfloat16), "rows").astype(jnp.float32),
        lax.psum(sum_val.astype(jnp.bfloat16), "rows").astype(jnp.float32),
        lax.psum(sum_out.astype(jnp.bfloat16), "rows").astype(jnp.float32),
        lax.psum(sum_cq.astype(jnp.bfloat16), "rows").astype(jnp.float32),
        lax.psum(sum_ck.astype(jnp.bfloat16), "rows").astype(jnp.float32),
        lax.psum(sum_cv.astype(jnp.bfloat16), "rows").astype(jnp.float32),
        lax.psum(sum_co.astype(jnp.bfloat16), "rows").astype(jnp.float32),
        lax.psum(sum_up.astype(jnp.bfloat16), "rows").astype(jnp.float32),
        lax.psum(sum_upb.astype(jnp.bfloat16), "rows").astype(jnp.float32),
        lax.psum(sum_down.astype(jnp.bfloat16), "rows").astype(jnp.float32),
        lax.psum(sum_table.astype(jnp.bfloat16), "rows").astype(jnp.float32),
        lax.psum(sum_rgb.astype(jnp.bfloat16), "rows").astype(jnp.float32),
        lax.psum(bank_part.astype(jnp.bfloat16), "rows").astype(jnp.float32),
    )
    entry_count = float(
        samples * lax.axis_size("batch") * in_rows * lax.axis_size("rows") * in_cols * channels
    )
    r1_value = lax.psum(jnp.sum(jnp.square(grad_input)), ("batch", "rows")) / entry_count
    feat_out = result.reshape(samples, out_rows, out_cols, channels)
    return (
        feat_out,
        rgb_out,
        grad_input,
        r1_value,
        sum_mod,
        sum_sel,
        bank_total,
        sum_bias,
        sum_gain,
        sum_qk,
        sum_val,
        sum_out,
        sum_cq,
        sum_ck,
        sum_cv,
        sum_co,
        sum_up,
        sum_upb,
        sum_down,
        sum_table,
        sum_rgb,
    )


def gather(x, axis_name, axis=0):
    return lax.all_gather(x, axis_name, axis=axis, tiled=True)


def trade(x):
    return lax.all_to_all(x, "batch", 0, 0, tiled=True)


def to_pair(x, step):
    return lax.ppermute(x, "batch", [(i, i ^ (2 * step)) for i in range(8)])


def spread(x):
    return jnp.concatenate([x] + [to_pair(x, step) for step in range(1, 4)])


def exchange(x):
    return [x] + [to_pair(x, step) for step in range(1, 4)]


def member_sum(parts):
    total = parts[0].astype(jnp.float32)
    for step in range(1, 4):
        total = total + to_pair(parts[step].astype(jnp.bfloat16), step).astype(jnp.float32)
    return total


def after(x, *earlier):
    return lax.optimization_barrier((x,) + earlier)[0]


def behind(x, earlier):
    nothing = jnp.minimum(jnp.abs(earlier[(0,) * earlier.ndim].astype(jnp.float32)), 0.0)
    return x + nothing.astype(x.dtype)


def swap_pair(x):
    return lax.ppermute(x, "batch", [(i, i ^ 1) for i in range(8)])


def move_table(turn):
    table = []
    for d in range(8):
        for z in range(4):
            slot = (z % 2) ^ turn
            pair = 2 * (d % 2) + slot
            table.append((4 * d + z, 4 * (2 * pair + z // 2) + d // 2))
    return table


def to_pixels(x, odd_z, odd_pair):
    sent = jnp.where(odd_z, x[::-1], x)
    first = lax.ppermute(sent[0], ("batch", "rows"), move_table(0))
    second = lax.ppermute(sent[1], ("batch", "rows"), move_table(1))
    return jnp.where(odd_pair, jnp.stack([second, first]), jnp.stack([first, second]))


def from_pixels(x, odd_z, odd_pair):
    sent = jnp.where(odd_pair, x[::-1], x)
    back = [[(b, a) for a, b in move_table(turn)] for turn in range(2)]
    first = lax.ppermute(sent[0], ("batch", "rows"), back[0])
    second = lax.ppermute(sent[1], ("batch", "rows"), back[1])
    return jnp.where(odd_z, jnp.stack([second, first]), jnp.stack([first, second]))


def contract(left, right, dims, precision=None):
    return lax.dot_general(
        left, right, (dims, ((), ())), precision=precision, preferred_element_type=jnp.float32
    )


def conv_kernel(
    select_ref, patch_ref, bank_ref, scale_ref, out_ref, square_ref, product_ref, acc_ref, sum_ref
):
    col, row = pl.program_id(0), pl.program_id(1)
    start = jnp.logical_and(col == 0, row == 0)
    last = jnp.logical_and(col == 2, row == 2)

    @pl.when(start)
    def _():
        acc_ref[...] = jnp.zeros_like(acc_ref)
        sum_ref[...] = jnp.zeros_like(sum_ref)
        product_ref[...] = jnp.zeros_like(product_ref)

    first = bank_ref[0, 0].astype(jnp.float32)
    second = bank_ref[1, 0].astype(jnp.float32)
    product_ref[0] += first * first
    product_ref[1] += first * second
    product_ref[2] += second * second
    for b in range(4):
        mixed = select_ref[b, 0] * first + select_ref[b, 1] * second
        scaled = mixed * scale_ref[b]
        sum_ref[b] += jnp.sum(jnp.square(scaled).reshape(-1, 8, 128), axis=0)
        begin = pl.multiple_of(row * 16, 16)
        left = patch_ref[b, 0, pl.ds(begin, 256), :]
        acc_ref[b] += jnp.dot(left, mixed.astype(jnp.bfloat16), preferred_element_type=jnp.float32)

    @pl.when(last)
    def _():
        out_ref[...] = acc_ref[...]
        square_ref[...] = sum_ref[...]


def conv_forward_plane(select, patch_cols, bank_cols, scale_cols):
    samples, _, _, width = patch_cols.shape
    cols = bank_cols.shape[-1]
    f32 = jnp.float32
    return pl.pallas_call(
        conv_kernel,
        grid=(3, 3),
        in_specs=[
            pl.BlockSpec(memory_space=pltpu.SMEM),
            pl.BlockSpec((samples, 1, 288, width), lambda c, a: (0, c, 0, 0)),
            pl.BlockSpec((2, 1, width, cols), lambda c, a: (0, 3 * a + c, 0, 0)),
            pl.BlockSpec((samples, width, cols), lambda c, a: (0, 0, 0)),
        ],
        out_specs=[
            pl.BlockSpec((samples, 256, cols), lambda c, a: (0, 0, 0)),
            pl.BlockSpec((samples, 8, cols), lambda c, a: (0, 0, 0)),
            pl.BlockSpec((3, width, cols), lambda c, a: (0, 0, 0)),
        ],
        out_shape=[
            jax.ShapeDtypeStruct((samples, 256, cols), f32),
            jax.ShapeDtypeStruct((samples, 8, cols), f32),
            jax.ShapeDtypeStruct((3, width, cols), f32),
        ],
        scratch_shapes=[
            pltpu.VMEM((samples, 256, cols), f32),
            pltpu.VMEM((samples, 8, cols), f32),
        ],
        compiler_params=pltpu.CompilerParams(vmem_limit_bytes=40 << 20),
        cost_estimate=pl.CostEstimate(
            flops=2 * samples * 256 * 9 * width * cols, bytes_accessed=20 << 20, transcendentals=0
        ),
        name="conv_plane",
    )(select, patch_cols, bank_cols, scale_cols)


def head_scores(query, key):
    squares = jnp.square(key.astype(jnp.float32))
    upper = squares.astype(jnp.bfloat16)
    lower = (squares - upper.astype(jnp.float32)).astype(jnp.bfloat16)
    ones = jnp.ones((8, HEAD_DIM), jnp.bfloat16)
    over_last = ((1,), (1,))
    norms = contract(ones, upper, over_last) + contract(ones, lower, over_last)
    scale = 0.5 * HEAD_DIM ** (-0.5)
    return scale * (2.0 * contract(query, key, over_last) - norms[0:1])


def head_softmax(scores):
    raised = jnp.exp(scores - jnp.max(scores, axis=-1, keepdims=True))
    return raised * (1.0 / jnp.sum(raised, axis=-1, keepdims=True))


def attend_kernel(query_ref, key_ref, value_ref, out_ref):
    for h in range(query_ref.shape[1] // HEAD_DIM):
        part = slice(h * HEAD_DIM, (h + 1) * HEAD_DIM)
        probs = head_softmax(head_scores(query_ref[:, part], key_ref[:, part]))
        out_ref[:, part] = jnp.dot(
            probs.astype(jnp.bfloat16), value_ref[:, part], preferred_element_type=jnp.float32
        ).astype(jnp.bfloat16)


def attend(query, key, value):
    pixels, width = query.shape
    everything = key.shape[0]
    pair = 4 * HEAD_DIM
    return pl.pallas_call(
        attend_kernel,
        grid=(width // pair,),
        in_specs=[
            pl.BlockSpec((pixels, pair), lambda i: (0, i)),
            pl.BlockSpec((everything, pair), lambda i: (0, i)),
            pl.BlockSpec((everything, pair), lambda i: (0, i)),
        ],
        out_specs=pl.BlockSpec((pixels, pair), lambda i: (0, i)),
        out_shape=jax.ShapeDtypeStruct((pixels, width), jnp.bfloat16),
        cost_estimate=pl.CostEstimate(
            flops=4 * pixels * everything * width, bytes_accessed=3 << 20, transcendentals=1 << 19
        ),
        name="attend",
    )(query, key, value)


def attend_back_kernel(query_ref, key_ref, value_ref, grad_ref, gq_ref, gk_ref, gv_ref):
    bf16 = jnp.bfloat16
    twice = 2.0 * (0.5 * HEAD_DIM ** (-0.5))
    for h in range(query_ref.shape[1] // HEAD_DIM):
        part = slice(h * HEAD_DIM, (h + 1) * HEAD_DIM)
        query, key, value, grad = query_ref[:, part], key_ref[:, part], value_ref[:, part], grad_ref[:, part]
        probs = head_softmax(head_scores(query, key))
        grad_probs = contract(grad, value, ((1,), (1,)))
        mean = jnp.sum(grad_probs * probs, axis=-1, keepdims=True)
        grad_s = (probs * (grad_probs - mean)).astype(bf16)
        gv_ref[:, part] = contract(probs.astype(bf16), grad, ((0,), (0,)))
        gq_ref[:, part] = twice * jnp.dot(grad_s, key, preferred_element_type=jnp.float32)
        both = jnp.concatenate([query, jnp.ones_like(query)], axis=1)
        sums = contract(grad_s, both, ((0,), (0,)))
        gk_ref[:, part] = twice * (
            sums[:, :HEAD_DIM] - key.astype(jnp.float32) * sums[:, HEAD_DIM:]
        )


def attend_back(query, key, value, grad):
    pixels, width = query.shape
    everything = key.shape[0]
    pair = 4 * HEAD_DIM
    few = pl.BlockSpec((pixels, pair), lambda i: (0, i))
    many = pl.BlockSpec((everything, pair), lambda i: (0, i))
    f32 = jnp.float32
    return pl.pallas_call(
        attend_back_kernel,
        grid=(width // pair,),
        in_specs=[few, many, many, few],
        out_specs=[few, many, many],
        out_shape=[
            jax.ShapeDtypeStruct((pixels, width), f32),
            jax.ShapeDtypeStruct((everything, width), f32),
            jax.ShapeDtypeStruct((everything, width), f32),
        ],
        cost_estimate=pl.CostEstimate(
            flops=14 * pixels * everything * width, bytes_accessed=5 << 20, transcendentals=1 << 19
        ),
        name="attend_back",
    )(query, key, value, grad)


def split_terms(x, left):
    upper = x.astype(jnp.bfloat16)
    lower = (x - upper.astype(jnp.float32)).astype(jnp.bfloat16)
    return jnp.concatenate([upper, upper, lower] if left else [upper, lower, upper])


def bank_kernel(tap_ref, part_ref, left_ref, right_ref, own_ref, other_ref, same_ref, cross_ref, coef_ref, out_ref):
    del tap_ref, part_ref
    first = ((0,), (0,))
    out_ref[...] = (
        jnp.dot(left_ref[...], right_ref[0], preferred_element_type=jnp.float32)
        - own_ref[...].astype(jnp.float32) * contract(same_ref[...], coef_ref[...], first)
        - other_ref[...].astype(jnp.float32) * contract(cross_ref[...], coef_ref[...], first)
    )


def bank_gradient(taps, parts, left, right, own, other, same, cross, coef):
    lows = left.shape[1]
    count = taps.shape[0]
    rows = own.shape[0] // count
    out_cols = own.shape[1]
    terms = coef.shape[0]
    return pl.pallas_call(
        bank_kernel,
        grid_spec=pltpu.PrefetchScalarGridSpec(
            num_scalar_prefetch=2,
            grid=(count,),
            in_specs=[
                pl.BlockSpec((rows, lows), lambda m, t, q: (q[m], 0)),
                pl.BlockSpec((1, lows, out_cols), lambda m, t, q: (t[m], 0, 0)),
                pl.BlockSpec((rows, out_cols), lambda m, t, q: (m, 0)),
                pl.BlockSpec((rows, out_cols), lambda m, t, q: (m, 0)),
                pl.BlockSpec((terms, rows), lambda m, t, q: (0, q[m])),
                pl.BlockSpec((terms, rows), lambda m, t, q: (0, q[m])),
                pl.BlockSpec((terms, out_cols), lambda m, t, q: (0, 0)),
            ],
            out_specs=pl.BlockSpec((rows, out_cols), lambda m, t, q: (m, 0)),
        ),
        out_shape=jax.ShapeDtypeStruct((own.shape[0], out_cols), jnp.float32),
        compiler_params=pltpu.CompilerParams(vmem_limit_bytes=40 << 20),
        cost_estimate=pl.CostEstimate(
            flops=2 * lows * own.shape[0] * out_cols, bytes_accessed=32 << 20, transcendentals=0
        ),
        name="bank_gradient",
    )(taps, parts, left, right, own, other, same, cross, coef)


def pool_matrix(taps, side):
    half = side // 2
    shape = (taps.shape[0], half * half, side * side)
    block = lax.broadcasted_iota(jnp.int32, shape, 1)
    pixel = lax.broadcasted_iota(jnp.int32, shape, 2)
    tap = taps[:, None, None]
    row = pixel // side + tap // 3 - 1 - 2 * (block // half)
    col = pixel % side + tap % 3 - 1 - 2 * (block % half)
    inside = (row >= 0) & (row < 2) & (col >= 0) & (col < 2)
    return inside.astype(jnp.bfloat16)


def patch_matrix(low):
    side = 2 * low
    shape = (3 * (side + 2) * side, low * low)
    place = lax.broadcasted_iota(jnp.int32, shape, 0)
    source = lax.broadcasted_iota(jnp.int32, shape, 1)
    offset, place = place // ((side + 2) * side), place % ((side + 2) * side)
    row, col = place // side - 1, place % side + offset - 1
    inside = (row >= 0) & (row < side) & (col >= 0) & (col < side)
    return (inside & (source == (row // 2) * low + col // 2)).astype(jnp.bfloat16)


def pool_kernel(order_ref, matrix_ref, map_ref, out_ref):
    del order_ref
    pixels = matrix_ref.shape[1]
    taps, _, lows, width = out_ref.shape
    grid = map_ref[...].reshape(pixels, width)
    pooled = jnp.dot(matrix_ref[...], grid, preferred_element_type=jnp.float32)
    out_ref[...] = pooled.astype(jnp.bfloat16).reshape(taps, 1, lows, width)


def pool_samples(order, matrix, maps, piece):
    taps, lows, pixels = matrix.shape
    pairs, members, steps, _, width = maps.shape
    return pl.pallas_call(
        pool_kernel,
        grid_spec=pltpu.PrefetchScalarGridSpec(
            num_scalar_prefetch=1,
            grid=(steps, pairs),
            in_specs=[
                pl.BlockSpec((taps * lows, pixels), lambda k, c, o: (0, 0)),
                pl.BlockSpec((1, members, 1, piece, width), lambda k, c, o: (c, 0, k, 0, 0)),
            ],
            out_specs=pl.BlockSpec((taps, 1, lows, width), lambda k, c, o: (0, o[k] * pairs + c, 0, 0)),
        ),
        out_shape=jax.ShapeDtypeStruct((taps, steps * pairs, lows, width), jnp.bfloat16),
        compiler_params=pltpu.CompilerParams(vmem_limit_bytes=40 << 20),
        cost_estimate=pl.CostEstimate(
            flops=2 * taps * lows * pixels * width * steps * pairs, bytes_accessed=14 << 20, transcendentals=0
        ),
        name="pool_samples",
    )(order, matrix.reshape(taps * lows, pixels), maps)


def by_planes(
    feat_in,
    style_vec,
    labels,
    noise_map,
    cot_feat,
    cot_rgb,
    mod_w,
    sel_w,
    kernel_bank,
    conv_bias,
    noise_gain,
    qk_w,
    val_w,
    out_w,
    cq_w,
    ck_w,
    cv_w,
    co_w,
    up_w,
    up_b,
    down_w,
    class_table,
    rgb_w,
):
    f32, bf16 = jnp.float32, jnp.bfloat16
    device, plane = lax.axis_index("batch"), lax.axis_index("rows")
    pair, member = device // 2, device % 2
    odd_z, odd_pair = plane % 2 == 1, pair % 2 == 1
    slots, in_rows, in_cols, channels = feat_in.shape
    total = 8 * slots
    held = total // 4
    piece = 2 * in_rows * 2 * in_cols
    pixels = 2 * piece
    lows = 4 * in_rows * in_cols
    style_width = style_vec.shape[1]
    own_style = style_width // 8
    slim = channels // 8
    head_count = channels // HEAD_DIM

    point_maps = jnp.concatenate(
        [noise_map.reshape(slots, 1, piece), cot_rgb.reshape(slots, 3, piece)], axis=1
    )
    point_maps = to_pixels(point_maps, odd_z, odd_pair)
    point_cols = jnp.transpose(point_maps, (0, 2, 1)).reshape(pixels, 4)
    noise_col, grad_rgb = point_cols[:, :1], point_cols[:, 1:]

    packed = jnp.concatenate(
        [
            feat_in.reshape(-1, 128),
            style_vec.reshape(-1, 128),
            conv_bias.reshape(-1, 128),
            noise_gain.reshape(-1, 128),
            rgb_w.reshape(-1, 128),
            jnp.pad(jnp.stack([labels // 32, labels % 32]).astype(bf16), ((0, 0), (0, 128 - slots))),
        ]
    )
    bank_sent = jnp.transpose(kernel_bank.reshape(-1, 8, slim), (1, 0, 2))
    smalls = gather(after(packed, bank_sent, point_cols)[None], "batch")
    feat_rows = feat_in.size // 128
    style_rows = style_vec.size // 128
    at = feat_rows + style_rows
    feat_part = smalls[:, :feat_rows].reshape(total, in_rows * in_cols, channels)
    style_all = smalls[:, feat_rows:at].reshape(total, style_width)
    bias_full = smalls[:, at].astype(f32).reshape(channels)
    gain_full = smalls[:, at + 1].astype(f32).reshape(channels)
    rgb_full = jnp.transpose(smalls[:, at + 2 : at + 5], (1, 0, 2)).astype(f32).reshape(3, channels)
    label_parts = smalls[:, at + 5 : at + 7, :slots].astype(jnp.int32)
    labels_all = (32 * label_parts[:, 0] + label_parts[:, 1]).reshape(total)

    style_own = lax.dynamic_slice_in_dim(style_all, device * own_style, own_style, 1)
    context_own = jnp.take(class_table, labels_all, axis=0)
    partial_styles = jnp.concatenate(
        [
            product(style_own, mod_w),
            jnp.pad(product(style_own, sel_w), ((0, 0), (0, 126))),
            context_own.astype(f32),
        ],
        axis=1,
    )
    styles = gather(partial_styles[None], "batch")
    sums = jnp.sum(styles[:, :, : channels + 128], axis=0)
    scales = 1.0 + sums[:, :channels]
    select = jax.nn.softmax(sums[:, channels : channels + 2], axis=-1)
    context_all = jnp.transpose(styles[:, :, channels + 128 :], (1, 0, 2)).reshape(total, -1).astype(bf16)
    feat_all = gather(feat_part[None], "rows")
    feat_all = jnp.transpose(feat_all, (1, 0, 2, 3)).reshape(total, lows, channels)

    kernels = 2
    bank_cols = trade(after(bank_sent, styles)).reshape(kernels, 9, channels, slim)

    squares = jnp.stack(lax.optimization_barrier((qk_w, val_w, out_w, cq_w, co_w, styles))[:5])
    weights = gather(squares, "batch", 1)
    qk_full, val_full, out_full, cq_full, co_full = [weights[i] for i in range(5)]


    first = held * plane
    tokens = context_all.shape[1] // channels
    modulated = (feat_all.astype(f32) * scales[:, None, :]).astype(bf16)
    own_mod = lax.dynamic_slice_in_dim(modulated, first, held, 0)
    own_scales = lax.dynamic_slice_in_dim(scales, first, held, 0)
    own_select = lax.dynamic_slice_in_dim(select, first, held, 0)
    sides = 2 * in_cols
    patch_cols = jnp.einsum(
        "srl,slc->src",
        jnp.broadcast_to(patch_matrix(in_cols)[None], (held, 3 * (sides + 2) * sides, lows)),
        own_mod,
        preferred_element_type=f32,
    )
    patch_cols = patch_cols.astype(bf16).reshape(held, 3, (sides + 2) * sides, channels)
    kernel_id = device // 4
    own_share = lax.dynamic_index_in_dim(select, kernel_id, 1)
    share_other = lax.dynamic_index_in_dim(select, 1 - kernel_id, 1)
    left = (own_share[:, :, None] * modulated.astype(f32)).astype(bf16)
    left = jnp.transpose(left.reshape(total * lows, channels))
    scale_cols = jnp.broadcast_to(own_scales[:, :, None], (held, channels, slim))
    own_context = lax.dynamic_slice_in_dim(context_all, first, held, 0).reshape(held * tokens, channels)
    context_cols = lax.dynamic_slice_in_dim(own_context, device * slim, slim, 1)
    cross_partial = product(context_cols, jnp.concatenate([ck_w, cv_w], axis=1)).reshape(held, -1, slim)
    cross_partial = jnp.repeat(cross_partial, 2, axis=0)
    bank_cols, patch_cols, left, scale_cols, cross_partial = lax.optimization_barrier(
        (bank_cols, patch_cols, left, scale_cols, cross_partial)
    )

    conv_cols, square_cols, products = conv_forward_plane(own_select, patch_cols, bank_cols, scale_cols)

    demod_cols = lax.rsqrt(jnp.sum(square_cols, axis=1) + EPSILON)
    extra = jnp.broadcast_to(jnp.repeat(demod_cols, 2, axis=0)[:, None, :], (8, 8, slim))
    sent = jnp.concatenate([conv_cols.reshape(8, pixels, slim), extra, cross_partial], axis=1)
    back = trade(sent)
    cross_kv = jnp.sum(back[:, pixels + 8 :], axis=0).reshape(tokens, 2 * channels).astype(bf16)
    back = jnp.transpose(back[:, : pixels + 8], (1, 0, 2)).reshape(pixels + 8, channels)
    conv_out, demodulate = back[:pixels], back[pixels]

    pre_act = conv_out * demodulate + gain_full * noise_col + bias_full
    hidden = jnp.where(pre_act > 0, pre_act, SLOPE * pre_act)
    hidden_low = hidden.astype(bf16)

    queries = product(hidden_low, qk_full).astype(bf16)
    values = product(hidden_low, val_full).astype(bf16)
    quarter = kernel_bank.shape[0] // 4
    bank_quarter = lax.dynamic_slice_in_dim(kernel_bank, plane * quarter, quarter, 0)
    across = [[i, i + 4] for i in range(4)]
    bank_quarter = lax.all_gather(after(bank_quarter, queries), "batch", axis_index_groups=across)
    bank_quarter = lax.dynamic_index_in_dim(bank_quarter, 1 - device // 4, 0, keepdims=False)
    up_sent = jnp.transpose(up_w.reshape(slim, 8, -1), (1, 0, 2))
    up_cols = trade(after(up_sent, queries)).reshape(channels, -1)
    units = up_cols.shape[1]
    up_two = jnp.concatenate([up_cols, swap_pair(up_cols)], axis=1)
    down_two = jnp.concatenate([down_w, swap_pair(after(down_w, queries))])
    bias_two = jnp.concatenate([up_b, swap_pair(after(up_b, queries))]).astype(f32)
    theirs = swap_pair(jnp.concatenate([queries, values], axis=1))
    keys_all = jnp.concatenate([queries, theirs[:, :channels]])
    values_all = jnp.concatenate([values, theirs[:, channels:]])
    cot_sent = after(cot_feat, queries).reshape(slots, piece, channels)
    cot_pixels = to_pixels(cot_sent, odd_z, odd_pair).reshape(pixels, channels)
    attended = attend(queries, keys_all, values_all)
    grad_res = after(cot_pixels, attended).astype(f32) + jnp.dot(grad_rgb, rgb_full, precision=HIGH)
    branch = grad_res.astype(bf16)
    branch_rows = spread(branch)
    after_self = hidden + product(attended, out_full)
    self_low = after_self.astype(bf16)

    in_head = (jnp.arange(channels)[None, :] // HEAD_DIM == jnp.arange(head_count)[:, None])[None]

    def by_head(rows):
        return jnp.where(in_head, rows[:, None, :], 0).astype(bf16).reshape(tokens * head_count, channels)

    key_blocks, value_blocks = by_head(cross_kv[:, :channels]), by_head(cross_kv[:, channels:])
    cross_scale = HEAD_DIM ** (-0.5)
    cross_q = product(self_low, cq_full).astype(bf16)

    def per_token(x):
        return [x[:, i * head_count : (i + 1) * head_count] for i in range(tokens)]

    cross_s = per_token(contract(cross_q, key_blocks, ((1,), (1,))) * cross_scale)
    top = jnp.maximum(jnp.maximum(cross_s[0], cross_s[1]), jnp.maximum(cross_s[2], cross_s[3]))
    raised = [jnp.exp(x - top) for x in cross_s]
    whole = raised[0] + raised[1] + raised[2] + raised[3]
    cross_p = [x / whole for x in raised]
    cross_plow = jnp.concatenate(cross_p, axis=1).astype(bf16)
    cross_o = product(cross_plow, value_blocks).astype(bf16)
    cross_o = after(cross_o, up_two, down_two, branch_rows)
    after_cross = after_self + product(cross_o, co_full)
    cross_low = after_cross.astype(bf16)

    cross_rows, bank_quarter = lax.optimization_barrier((spread(cross_low), bank_quarter))
    bank_other = gather(bank_quarter, "rows")

    def of_pair(x, step, width, axis):
        return lax.dynamic_slice_in_dim(x, (pair ^ step) * width, width, axis)

    inward = after(jnp.stack([cross_o, self_low, attended, hidden_low]), cross_rows)
    inward = [of_pair(inward, 0, 2 * slim, 2)] + [
        to_pair(of_pair(inward, step, 2 * slim, 2), step) for step in range(1, 4)
    ]
    inner = product(cross_rows, up_two) + bias_two
    activated, gelu_pull = jax.vjp(jax.nn.gelu, inner)
    act_low = activated.astype(bf16)
    (grad_inner,) = gelu_pull(contract(branch_rows, down_two, ((1,), (1,))))
    inner_low = grad_inner.astype(bf16)
    over_rows = ((0,), (0,))

    def pair_sum(x, axis):
        half = x.shape[axis] // 2
        kept = lax.dynamic_slice_in_dim(x, member * half, half, axis)
        sent = lax.dynamic_slice_in_dim(x, (1 - member) * half, half, axis)
        return kept + swap_pair(sent.astype(bf16)).astype(f32)

    def own_sum(x):
        half = x.shape[0] // 2
        return x[:half] + swap_pair(x[half:].astype(bf16)).astype(f32)

    cross_sums = contract(inner_low, up_two, ((1,), (1,))).reshape(4, pixels, channels)
    grad_cross = grad_res + member_sum(cross_sums)
    grad_down = own_sum(contract(act_low, branch_rows, over_rows)).astype(bf16)
    grad_upb = own_sum(jnp.sum(inner_low.astype(f32), axis=0))
    relative = pair ^ jnp.arange(4, dtype=jnp.int32)
    grad_up = contract(cross_rows, inner_low, over_rows).reshape(4, 2, slim, 2 * units)
    kept = lax.dynamic_index_in_dim(grad_up, member, 1, keepdims=False)
    sent = lax.dynamic_index_in_dim(grad_up, 1 - member, 1, keepdims=False).astype(bf16)
    sent = swap_pair(jnp.concatenate([sent[:, :, units:], sent[:, :, :units]], axis=2))
    ups = (kept + sent.astype(f32)).astype(bf16)
    ups = [lax.dynamic_index_in_dim(ups, pair ^ step, 0, keepdims=False) for step in range(4)]
    ups = [ups[0]] + [to_pair(ups[step], step) for step in range(1, 4)]

    cbranch = grad_cross.astype(bf16)
    grad_co = contract(cbranch, co_full, ((1,), (1,))).astype(bf16)
    grad_cp = per_token(contract(grad_co, value_blocks, ((1,), (1,))))
    mean = grad_cp[0] * cross_p[0] + grad_cp[1] * cross_p[1] + grad_cp[2] * cross_p[2] + grad_cp[3] * cross_p[3]
    grad_cs = jnp.concatenate([p * (g - mean) for p, g in zip(cross_p, grad_cp)], axis=1).astype(bf16)
    grad_cq = (product(grad_cs, key_blocks) * cross_scale).astype(bf16)

    def from_heads(blocks):
        return jnp.sum(jnp.where(in_head, blocks.reshape(tokens, head_count, channels), 0.0), axis=1)

    grad_kv = jnp.concatenate(
        [
            from_heads(contract(grad_cs, cross_q, over_rows)) * cross_scale,
            from_heads(contract(cross_plow, grad_co, over_rows)),
        ],
        axis=1,
    )
    grad_kv = (grad_kv + swap_pair(grad_kv)).astype(bf16)
    grad_self = grad_cross + contract(grad_cq, cq_full, ((1,), (1,)))

    sbranch = grad_self.astype(bf16)

    token_rows = jnp.pad(grad_kv.reshape(2 * tokens, channels), ((0, 16 - 2 * tokens), (0, 0)))
    out_first = exchange(cbranch)
    out_second = exchange(jnp.concatenate([grad_cq, token_rows]))
    out_third = exchange(sbranch)
    sbranch = after(sbranch, *out_first, *inward)
    grad_att = contract(sbranch, out_full, ((1,), (1,))).astype(bf16)
    mlp_grads = jnp.concatenate([grad_down.reshape(4, -1, channels)] + [x[None] for x in ups])
    grad_att = after(grad_att, mlp_grads, *out_second)
    grad_qloc, grad_kall, grad_vall = attend_back(queries, keys_all, values_all, grad_att)
    theirs = jnp.concatenate([grad_kall[pixels:], grad_vall[pixels:]], axis=1)
    theirs, mlp_grads = lax.optimization_barrier((theirs, mlp_grads, bank_other, *out_third))[:2]
    mlp_grads = lax.psum(mlp_grads, "rows")
    theirs = swap_pair(theirs)
    grad_q = (grad_qloc + (grad_kall[:pixels] + theirs[:, :channels])).astype(bf16)
    grad_v = (grad_vall[:pixels] + theirs[:, channels:]).astype(bf16)
    grad_hidden = grad_self + contract(grad_q, qk_full, ((1,), (1,))) + contract(grad_v, val_full, ((1,), (1,)))
    grad_pre = grad_hidden * jnp.where(pre_act > 0, 1.0, SLOPE)
    grad_conv = (grad_pre * demodulate).astype(bf16)

    with_tokens = jnp.concatenate([grad_conv, token_rows])
    steps = [with_tokens] + [
        lax.ppermute(with_tokens, "rows", [(z, (z + k) % 4) for z in range(4)]) for k in range(1, 4)
    ]
    grad_cols = trade(jnp.transpose(grad_conv.reshape(pixels, 8, slim), (1, 0, 2)))
    grad_maps = grad_cols.reshape(held, sides * sides, slim)
    coef_cols = jnp.square(demod_cols) * jnp.sum(grad_maps.astype(f32) * conv_cols, axis=1)
    all_taps = pool_matrix(jnp.arange(9, dtype=jnp.int32), sides)
    shifted = jnp.einsum(
        "tlp,spo->tslo", all_taps, grad_maps, preferred_element_type=f32
    )
    shifted = shifted.astype(bf16).reshape(9, held * lows, slim)
    grad_low = lax.dot_general(
        shifted, bank_cols[0], (((0, 2), (0, 2)), ((), ())), preferred_element_type=f32
    ).reshape(held, lows, channels)
    grad_low_other = lax.dot_general(
        shifted, bank_cols[1], (((0, 2), (0, 2)), ((), ())), preferred_element_type=f32
    ).reshape(held, lows, channels)
    mod_low = own_mod.astype(f32)
    select_taps = jnp.stack(
        [jnp.sum(mod_low * grad_low, axis=(1, 2)), jnp.sum(mod_low * grad_low_other, axis=(1, 2))], axis=1
    )
    low_partial = own_select[:, 0, None, None] * grad_low + own_select[:, 1, None, None] * grad_low_other
    late = exchange(after(jnp.concatenate([grad_q, grad_v], axis=1), grad_maps))
    low_partial = after(low_partial, *late)
    conv_all = gather(jnp.stack(lax.optimization_barrier((*steps, low_partial))[:4])[None], "batch")
    low_parts = trade(low_partial.astype(bf16).reshape(8, lows // 2, channels))
    low_total = jnp.sum(low_parts.astype(f32), axis=0)

    held_back = lax.optimization_barrier((act_low, low_partial, *inward, *out_first, *out_second, *out_third))
    act_low, inward = held_back[0], jnp.stack(held_back[2:6])
    out_first, out_second, out_third = [jnp.stack(held_back[6 + 4 * i : 10 + 4 * i]) for i in range(3)]
    result = product(act_low, down_two).reshape(4, pixels, channels)
    result = (after_cross + member_sum(result)).astype(bf16)
    colour = contract(rgb_full.astype(bf16), result, ((1,), (1,)))
    grad_rgb_w = contract(grad_rgb, result.astype(f32), ((0,), (0,)), HIGH)
    kv_all = out_second[:, pixels:].reshape(held, -1)[:, : grad_kv.size].reshape(held * tokens, 2 * channels)
    grad_context = contract(kv_all[:, :channels], ck_w, ((1,), (1,))) + contract(kv_all[:, channels:], cv_w, ((1,), (1,)))
    grad_context = jnp.take(grad_context.reshape(held, -1), relative, axis=0)
    to_channel = [contract(coef_cols, x, ((1,), (1,)), HIGH) for x in products]
    first_share, other_share = own_select[:, :1], own_select[:, 1:]
    scale_term = -own_scales * (
        first_share * first_share * to_channel[0]
        + 2.0 * first_share * other_share * to_channel[1]
        + other_share * other_share * to_channel[2]
    )
    square_scales = jnp.square(own_scales)
    energy = [jnp.sum(square_scales * x, axis=1, keepdims=True) for x in to_channel]
    select_term = jnp.concatenate(
        [
            first_share * energy[0] + other_share * energy[1],
            first_share * energy[1] + other_share * energy[2],
        ],
        axis=1,
    )
    select_partial = select_taps - select_term

    member_scales = lax.dynamic_index_in_dim(own_scales, pair, 0, keepdims=False)
    feat_own = feat_all.reshape(total * lows, channels)
    feat_own = lax.dynamic_slice_in_dim(feat_own, first * lows + device * (lows // 2), lows // 2, 0).astype(f32)
    grad_input_rows = low_total * member_scales
    square_sum = jnp.sum(jnp.square(grad_input_rows))


    def weight_gradients(pairs):
        parts = [contract(inward[:, pick], right, ((0, 1), (0, 1))) for pick, right in pairs]
        parts = pair_sum(jnp.stack(parts).reshape(len(parts), 2 * slim, channels), 1)
        return parts.astype(bf16)

    grads_three = weight_gradients([(0, out_first), (1, out_second[:, :pixels]), (2, out_third)])
    grad_hidden_sums = jnp.stack([jnp.sum(grad_pre, axis=0), jnp.sum(grad_pre * noise_col, axis=0)])
    singles = jnp.concatenate([select_partial.reshape(-1), square_sum[None], jnp.zeros((127 - 2 * held,), f32)])
    singles = jnp.concatenate([coef_cols.reshape(-1), singles])
    last_sent = jnp.concatenate(
        [
            grad_hidden_sums,
            grad_rgb_w,
            grad_context.reshape(-1, channels),
            jnp.sum(low_total * feat_own, axis=0)[None],
            scale_term,
            jnp.pad(singles, (0, channels - singles.shape[0]))[None],
        ]
    )
    last_all = gather(last_sent[None], "batch")
    col_sums = jnp.sum(lax.dynamic_slice_in_dim(last_all[:, :5], device * slim, slim, 2), axis=0)
    context_grads = jnp.transpose(last_all[:, 5:7].reshape(8, held * tokens, slim), (1, 0, 2)).reshape(held, -1)
    table_cols = class_table.shape[1]
    context_grads = lax.dynamic_slice_in_dim(context_grads, device * table_cols, table_cols, 1)
    grad_scales = jnp.sum(last_all[:, 7].reshape(held, 2, channels), axis=1) + jnp.sum(last_all[:, 8 : 8 + held], axis=0)
    singles = last_all[:, 8 + held]
    coef_plane = jnp.transpose(singles[:, : held * slim].reshape(8, held, slim), (1, 0, 2)).reshape(-1)
    singles = jnp.sum(singles[:, held * slim : held * slim + 128], axis=0)
    pieces = [coef_plane, context_grads.reshape(-1), grad_scales.reshape(-1), col_sums.reshape(-1), grad_upb, singles]
    ends = []
    for x in pieces:
        ends.append(x.shape[0] + (ends[-1] if ends else 0))
    rows_all = gather(jnp.concatenate(pieces).reshape(1, -1, 128), "rows").reshape(4, -1)
    late = jnp.stack(late)
    grads_two = weight_gradients([(3, late[:, :, :channels]), (3, late[:, :, channels:])])

    mids = jnp.concatenate([grads_three, grads_two])
    mids = lax.psum(after(mids, mlp_grads), "rows")
    coef = rows_all[:, : ends[0]].reshape(total, channels)
    first_tap = 2 * (device % 4)
    matrix = pool_matrix(first_tap + jnp.arange(3, dtype=jnp.int32), sides)
    order = (plane - jnp.arange(4, dtype=jnp.int32)) % 4
    shifted_all = pool_samples(order, matrix, conv_all.reshape(4, 2, 4, pixels + 16, channels), pixels)
    kv_every = jnp.transpose(conv_all[::2, :, pixels : pixels + 2 * tokens], (1, 0, 2, 3))
    kv_every = kv_every.reshape(total * tokens, 2 * channels)
    context_every = lax.dynamic_slice_in_dim(after(context_all, low_total).reshape(4, held * tokens, channels), device * slim, slim, 2)
    context_every = jnp.take(context_every, order, axis=0).reshape(total * tokens, slim)
    sum_ck = contract(context_every, kv_every[:, :channels], over_rows)
    sum_cv = contract(context_every, kv_every[:, channels:], over_rows)
    square_all = jnp.square(scales)
    blocks = (device % 4) * 9 + jnp.arange(9, dtype=jnp.int32)
    bank_total = bank_gradient(
        blocks // 4 - first_tap,
        blocks % 4,
        left,
        shifted_all.reshape(3, total * lows, channels),
        kernel_bank,
        bank_other,
        split_terms(own_share * own_share * square_all, True),
        split_terms(own_share * share_other * square_all, True),
        split_terms(coef, False),
    )

    mlp_grads = after(mlp_grads, bank_total).astype(f32)
    sum_down = mlp_grads[:4].reshape(units, channels)
    ordered = [lax.dynamic_index_in_dim(mlp_grads, 4 + (pair ^ c), 0, keepdims=False) for c in range(4)]
    swapped = [jnp.concatenate([x[:, units:], x[:, :units]], axis=1) for x in ordered]
    sum_up = jnp.where(member == 0, jnp.concatenate(ordered, axis=1), jnp.concatenate(swapped, axis=1))

    rows_late = after(rows_all, bank_total)
    context_grads = rows_late[:, ends[0] : ends[1]].reshape(total, table_cols)
    grad_scales = rows_late[:, ends[1] : ends[2]].reshape(total, channels)
    rows_total = jnp.sum(rows_late[:, ends[2] : ends[4]], axis=0)
    sum_bias, sum_gain = rows_total[:slim], rows_total[slim : 2 * slim]
    sum_rgb = rows_total[2 * slim : 5 * slim].reshape(3, slim)
    sum_upb = rows_total[5 * slim :]
    singles = rows_late[:, ends[4] :]
    grad_select = singles[:, : 2 * held].reshape(total, 2)
    square_sum = jnp.sum(singles[:, 2 * held])
    classes = class_table.shape[0]
    one_hot = (labels_all[:, None] == jnp.arange(classes)[None, :]).astype(f32)
    sum_table = contract(one_hot, context_grads, over_rows, HIGH)
    entries = float(total * 4 * in_rows * in_cols * channels)
    r1_value = square_sum / entries
    style_f32 = style_own.astype(f32)
    grad_logits = select * (grad_select - jnp.sum(grad_select * select, axis=-1, keepdims=True))
    sum_mod = contract(style_f32, grad_scales, over_rows, HIGH)
    sum_sel = contract(style_f32, grad_logits, over_rows, HIGH)

    feat_out = from_pixels(after(result, coef).reshape(2, piece, channels), odd_z, odd_pair)
    feat_out = feat_out.reshape(slots, 2 * in_rows, sides, channels)
    colour_sent = jnp.transpose(colour.reshape(3, 2, piece), (1, 0, 2)).reshape(2, 1, 3 * piece)
    colour_sent = jnp.pad(colour_sent, ((0, 0), (0, 0), (0, channels - 3 * piece)))
    low_sent = jnp.concatenate([grad_input_rows.reshape(2, lows // 4, channels), colour_sent], axis=1)
    low_back = from_pixels(after(low_sent, coef), odd_z, odd_pair)
    rgb_out = low_back[:, lows // 4, : 3 * piece].reshape(slots, 3, 2 * in_rows, sides)
    grad_input = low_back[:, : lows // 4].reshape(slots, in_rows, in_cols, channels)
    mids = after(mids, feat_out, low_back, sum_up, sum_down, sum_table, sum_mod, sum_ck, sum_cv, sum_rgb)
    sum_co, sum_cq, sum_out, sum_qk, sum_val = [mids[i].astype(f32) for i in range(5)]
    return (
        feat_out,
        rgb_out,
        grad_input,
        r1_value,
        sum_mod,
        sum_sel,
        bank_total,
        sum_bias,
        sum_gain,
        sum_qk,
        sum_val,
        sum_out,
        sum_cq,
        sum_ck,
        sum_cv,
        sum_co,
        sum_up,
        sum_upb,
        sum_down,
        sum_table,
        sum_rgb,
    )


def solution(mesh):
    split = mesh.shape["batch"] == 8 and mesh.shape["rows"] == 4
    return jax.shard_map(
        by_planes if split else per_device,
        mesh=mesh,
        in_specs=(
            P("batch", "rows", None, None),
            P("batch", None),
            P("batch"),
            P("batch", "rows", None),
            P("batch", "rows", None, None),
            P("batch", None, "rows", None),
            P("batch", None),
            P("batch", None),
            P("batch", None),
            P("batch"),
            P("batch"),
            P("batch", None),
            P("batch", None),
            P("batch", None),
            P("batch", None),
            P("batch", None),
            P("batch", None),
            P("batch", None),
            P("batch", None),
            P("batch"),
            P("batch", None),
            P(None, "batch"),
            P(None, "batch"),
        ),
        out_specs=(
            P("batch", "rows", None, None),
            P("batch", None, "rows", None),
            P("batch", "rows", None, None),
            P(),
            P("batch", None),
            P("batch", None),
            P("batch", None),
            P("batch"),
            P("batch"),
            P("batch", None),
            P("batch", None),
            P("batch", None),
            P("batch", None),
            P("batch", None),
            P("batch", None),
            P("batch", None),
            P("batch", None),
            P("batch"),
            P("batch", None),
            P(None, "batch"),
            P(None, "batch"),
        ),
        check_vma=False,
    )
```
